512 devices in a mesh: frame: 16 (over z, core), height: 32 (over x, y).
Axes of the slice: x: 4, y: 8, z: 8, core: 2. Of those that a mesh axis runs over, the one named last changes fastest.
Arguments:
- video: bfloat16 [33, 64, 128, 256], P(None, 'height', 'frame'), may hold values from -48 to 48
- frame_counts: int32 [16], replicated, may hold values from 1 to 6, 33 in all
- temporal_weight: bfloat16 [6912, 256], replicated, may hold values from -0.125 to 0.125
- temporal_bias: float32 [256], replicated, may hold values from -4 to 4
- first_gain: float32 [256], replicated, may hold values from 0.1 to 1.9
- first_shift: float32 [256], replicated, may hold values from -3 to 3
- first_weight: bfloat16 [2304, 256], P('height'), may hold values from -0.125 to 0.125
- first_bias: float32 [256], replicated, may hold values from -4 to 4
- second_gain: float32 [256], replicated, may hold values from 0.1 to 1.9
- second_shift: float32 [256], replicated, may hold values from -3 to 3
- second_weight: bfloat16 [2304, 256], P('height'), may hold values from -0.125 to 0.125
- second_bias: float32 [256], replicated, may hold values from -4 to 4
Outputs:
- owned: bfloat16 [96, 64, 128, 256], P('frame', 'height')
The draws below stay inside these ranges and needn't reach their ends.
Inputs may be any that keep to these rules, and one draw needn't show every extreme that they name: frame_counts[k] consecutive frames belong to index k of frame; the counts add up to 33 and the largest is exactly 6.
All inputs are finite; a program needn't handle non-finite values.
Results may differ from the reference program's by a relative error of at most 0.0055.
Values may be sent and summed in bfloat16 or wider, within the bound.
A program may use at most 64 MiB of HBM per device.

```python
import math
import jax
import jax.numpy as jnp
import numpy as np
from jax import lax

C = 256
GROUPS = 32
FRAMES = 33
H = 64
W = 128
MOST = 6
SLOTS = 96
N_FRAME = 16


def draw_video(key, part):
    key_base, key_rows, key_cols = jax.random.split(key, 3)
    position = jnp.arange(H, dtype=jnp.float32) / max(H - 1, 1)
    row_log = math.log(3.0) * (position - 0.5) + jax.random.uniform(key_rows, (H,), jnp.float32, -0.6, 0.6)
    col_log = jax.random.uniform(key_cols, (W,), jnp.float32, -0.8, 0.8)
    base = jnp.clip(jax.random.normal(key_base, (FRAMES, H, W, C), jnp.float32), -6.0, 6.0)
    scaled = base * jnp.exp(row_log)[None, :, None, None] * jnp.exp(col_log)[None, None, :, None]
    return jnp.clip(scaled, -48.0, 48.0).astype(jnp.bfloat16)


def shard_levels(stream_key, shape, cuts, least, high):
    factor_of = 1.0
    for dim, shards_of in cuts:
        draws = jax.random.uniform(jax.random.fold_in(jax.random.fold_in(stream_key, 6), dim), (shards_of,), jnp.float32, least / len(cuts), high / len(cuts))
        factor_of = factor_of * jnp.repeat(jnp.exp(draws), shape[dim] // shards_of).reshape((-1,) + (1,) * (len(shape) - 1 - dim))
    return factor_of


def split_up(number_of, total, limit, slope):
    weights = [(1 << 20) // math.isqrt(standing ** slope) + 1 for standing in range(2, number_of + 1)]
    surplus, given = total - limit - (number_of - 1), [1] * (number_of - 1)
    while surplus > 0:
        movable = [i for i in range(number_of - 1) if given[i] < limit]
        mass, budget = sum([weights[i] for i in movable]), surplus
        for i in movable:
            addition = min(limit - given[i], max(1, budget * weights[i] // mass), surplus)
            given[i] = given[i] + addition
            surplus = surplus - addition
    return np.array([limit] + given)


def ragged(key, number_of, total, most, lean):
    if number_of == 2:
        one = jax.random.randint(key, (), max(1, total - most), min(most, total - 1) + 1)
        return jnp.stack([one, total - one])
    sizes = jnp.asarray(split_up(number_of, total, most, lean), jnp.int32)
    pairs = (number_of - 1) // 2
    giver, taker = sizes[1:1 + 2 * pairs:2], sizes[2:2 + 2 * pairs:2]
    margin = jnp.minimum(giver - 1, most - taker)
    shifted = jax.random.randint(jax.random.fold_in(key, 1), (pairs,), 0, 1 << 20) % (margin + 1)
    sizes = sizes.at[1:1 + 2 * pairs:2].set(giver - shifted).at[2:2 + 2 * pairs:2].set(taker + shifted)
    return sizes[jax.random.permutation(jax.random.fold_in(key, 2), number_of)]


def normal_values(stream_key, extent, deviation, reach, cuts=(), kind=jnp.bfloat16):
    gain = shard_levels(stream_key, extent, cuts, -0.22, 0.18) if cuts else 1.0
    drawn = jax.random.normal(stream_key, extent, jnp.float32) * deviation * gain
    return jnp.minimum(jnp.maximum(drawn, -reach), reach).astype(kind)


def setup_inputs(seed: int = 0) -> dict:
    streams_of = jax.random.split(jax.random.key(seed), 13)
    video = draw_video(jax.random.fold_in(streams_of[12], 71), 0)
    frame_counts = ragged(streams_of[1], N_FRAME, FRAMES, MOST, 2).astype(jnp.int32)
    temporal_weight = normal_values(streams_of[2], (27 * C, C), (9 * C) ** -0.5, 0.125)
    temporal_bias = normal_values(streams_of[3], (C,), 1.0, 4.0, (), jnp.float32)
    first_gain = jnp.clip(1.0 + 0.18 * jax.random.normal(streams_of[4], (C,), jnp.float32), 0.1, 1.9)
    first_shift = normal_values(streams_of[5], (C,), 0.5, 3.0, (), jnp.float32)
    first_weight = normal_values(streams_of[6], (9 * C, C), (9 * C) ** -0.5, 0.125, ((0, 32),))
    first_bias = normal_values(streams_of[7], (C,), 1.0, 4.0, (), jnp.float32)
    second_gain = jnp.clip(1.0 + 0.18 * jax.random.normal(streams_of[8], (C,), jnp.float32), 0.1, 1.9)
    second_shift = normal_values(streams_of[9], (C,), 0.5, 3.0, (), jnp.float32)
    second_weight = normal_values(streams_of[10], (9 * C, C), (9 * C) ** -0.5, 0.125, ((0, 32),))
    second_bias = normal_values(streams_of[11], (C,), 1.0, 4.0, (), jnp.float32)
    return {"video": video, "frame_counts": frame_counts, "temporal_weight": temporal_weight, "temporal_bias": temporal_bias, "first_gain": first_gain, "first_shift": first_shift, "first_weight": first_weight, "first_bias": first_bias, "second_gain": second_gain, "second_shift": second_shift, "second_weight": second_weight, "second_bias": second_bias}


def spatial_patches(padded, row_count, col_count):
    pieces = []
    for row_tap in range(3):
        for col_tap in range(3):
            pieces.append(padded[..., row_tap:row_tap + row_count, col_tap:col_tap + col_count, :])
    return jnp.concatenate(pieces, axis=-1)

def group_act(values, gain_row, shift_row):
    grouped = values.reshape(H, W, GROUPS, C // GROUPS)
    group_mean = lax.optimization_barrier(jnp.mean(grouped, axis=(0, 1, 3), keepdims=True))
    centered = grouped - group_mean
    group_var = lax.optimization_barrier(jnp.mean(centered * centered, axis=(0, 1, 3), keepdims=True))
    normed = (centered * lax.rsqrt(group_var + 1e-06)).reshape(H, W, C) * gain_row + shift_row
    return jax.nn.silu(normed).astype(jnp.bfloat16)

def conv_frame(inputs, weight, offset_bias):
    padded = jnp.pad(inputs, ((1, 1), (1, 1), (0, 0)))
    patches = spatial_patches(padded, H, W).reshape(H * W, 9 * C)
    summed = jnp.dot(patches, weight, preferred_element_type=jnp.float32) + offset_bias
    return summed.reshape(H, W, C)

def reference(video, frame_counts, temporal_weight, temporal_bias, first_gain, first_shift, first_weight, first_bias, second_gain, second_shift, second_weight, second_bias):
    activated = jax.nn.silu(video.astype(jnp.float32)).astype(jnp.bfloat16)
    causal = jnp.pad(activated, ((2, 0), (1, 1), (1, 1), (0, 0)))

    def one_frame(frame_idx):
        window = lax.dynamic_slice_in_dim(causal, frame_idx, 3, 0)
        accumulated = jnp.zeros((H * W, C), jnp.float32)
        for tap_time in range(3):
            patches = spatial_patches(window[tap_time], H, W).reshape(H * W, 9 * C)
            accumulated = accumulated + jnp.dot(patches, temporal_weight[tap_time * 9 * C:(tap_time + 1) * 9 * C], preferred_element_type=jnp.float32)
        source = lax.dynamic_index_in_dim(video, frame_idx, 0, keepdims=False)
        blended = (source.astype(jnp.float32) + accumulated.reshape(H, W, C) + temporal_bias).astype(jnp.bfloat16)
        first_in = group_act(blended.astype(jnp.float32), first_gain, first_shift)
        first_out = conv_frame(first_in, first_weight, first_bias).astype(jnp.bfloat16)
        second_in = group_act(first_out.astype(jnp.float32), second_gain, second_shift)
        return (blended.astype(jnp.float32) + conv_frame(second_in, second_weight, second_bias)).astype(jnp.bfloat16)
    decoded = lax.map(one_frame, jnp.arange(FRAMES, dtype=jnp.int32))
    offsets = jnp.cumsum(frame_counts) - frame_counts
    slot_ids = jnp.arange(SLOTS, dtype=jnp.int32)
    owner_idx = slot_ids // MOST
    within = slot_ids - owner_idx * MOST
    first_frame = jnp.take(offsets, owner_idx)
    frame_total = jnp.take(frame_counts, owner_idx)
    source_idx = jnp.clip(first_frame + within, 0, FRAMES - 1).astype(jnp.int32)
    picked = jnp.take(decoded, source_idx, axis=0)
    return jnp.where((within < frame_total)[:, None, None, None], picked, jnp.zeros_like(picked))
```

```python
import functools

import jax
import jax.numpy as jnp
from jax import lax
from jax.experimental import pallas as pl
from jax.experimental.pallas import tpu as pltpu
from jax.sharding import PartitionSpec as P

GROUPS = 32
C = 256
J = 8
MOST = 6
F32 = jnp.float32
BF16 = jnp.bfloat16
HIGH = lax.Precision.HIGHEST
MESH = pl.DeviceIdType.MESH
SUM_LANES = 128


def silu(v):
    half = 0.5 * v
    return half * jnp.tanh(half) + half


def hdot(a, b):
    return jnp.dot(a, b, precision=HIGH, preferred_element_type=F32)


def one_hot(rows, cols, fn):
    r = lax.broadcasted_iota(jnp.int32, (rows, cols), 0)
    c = lax.broadcasted_iota(jnp.int32, (rows, cols), 1)
    return jnp.where(fn(r, c), 1.0, 0.0).astype(F32)


def kernel(
    nf, nx, ny, frames, su, cells,
    counts, video, tw, w1, w2, tb, g1, s1, b1, g2, s2, b2,
    out,
    vid, twv, rowb, colb, hr, hc, gt, se, tc, bs, stage, sts, rs, ysc, xsc, fsb,
    rec, ha, hb, first, g4, so, wb, wr, stat, mu, sc, outv, offs,
    local_sem, p1_send, p1_recv, wl_sem, wy_send, wy_recv, wx_send, wx_recv, wp_send, wp_recv,
    a2a_send, a2a_recv, st_send, st_recv, y_send, y_recv, x_send, x_recv,
    ha_send, ha_recv, hb_send, hb_recv, out_sem,
):
    nh = nx * ny
    tp = frames + 1
    wide = tp * J
    fr = bs.shape[0]
    width = nf * J
    f = lax.axis_index("frame")
    h = lax.axis_index("height")
    x = h // ny
    y = lax.rem(h, ny)
    core = lax.rem(f, 2)
    hup, hdn = lax.rem(h + nh - 1, nh), lax.rem(h + 1, nh)
    fl, fr_ = lax.rem(f + nf - 1, nf), lax.rem(f + 1, nf)

    def dev(hh, ff):
        return {"height": hh, "frame": ff}

    def remote(src, dst, send, recv, hh, ff):
        return pltpu.make_async_remote_copy(
            src_ref=src, dst_ref=dst, send_sem=send, recv_sem=recv,
            device_id=dev(hh, ff), device_id_type=MESH,
        )

    def await_bytes(ref, sem):
        pltpu.make_async_copy(ref, ref, sem).wait()

    barrier = pltpu.get_barrier_semaphore()

    def greet(hh, ff):
        pl.semaphore_signal(barrier, inc=1, device_id=dev(hh, ff), device_id_type=MESH)

    for hh, ff in ((hup, f), (hdn, f), (hup, fl), (hup, fr_), (hdn, fl), (hdn, fr_)):
        greet(hh, ff)
    for s in range(1, ny):
        greet(x * ny + lax.rem(y + s, ny), f)
    for s in range(1, nx):
        greet(lax.rem(x + s, nx) * ny + y, f)
    for s in range(1, nf):
        greet(h, lax.rem(f + s, nf))
    greeted = 6 + (ny - 1) + (nx - 1) + (nf - 1)

    copy_video = pltpu.make_async_copy(video, vid, local_sem.at[0])
    copy_video.start()
    copy_tw = pltpu.make_async_copy(tw, twv, local_sem.at[1])
    copy_tw.start()
    lane0 = pl.multiple_of(core * 128, 128)
    lanes = pl.ds(lane0, 128)
    mine = pl.ds(h * su, su)
    own_w = [
        pltpu.make_async_copy(w.at[:, :, lanes], wb.at[i, mine, :, lanes], wl_sem.at[i])
        for i, w in enumerate((w1, w2))
    ]
    for copy in own_w:
        copy.start()

    total = jnp.int32(0)
    for k in range(nf):
        offs[k] = total
        total = total + counts[k]

    zero8 = jnp.zeros((8, C), F32)
    gt[0:8, :] = zero8
    gt[8 + wide : 16 + wide, :] = zero8
    g4[0:8, :] = zero8
    g4[8 + width : 16 + width, :] = zero8
    for a in range(3):
        for i in range(2):
            tc[a, i, 0:16, :] = jnp.zeros((16, C), F32)

    pick_left = one_hot(fr, wide, lambda r, c: c == r * J).astype(BF16)
    pick_right = one_hot(fr, wide, lambda r, c: c == r * J + J - 1).astype(BF16)

    copy_video.wait()
    for i in range(2):
        act = silu(vid[:, i].astype(F32)).astype(BF16)
        rowb[i, 0:frames] = act
        rowb[i, frames:tp] = jnp.zeros((1, J, C), BF16)
        flat = rowb[i].astype(F32).reshape(wide, C).astype(BF16)
        colb[0, i] = jnp.dot(pick_left, flat, preferred_element_type=F32).astype(BF16)
        colb[1, i] = jnp.dot(pick_right, flat, preferred_element_type=F32).astype(BF16)

    pl.semaphore_wait(barrier, greeted)

    borders = [
        (rowb.at[0], hr.at[1], hup, f),
        (rowb.at[1], hr.at[0], hdn, f),
        (colb.at[0], hc.at[1, 1:3], h, fl),
        (colb.at[1], hc.at[0, 1:3], h, fr_),
        (colb.at[0, 0], hc.at[1, 3], hup, fl),
        (colb.at[1, 0], hc.at[0, 3], hup, fr_),
        (colb.at[0, 1], hc.at[1, 0], hdn, fl),
        (colb.at[1, 1], hc.at[0, 0], hdn, fr_),
    ]
    p1 = [
        remote(src, dst, p1_send.at[n], p1_recv.at[n], hh, ff)
        for n, (src, dst, hh, ff) in enumerate(borders)
    ]
    for copy in p1:
        copy.start()

    for copy in own_w:
        copy.wait()
    for i in range(2):
        for s in range(1, ny):
            here = wb.at[i, mine, :, lanes]
            remote(
                here, here, wy_send.at[i], wy_recv.at[i], x * ny + lax.rem(y + s, ny), f
            ).start()

    for copy in p1:
        copy.wait()

    put_left = one_hot(wide, fr, lambda r, c: r == c * J).astype(BF16)
    put_right = one_hot(wide, fr, lambda r, c: r == c * J + J - 1).astype(BF16)
    col = lax.rem(lax.broadcasted_iota(jnp.int32, (wide, C), 0), J)
    keep_left = jnp.where(f > 0, 1.0, 0.0)
    keep_right = jnp.where(f < nf - 1, 1.0, 0.0)
    keep_top = jnp.where(h > 0, 1.0, 0.0)
    keep_bottom = jnp.where(h < nh - 1, 1.0, 0.0)
    for ip in range(4):
        source = (hr.at[0], rowb.at[0], rowb.at[1], hr.at[1])[ip]
        keep = (keep_top, 1.0, 1.0, keep_bottom)[ip]
        middle = source[...].astype(F32).reshape(wide, C) * keep
        gt[8 : 8 + wide, :] = middle
        lefts = jnp.dot(put_left, hc[0, ip], preferred_element_type=F32) * (keep * keep_left)
        rights = jnp.dot(put_right, hc[1, ip], preferred_element_type=F32) * (keep * keep_right)
        rows = slice(ip * wide, (ip + 1) * wide)
        se[rows, 0:C] = jnp.where(col == 0, lefts, gt[7 : 7 + wide, :]).astype(BF16)
        se[rows, C : 2 * C] = middle.astype(BF16)
        se[rows, 2 * C : 3 * C] = jnp.where(col == J - 1, rights, gt[9 : 9 + wide, :]).astype(BF16)
    copy_tw.wait()

    def taps(a, carry):
        for i in range(2):
            acc = jnp.zeros((wide, C), F32)
            for b in range(3):
                start = pl.multiple_of(a * (9 * C) + b * (3 * C), 3 * C)
                acc = acc + jnp.dot(
                    se[(i + b) * wide : (i + b + 1) * wide, :],
                    twv[pl.ds(start, 3 * C), :],
                    preferred_element_type=F32,
                )
            tc[a, i, 16 : 16 + wide, :] = acc
        return carry

    lax.fori_loop(0, 3, taps, 0)

    n_all = frames * J
    sums = jnp.zeros((n_all, C), F32)
    squares = jnp.zeros((n_all, C), F32)
    for i in range(2):
        value = (
            vid[:, i].astype(F32).reshape(n_all, C)
            + (tc[0, i, 0:n_all, :] + tc[1, i, 8 : 8 + n_all, :] + tc[2, i, 16 : 16 + n_all, :])
            + tb[...]
        )
        bs[0:frames, i] = value.reshape(frames, J, C).astype(BF16)
        rounded = bs[0:frames, i].astype(F32).reshape(n_all, C)
        sums = sums + rounded
        squares = squares + rounded * rounded
        bs[frames:fr, i] = jnp.zeros((fr - frames, J, C), BF16)

    per = C // GROUPS
    sum_map = one_hot(C, SUM_LANES, lambda r, c: c == r // per)
    sq_map = one_hot(C, SUM_LANES, lambda r, c: c == r // per + GROUPS)
    fsum = jnp.sum(sums.reshape(frames, J, C), axis=1)
    fsq = jnp.sum(squares.reshape(frames, J, C), axis=1)
    fsb[0:frames, :] = hdot(fsum, sum_map) + hdot(fsq, sq_map)
    fsb[frames:fr, :] = jnp.zeros((fr - frames, SUM_LANES), F32)

    def pack(k, carry):
        start = offs[k]
        sts[k] = fsb[pl.ds(start, 8), :]
        for r in range(MOST):
            stage[r, k] = bs[start + r]
        return carry

    lax.fori_loop(0, nf, pack, 0)

    def send_sums(s, carry):
        k = lax.rem(f + s, nf)
        remote(sts.at[k], rs.at[f], st_send, st_recv, h, k).start()
        return carry

    lax.fori_loop(1, nf, send_sums, 0)

    def send_slot(n, carry):
        r = n // (nf - 1)
        k = lax.rem(f + 1 + lax.rem(n, nf - 1), nf)
        remote(stage.at[r, k], rec.at[r, :, f], a2a_send, a2a_recv.at[r], h, k).start()
        return carry

    lax.fori_loop(0, MOST * (nf - 1), send_slot, 0)
    my_offset = offs[f]
    rs[f] = fsb[pl.ds(my_offset, 8), :]
    for r in range(MOST):
        rec[r, :, f] = bs[my_offset + r]

    block = pl.ds(x * (ny * su), ny * su)
    for i in range(2):
        await_bytes(wb.at[i, pl.ds(0, (ny - 1) * su), :, lanes], wy_recv.at[i])
        for s in range(1, nx):
            here = wb.at[i, block, :, lanes]
            remote(
                here, here, wx_send.at[i], wx_recv.at[i], lax.rem(x + s, nx) * ny + y, f
            ).start()

    def y_start(q, value):
        ysc[q, y] = value
        for s in range(1, ny):
            remote(
                ysc.at[q, y], ysc.at[q, y], y_send.at[q], y_recv.at[q],
                x * ny + lax.rem(y + s, ny), f,
            ).start()

    def y_finish(q):
        await_bytes(ysc.at[q, 0 : ny - 1], y_recv.at[q])
        return jnp.sum(ysc[q], axis=0)

    def x_start(q, value):
        xsc[q, x] = value
        for s in range(1, nx):
            remote(
                xsc.at[q, x], xsc.at[q, x], x_send.at[q], x_recv.at[q],
                lax.rem(x + s, nx) * ny + y, f,
            ).start()

    def x_finish(q):
        await_bytes(xsc.at[q, 0 : nx - 1], x_recv.at[q])
        return jnp.sum(xsc[q], axis=0)

    def set_norm(q, totals, gain):
        sum_back = one_hot(SUM_LANES, C, lambda r, c: r == c // per)
        sq_back = one_hot(SUM_LANES, C, lambda r, c: r == c // per + GROUPS)
        mean = hdot(totals, sum_back) / cells
        var = hdot(totals, sq_back) / cells - mean * mean
        mu[q] = mean
        sc[q] = lax.rsqrt(jnp.maximum(var, 0.0) + 1e-06) * gain

    await_bytes(rs.at[0 : nf - 1], st_recv)
    y_start(0, jnp.sum(rs[...], axis=0))
    x_start(0, y_finish(0))
    set_norm(0, x_finish(0), g1[...])

    partner = f + 1 - 2 * core
    for i in range(2):
        await_bytes(wb.at[i, pl.ds(0, (nx - 1) * ny * su), :, lanes], wx_recv.at[i])
        half = wb.at[i, :, :, lanes]
        remote(half, half, wp_send.at[i], wp_recv.at[i], h, partner).start()

    other = pl.ds(pl.multiple_of(128 - core * 128, 128), 128)

    def ready_weight(i):
        await_bytes(wb.at[i, :, :, other], wp_recv.at[i])
        step = 18

        def widen(n, carry):
            rows = wb[i, pl.ds(n * step, step)].astype(F32).reshape(step * 8, C)
            wr[i, pl.ds(pl.multiple_of(n * step * 8, step * 8), step * 8), :] = rows.astype(BF16)
            return carry

        lax.fori_loop(0, nh * su // step, widen, 0)

    def slot_in(r):
        await_bytes(rec.at[r, :, 0 : nf - 1], a2a_recv.at[r])
        remote(rec.at[r, 0], ha.at[r, 1], ha_send.at[r, 0], ha_recv.at[r, 0], hup, f).start()
        remote(rec.at[r, 1], ha.at[r, 0], ha_send.at[r, 1], ha_recv.at[r, 1], hdn, f).start()

    keeps = (keep_top, None, None, keep_bottom)

    def convolve(r, rows_of, q, shift, weight):
        mean = mu[q, pl.ds(r, 1), :]
        scale = sc[q, pl.ds(r, 1), :]
        for ip in range(4):
            normed = silu((rows_of(ip) - mean) * scale + shift)
            if keeps[ip] is not None:
                normed = normed * keeps[ip]
            g4[8 : 8 + width, :] = normed
            rows = slice(ip * width, (ip + 1) * width)
            so[rows, 0:C] = g4[7 : 7 + width, :].astype(BF16)
            so[rows, C : 2 * C] = normed.astype(BF16)
            so[rows, 2 * C : 3 * C] = g4[9 : 9 + width, :].astype(BF16)
        acc = jnp.zeros((2 * width, C), F32)
        for b in range(3):
            acc = acc + jnp.dot(
                so[b * width : (b + 2) * width, :],
                wr[weight, b * 3 * C : (b + 1) * 3 * C, :],
                preferred_element_type=F32,
            )
        return acc

    def first_rows(r):
        def get(ip):
            ref = (ha.at[r, 0], rec.at[r, 0], rec.at[r, 1], ha.at[r, 1])[ip]
            return ref[...].astype(F32).reshape(width, C)

        return get

    def second_rows(r):
        def get(ip):
            ref = (hb.at[r, 0], first.at[r, 0], first.at[r, 1], hb.at[r, 1])[ip]
            return ref[...].astype(F32)

        return get

    stat[...] = jnp.zeros_like(stat)
    ready_weight(0)
    slot_in(0)

    def first_conv(r, carry):
        @pl.when(r + 1 < MOST)
        def _():
            slot_in(r + 1)

        await_bytes(ha.at[r, 0], ha_recv.at[r, 0])
        await_bytes(ha.at[r, 1], ha_recv.at[r, 1])
        result = convolve(r, first_rows(r), 0, s1[...], 0) + b1[...]
        first[r, 0] = result[0:width].astype(BF16)
        first[r, 1] = result[width : 2 * width].astype(BF16)
        remote(first.at[r, 0], hb.at[r, 1], hb_send.at[r, 0], hb_recv.at[r, 0], hup, f).start()
        remote(first.at[r, 1], hb.at[r, 0], hb_send.at[r, 1], hb_recv.at[r, 1], hdn, f).start()
        rounded = first[r, 0].astype(F32), first[r, 1].astype(F32)
        sums = rounded[0] + rounded[1]
        squares = rounded[0] * rounded[0] + rounded[1] * rounded[1]
        stat[0, pl.ds(r, 1), :] = jnp.sum(sums, axis=0, keepdims=True)
        stat[1, pl.ds(r, 1), :] = jnp.sum(squares, axis=0, keepdims=True)
        return carry

    lax.fori_loop(0, MOST, first_conv, 0)
    y_start(1, hdot(stat[0], sum_map) + hdot(stat[1], sq_map))
    ready_weight(1)
    x_start(1, y_finish(1))
    set_norm(1, x_finish(1), g2[...])

    my_count = counts[f]

    def second_conv(r, carry):
        await_bytes(hb.at[r, 0], hb_recv.at[r, 0])
        await_bytes(hb.at[r, 1], hb_recv.at[r, 1])
        result = convolve(r, second_rows(r), 1, s2[...], 1) + b2[...]
        live = r < my_count
        for i in range(2):
            kept = rec[r, i].astype(F32).reshape(width, C)
            value = kept + result[i * width : (i + 1) * width]
            outv[r, i] = jnp.where(live, value, 0.0).astype(BF16)
        pltpu.make_async_copy(outv.at[r], out.at[r], out_sem.at[r]).start()
        return carry

    lax.fori_loop(0, MOST, second_conv, 0)

    for i in range(2):
        await_bytes(wb.at[i, pl.ds(0, (ny - 1) * su), :, lanes], wy_send.at[i])
        await_bytes(wb.at[i, pl.ds(0, (nx - 1) * ny * su), :, lanes], wx_send.at[i])
        await_bytes(wb.at[i, :, :, lanes], wp_send.at[i])
    await_bytes(sts.at[0 : nf - 1], st_send)
    await_bytes(stage.at[:, 0 : nf - 1], a2a_send)
    for q in range(2):
        await_bytes(ysc.at[q, 0 : ny - 1], y_send.at[q])
        await_bytes(xsc.at[q, 0 : nx - 1], x_send.at[q])
    for r in range(MOST):
        for i in range(2):
            await_bytes(rec.at[r, i], ha_send.at[r, i])
            await_bytes(first.at[r, i], hb_send.at[r, i])
        pltpu.make_async_copy(outv.at[r], out.at[r], out_sem.at[r]).wait()


def per_device(nf, nh, video, counts, tw, tb, g1, s1, w1, b1, g2, s2, w2, b2):
    frames = video.shape[0]
    ny = 8 if nh % 8 == 0 else 2
    nx = nh // ny
    su = w1.shape[0] // 8
    tp = frames + 1
    wide = tp * J
    fr = -(-(frames + 7) // 8) * 8
    width = nf * J
    cells = float(2 * nh * width * (C // GROUPS))
    row = lambda v: v.reshape(1, C)
    vm = pl.BlockSpec(memory_space=pltpu.VMEM)
    anyspace = pl.BlockSpec(memory_space=pl.ANY)
    dma = pltpu.SemaphoreType.DMA
    V = pltpu.VMEM
    scratch = [
        V((frames, 2, J, C), BF16),
        V((27 * C, C), BF16),
        V((2, tp, J, C), BF16),
        V((2, 2, fr, C), BF16),
        V((2, tp, J, C), BF16),
        V((2, 4, fr, C), BF16),
        V((wide + 16, C), F32),
        V((4 * wide, 3 * C), BF16),
        V((3, 2, wide + 16, C), F32),
        V((fr, 2, J, C), BF16),
        V((MOST, nf, 2, J, C), BF16),
        V((nf, 8, SUM_LANES), F32),
        V((nf, 8, SUM_LANES), F32),
        V((2, ny, 8, SUM_LANES), F32),
        V((2, nx, 8, SUM_LANES), F32),
        V((fr, SUM_LANES), F32),
        V((MOST, 2, nf, J, C), BF16),
        V((MOST, 2, nf, J, C), BF16),
        V((MOST, 2, width, C), BF16),
        V((MOST, 2, width, C), BF16),
        V((width + 16, C), F32),
        V((4 * width, 3 * C), BF16),
        V((2, nh * su, 8, C), BF16),
        V((2, 9 * C, C), BF16),
        V((2, 8, C), F32),
        V((2, 8, C), F32),
        V((2, 8, C), F32),
        V((MOST, 2, width, C), BF16),
        pltpu.SMEM((nf,), jnp.int32),
        dma((2,)), dma((8,)), dma((8,)), dma((2,)),
        dma((2,)), dma((2,)), dma((2,)), dma((2,)), dma((2,)), dma((2,)),
        dma, dma((MOST,)), dma, dma, dma((2,)), dma((2,)), dma((2,)), dma((2,)),
        dma((MOST, 2)), dma((MOST, 2)), dma((MOST, 2)), dma((MOST, 2)), dma((MOST,)),
    ]
    return pl.pallas_call(
        functools.partial(kernel, nf, nx, ny, frames, su, cells),
        out_shape=jax.ShapeDtypeStruct((MOST, 2, width, C), BF16),
        in_specs=[pl.BlockSpec(memory_space=pltpu.SMEM)] + [anyspace] * 4 + [vm] * 7,
        out_specs=anyspace,
        scratch_shapes=scratch,
        compiler_params=pltpu.CompilerParams(
            collective_id=0, has_side_effects=True, vmem_limit_bytes=60 * 2**20
        ),
        name="block",
    )(
        counts, video, tw, w1.reshape(su, 8, C), w2.reshape(su, 8, C),
        row(tb), row(g1), row(s1), row(b1), row(g2), row(s2), row(b2),
    )


def solution(mesh):
    placed = (
        P(None, "height", "frame", None),
        P(), P(), P(), P(), P(),
        P("height", None),
        P(), P(), P(),
        P("height", None),
        P(),
    )
    return jax.shard_map(
        functools.partial(per_device, mesh.shape["frame"], mesh.shape["height"]),
        mesh=mesh,
        in_specs=placed,
        out_specs=P("frame", "height", None, None),
        check_vma=False,
    )
```

```python
import functools

import jax
import jax.numpy as jnp
from jax import lax
from jax.experimental import pallas as pl
from jax.experimental.pallas import tpu as pltpu
from jax.sharding import PartitionSpec as P

GROUPS = 32
C = 256
J = 8
MOST = 6
F32 = jnp.float32
BF16 = jnp.bfloat16
HIGH = lax.Precision.HIGHEST
MESH = pl.DeviceIdType.MESH
SUM_LANES = 128


def silu(v):
    half = 0.5 * v
    return half * jnp.tanh(half) + half


def hdot(a, b):
    return jnp.dot(a, b, precision=HIGH, preferred_element_type=F32)


def one_hot(rows, cols, fn):
    r = lax.broadcasted_iota(jnp.int32, (rows, cols), 0)
    c = lax.broadcasted_iota(jnp.int32, (rows, cols), 1)
    return jnp.where(fn(r, c), 1.0, 0.0).astype(F32)


def kernel(
    nf, nx, ny, frames, su, cells,
    counts, video, tw, w1, w2, tb_in, g1_in, s1_in, b1_in, g2_in, s2_in, b2_in,
    out,
    vid, twv, rowb, colb, hr, hc, gt, se, tc, bs, stage, sts, rs, ysc, xsc, fsb,
    rec, ha, hb, first, g4, so, wb, wr, stat, mu, sc, outv, pv, offs,
    local_sem, p1_send, p1_recv, wl_sem, wy_send, wy_recv, wx_send, wx_recv, wp_send, wp_recv,
    a2a_send, a2a_recv, st_send, st_recv, y_send, y_recv, x_send, x_recv,
    ha_send, ha_recv, hb_send, hb_recv, out_sem, pv_sem, known,
):
    nh = nx * ny
    tp = frames + 1
    wide = tp * J
    fr = bs.shape[0]
    width = nf * J
    f = lax.axis_index("frame")
    h = lax.axis_index("height")
    x = h // ny
    y = lax.rem(h, ny)
    core = lax.rem(f, 2)
    hup, hdn = lax.rem(h + nh - 1, nh), lax.rem(h + 1, nh)
    fl, fr_ = lax.rem(f + nf - 1, nf), lax.rem(f + 1, nf)

    def dev(hh, ff):
        return {"height": hh, "frame": ff}

    def remote(src, dst, send, recv, hh, ff):
        return pltpu.make_async_remote_copy(
            src_ref=src, dst_ref=dst, send_sem=send, recv_sem=recv,
            device_id=dev(hh, ff), device_id_type=MESH,
        )

    def await_bytes(ref, sem):
        pltpu.make_async_copy(ref, ref, sem).wait()

    barrier = pltpu.get_barrier_semaphore()

    def greet(sem, hh, ff):
        pl.semaphore_signal(sem, inc=1, device_id=dev(hh, ff), device_id_type=MESH)

    def on_z(s):
        return h, lax.rem(f + nf + s, nf)

    def on_y(s):
        return x * ny + lax.rem(y + ny + s, ny), f

    def on_x(s):
        return lax.rem(x + nx + s, nx) * ny + y, f

    near = [(hup, f), (hdn, f), (hup, fl), (hup, fr_), (hdn, fl), (hdn, fr_)]
    for step in (-1, 1):
        near += [on_z(step), on_y(step), on_x(step)]
    for hh, ff in near:
        greet(barrier, hh, ff)

    copy_video = pltpu.make_async_copy(video, vid, local_sem.at[0])
    copy_video.start()
    copy_tw = pltpu.make_async_copy(tw, twv, local_sem.at[1])
    copy_tw.start()
    lane0 = pl.multiple_of(core * 128, 128)
    lanes = pl.ds(lane0, 128)
    mine = pl.ds(h * su, su)
    own_w = [
        pltpu.make_async_copy(w.at[:, :, lanes], wb.at[i, mine, :, lanes], wl_sem.at[i])
        for i, w in enumerate((w1, w2))
    ]
    for copy in own_w:
        copy.start()

    vectors = [
        pltpu.make_async_copy(v, pv.at[n], pv_sem.at[n])
        for n, v in enumerate((tb_in, g1_in, s1_in, b1_in, g2_in, s2_in, b2_in))
    ]
    for copy in vectors:
        copy.start()
    tb, g1, s1, b1, g2, s2, b2 = (pv.at[n] for n in range(7))

    total = jnp.int32(0)
    for k in range(nf):
        offs[k] = total
        total = total + counts[k]

    zero8 = jnp.zeros((8, C), F32)
    gt[0:8, :] = zero8
    gt[8 + wide : 16 + wide, :] = zero8
    g4[0:8, :] = zero8
    g4[8 + width : 16 + width, :] = zero8
    for a in range(3):
        for i in range(2):
            tc[a, i, 0:16, :] = jnp.zeros((16, C), F32)

    pick_left = one_hot(fr, wide, lambda r, c: c == r * J).astype(BF16)
    pick_right = one_hot(fr, wide, lambda r, c: c == r * J + J - 1).astype(BF16)

    copy_video.wait()
    for i in range(2):
        act = silu(vid[:, i].astype(F32)).astype(BF16)
        rowb[i, 0:frames] = act
        rowb[i, frames:tp] = jnp.zeros((1, J, C), BF16)
        flat = rowb[i].astype(F32).reshape(wide, C).astype(BF16)
        colb[0, i] = jnp.dot(pick_left, flat, preferred_element_type=F32).astype(BF16)
        colb[1, i] = jnp.dot(pick_right, flat, preferred_element_type=F32).astype(BF16)

    pl.semaphore_wait(barrier, len(near))

    borders = [
        (rowb.at[0], hr.at[1], hup, f),
        (rowb.at[1], hr.at[0], hdn, f),
        (colb.at[0], hc.at[1, 1:3], h, fl),
        (colb.at[1], hc.at[0, 1:3], h, fr_),
        (colb.at[0, 0], hc.at[1, 3], hup, fl),
        (colb.at[1, 0], hc.at[0, 3], hup, fr_),
        (colb.at[0, 1], hc.at[1, 0], hdn, fl),
        (colb.at[1, 1], hc.at[0, 0], hdn, fr_),
    ]
    p1 = [
        remote(src, dst, p1_send.at[n], p1_recv.at[n], hh, ff)
        for n, (src, dst, hh, ff) in enumerate(borders)
    ]
    for copy in p1:
        copy.start()

    rings = ((on_z, nf), (on_y, ny), (on_x, nx))
    reach = 1
    while reach < nf // 2:
        for n, (on, size) in enumerate(rings):
            if reach < size // 2:
                for step in (-reach, reach):
                    greet(known.at[n, reach // 2], *on(step))
        for n, (on, size) in enumerate(rings):
            if reach < size // 2:
                pl.semaphore_wait(known.at[n, reach // 2], 2)
        reach *= 2

    for copy in p1:
        copy.wait()

    for copy in own_w:
        copy.wait()
    for i in range(2):
        for s in range(1, ny):
            here = wb.at[i, mine, :, lanes]
            remote(here, here, wy_send.at[i], wy_recv.at[i], *on_y(s)).start()

    put_left = one_hot(wide, fr, lambda r, c: r == c * J).astype(BF16)
    put_right = one_hot(wide, fr, lambda r, c: r == c * J + J - 1).astype(BF16)
    col = lax.rem(lax.broadcasted_iota(jnp.int32, (wide, C), 0), J)
    keep_left = jnp.where(f > 0, 1.0, 0.0)
    keep_right = jnp.where(f < nf - 1, 1.0, 0.0)
    keep_top = jnp.where(h > 0, 1.0, 0.0)
    keep_bottom = jnp.where(h < nh - 1, 1.0, 0.0)
    for ip in range(4):
        source = (hr.at[0], rowb.at[0], rowb.at[1], hr.at[1])[ip]
        keep = (keep_top, 1.0, 1.0, keep_bottom)[ip]
        middle = source[...].astype(F32).reshape(wide, C) * keep
        gt[8 : 8 + wide, :] = middle
        lefts = jnp.dot(put_left, hc[0, ip], preferred_element_type=F32) * (keep * keep_left)
        rights = jnp.dot(put_right, hc[1, ip], preferred_element_type=F32) * (keep * keep_right)
        rows = slice(ip * wide, (ip + 1) * wide)
        se[rows, 0:C] = jnp.where(col == 0, lefts, gt[7 : 7 + wide, :]).astype(BF16)
        se[rows, C : 2 * C] = middle.astype(BF16)
        se[rows, 2 * C : 3 * C] = jnp.where(col == J - 1, rights, gt[9 : 9 + wide, :]).astype(BF16)
    copy_tw.wait()
    for copy in vectors:
        copy.wait()

    def taps(a, carry):
        for i in range(2):
            acc = jnp.zeros((wide, C), F32)
            for b in range(3):
                start = pl.multiple_of(a * (9 * C) + b * (3 * C), 3 * C)
                acc = acc + jnp.dot(
                    se[(i + b) * wide : (i + b + 1) * wide, :],
                    twv[pl.ds(start, 3 * C), :],
                    preferred_element_type=F32,
                )
            tc[a, i, 16 : 16 + wide, :] = acc
        return carry

    lax.fori_loop(0, 3, taps, 0)

    n_all = frames * J
    sums = jnp.zeros((n_all, C), F32)
    squares = jnp.zeros((n_all, C), F32)
    for i in range(2):
        value = (
            vid[:, i].astype(F32).reshape(n_all, C)
            + (tc[0, i, 0:n_all, :] + tc[1, i, 8 : 8 + n_all, :] + tc[2, i, 16 : 16 + n_all, :])
            + tb[...]
        )
        bs[0:frames, i] = value.reshape(frames, J, C).astype(BF16)
        rounded = bs[0:frames, i].astype(F32).reshape(n_all, C)
        sums = sums + rounded
        squares = squares + rounded * rounded
        bs[frames:fr, i] = jnp.zeros((fr - frames, J, C), BF16)

    per = C // GROUPS
    sum_map = one_hot(C, SUM_LANES, lambda r, c: c == r // per)
    sq_map = one_hot(C, SUM_LANES, lambda r, c: c == r // per + GROUPS)
    fsum = jnp.sum(sums.reshape(frames, J, C), axis=1)
    fsq = jnp.sum(squares.reshape(frames, J, C), axis=1)
    fsb[0:frames, :] = hdot(fsum, sum_map) + hdot(fsq, sq_map)
    fsb[frames:fr, :] = jnp.zeros((fr - frames, SUM_LANES), F32)

    def pack(k, carry):
        start = offs[k]
        sts[k] = fsb[pl.ds(start, 8), :]
        for r in range(MOST):
            stage[r, k] = bs[start + r]
        return carry

    lax.fori_loop(0, nf, pack, 0)

    def send_sums(s, carry):
        k = lax.rem(f + s, nf)
        remote(sts.at[k], rs.at[f], st_send, st_recv, h, k).start()
        return carry

    lax.fori_loop(1, nf, send_sums, 0)

    def send_slot(n, carry):
        r = n // (nf - 1)
        k = lax.rem(f + 1 + lax.rem(n, nf - 1), nf)
        remote(stage.at[r, k], rec.at[r, :, f], a2a_send, a2a_recv.at[r], h, k).start()
        return carry

    lax.fori_loop(0, MOST * (nf - 1), send_slot, 0)
    my_offset = offs[f]
    rs[f] = fsb[pl.ds(my_offset, 8), :]
    for r in range(MOST):
        rec[r, :, f] = bs[my_offset + r]

    block = pl.ds(x * (ny * su), ny * su)

    def along_x(i):
        await_bytes(wb.at[i, pl.ds(0, (ny - 1) * su), :, lanes], wy_recv.at[i])
        for s in range(1, nx):
            here = wb.at[i, block, :, lanes]
            remote(here, here, wx_send.at[i], wx_recv.at[i], *on_x(s)).start()

    partner = f + 1 - 2 * core
    other = pl.ds(pl.multiple_of(128 - core * 128, 128), 128)

    def to_partner(i):
        await_bytes(wb.at[i, pl.ds(0, (nx - 1) * ny * su), :, lanes], wx_recv.at[i])
        half = wb.at[i, :, :, lanes]
        remote(half, half, wp_send.at[i], wp_recv.at[i], h, partner).start()

    def y_start(q, value):
        ysc[q, y] = value
        for s in range(1, ny):
            remote(
                ysc.at[q, y], ysc.at[q, y], y_send.at[q], y_recv.at[q],
                *on_y(s),
            ).start()

    def y_finish(q):
        await_bytes(ysc.at[q, 0 : ny - 1], y_recv.at[q])
        return jnp.sum(ysc[q], axis=0)

    def x_start(q, value):
        xsc[q, x] = value
        for s in range(1, nx):
            remote(
                xsc.at[q, x], xsc.at[q, x], x_send.at[q], x_recv.at[q],
                *on_x(s),
            ).start()

    def x_finish(q):
        await_bytes(xsc.at[q, 0 : nx - 1], x_recv.at[q])
        return jnp.sum(xsc[q], axis=0)

    def set_norm(q, totals, gain):
        sum_back = one_hot(SUM_LANES, C, lambda r, c: r == c // per)
        sq_back = one_hot(SUM_LANES, C, lambda r, c: r == c // per + GROUPS)
        mean = hdot(totals, sum_back) / cells
        var = hdot(totals, sq_back) / cells - mean * mean
        mu[q] = mean
        sc[q] = lax.rsqrt(jnp.maximum(var, 0.0) + 1e-06) * gain

    def ready_weight(i):
        await_bytes(wb.at[i, :, :, other], wp_recv.at[i])
        step = 18

        def widen(n, carry):
            rows = wb[i, pl.ds(n * step, step)].astype(F32).reshape(step * 8, C)
            wr[i, pl.ds(pl.multiple_of(n * step * 8, step * 8), step * 8), :] = rows.astype(BF16)
            return carry

        lax.fori_loop(0, nh * su // step, widen, 0)

    def slot_in(r):
        await_bytes(rec.at[r, :, 0 : nf - 1], a2a_recv.at[r])
        remote(rec.at[r, 0], ha.at[r, 1], ha_send.at[r, 0], ha_recv.at[r, 0], hup, f).start()
        remote(rec.at[r, 1], ha.at[r, 0], ha_send.at[r, 1], ha_recv.at[r, 1], hdn, f).start()

    along_x(0)
    await_bytes(rs.at[0 : nf - 1], st_recv)
    y_start(0, jnp.sum(rs[...], axis=0))
    slot_in(0)
    x_start(0, y_finish(0))
    along_x(1)
    slot_in(1)
    set_norm(0, x_finish(0), g1[...])
    to_partner(0)

    keeps = (keep_top, None, None, keep_bottom)

    def convolve(r, rows_of, q, shift, weight):
        mean = mu[q, pl.ds(r, 1), :]
        scale = sc[q, pl.ds(r, 1), :]
        for ip in range(4):
            normed = silu((rows_of(ip) - mean) * scale + shift)
            if keeps[ip] is not None:
                normed = normed * keeps[ip]
            g4[8 : 8 + width, :] = normed
            rows = slice(ip * width, (ip + 1) * width)
            so[rows, 0:C] = g4[7 : 7 + width, :].astype(BF16)
            so[rows, C : 2 * C] = normed.astype(BF16)
            so[rows, 2 * C : 3 * C] = g4[9 : 9 + width, :].astype(BF16)
        acc = jnp.zeros((2 * width, C), F32)
        for b in range(3):
            acc = acc + jnp.dot(
                so[b * width : (b + 2) * width, :],
                wr[weight, b * 3 * C : (b + 1) * 3 * C, :],
                preferred_element_type=F32,
            )
        return acc

    def first_rows(r):
        def get(ip):
            ref = (ha.at[r, 0], rec.at[r, 0], rec.at[r, 1], ha.at[r, 1])[ip]
            return ref[...].astype(F32).reshape(width, C)

        return get

    def second_rows(r):
        def get(ip):
            ref = (hb.at[r, 0], first.at[r, 0], first.at[r, 1], hb.at[r, 1])[ip]
            return ref[...].astype(F32)

        return get

    stat[...] = jnp.zeros_like(stat)
    split = MOST - 2

    def sums_start(q):
        y_start(q, hdot(stat[0], sum_map) + hdot(stat[1], sq_map))

    def first_conv(r, carry):
        @pl.when(r + 2 < MOST)
        def _():
            slot_in(r + 2)

        @pl.when(r == 0)
        def _():
            ready_weight(0)

        await_bytes(ha.at[r, 0], ha_recv.at[r, 0])
        await_bytes(ha.at[r, 1], ha_recv.at[r, 1])
        result = convolve(r, first_rows(r), 0, s1[...], 0) + b1[...]
        first[r, 0] = result[0:width].astype(BF16)
        first[r, 1] = result[width : 2 * width].astype(BF16)
        rounded = first[r, 0].astype(F32), first[r, 1].astype(F32)
        sums = rounded[0] + rounded[1]
        squares = rounded[0] * rounded[0] + rounded[1] * rounded[1]
        stat[0, pl.ds(r, 1), :] = jnp.sum(sums, axis=0, keepdims=True)
        stat[1, pl.ds(r, 1), :] = jnp.sum(squares, axis=0, keepdims=True)

        @pl.when(r == split - 1)
        def _():
            sums_start(1)

        @pl.when(r == MOST - 1)
        def _():
            sums_start(2)

        remote(first.at[r, 0], hb.at[r, 1], hb_send.at[r, 0], hb_recv.at[r, 0], hup, f).start()
        remote(first.at[r, 1], hb.at[r, 0], hb_send.at[r, 1], hb_recv.at[r, 1], hdn, f).start()

        @pl.when(r == split - 1)
        def _():
            to_partner(1)

        return carry

    lax.fori_loop(0, MOST, first_conv, 0)
    x_start(1, y_finish(1))
    ready_weight(1)
    x_start(2, y_finish(2))
    set_norm(1, x_finish(1), g2[...])

    my_count = counts[f]

    def second_conv(q, r, carry):
        await_bytes(hb.at[r, 0], hb_recv.at[r, 0])
        await_bytes(hb.at[r, 1], hb_recv.at[r, 1])
        result = convolve(r, second_rows(r), q, s2[...], 1) + b2[...]
        live = r < my_count
        for i in range(2):
            kept = rec[r, i].astype(F32).reshape(width, C)
            value = kept + result[i * width : (i + 1) * width]
            outv[r, i] = jnp.where(live, value, 0.0).astype(BF16)
        pltpu.make_async_copy(outv.at[r], out.at[r], out_sem.at[r]).start()
        return carry

    lax.fori_loop(0, split, functools.partial(second_conv, 1), 0)
    set_norm(2, x_finish(2), g2[...])
    lax.fori_loop(split, MOST, functools.partial(second_conv, 2), 0)

    for i in range(2):
        await_bytes(wb.at[i, pl.ds(0, (ny - 1) * su), :, lanes], wy_send.at[i])
        await_bytes(wb.at[i, pl.ds(0, (nx - 1) * ny * su), :, lanes], wx_send.at[i])
        await_bytes(wb.at[i, :, :, lanes], wp_send.at[i])
    await_bytes(sts.at[0 : nf - 1], st_send)
    await_bytes(stage.at[:, 0 : nf - 1], a2a_send)
    for q in range(3):
        await_bytes(ysc.at[q, 0 : ny - 1], y_send.at[q])
        await_bytes(xsc.at[q, 0 : nx - 1], x_send.at[q])
    for r in range(MOST):
        for i in range(2):
            await_bytes(rec.at[r, i], ha_send.at[r, i])
            await_bytes(first.at[r, i], hb_send.at[r, i])
        pltpu.make_async_copy(outv.at[r], out.at[r], out_sem.at[r]).wait()


def per_device(nf, nh, video, counts, tw, tb, g1, s1, w1, b1, g2, s2, w2, b2):
    frames = video.shape[0]
    ny = 8 if nh % 8 == 0 else 2
    nx = nh // ny
    su = w1.shape[0] // 8
    tp = frames + 1
    wide = tp * J
    fr = -(-(frames + 7) // 8) * 8
    width = nf * J
    cells = float(2 * nh * width * (C // GROUPS))
    row = lambda v: v.reshape(1, C)
    anyspace = pl.BlockSpec(memory_space=pl.ANY)
    dma = pltpu.SemaphoreType.DMA
    V = pltpu.VMEM
    scratch = [
        V((frames, 2, J, C), BF16),
        V((27 * C, C), BF16),
        V((2, tp, J, C), BF16),
        V((2, 2, fr, C), BF16),
        V((2, tp, J, C), BF16),
        V((2, 4, fr, C), BF16),
        V((wide + 16, C), F32),
        V((4 * wide, 3 * C), BF16),
        V((3, 2, wide + 16, C), F32),
        V((fr, 2, J, C), BF16),
        V((MOST, nf, 2, J, C), BF16),
        V((nf, 8, SUM_LANES), F32),
        V((nf, 8, SUM_LANES), F32),
        V((3, ny, 8, SUM_LANES), F32),
        V((3, nx, 8, SUM_LANES), F32),
        V((fr, SUM_LANES), F32),
        V((MOST, 2, nf, J, C), BF16),
        V((MOST, 2, nf, J, C), BF16),
        V((MOST, 2, width, C), BF16),
        V((MOST, 2, width, C), BF16),
        V((width + 16, C), F32),
        V((4 * width, 3 * C), BF16),
        V((2, nh * su, 8, C), BF16),
        V((2, 9 * C, C), BF16),
        V((2, 8, C), F32),
        V((3, 8, C), F32),
        V((3, 8, C), F32),
        V((MOST, 2, width, C), BF16),
        V((7, 1, C), F32),
        pltpu.SMEM((nf,), jnp.int32),
        dma((2,)), dma((8,)), dma((8,)), dma((2,)),
        dma((2,)), dma((2,)), dma((2,)), dma((2,)), dma((2,)), dma((2,)),
        dma, dma((MOST,)), dma, dma, dma((3,)), dma((3,)), dma((3,)), dma((3,)),
        dma((MOST, 2)), dma((MOST, 2)), dma((MOST, 2)), dma((MOST, 2)), dma((MOST,)), dma((7,)),
        pltpu.SemaphoreType.REGULAR((3, 3)),
    ]
    return pl.pallas_call(
        functools.partial(kernel, nf, nx, ny, frames, su, cells),
        out_shape=jax.ShapeDtypeStruct((MOST, 2, width, C), BF16),
        in_specs=[pl.BlockSpec(memory_space=pltpu.SMEM)] + [anyspace] * 11,
        out_specs=anyspace,
        scratch_shapes=scratch,
        compiler_params=pltpu.CompilerParams(
            collective_id=0, has_side_effects=True, vmem_limit_bytes=60 * 2**20
        ),
        name="block",
    )(
        counts, video, tw, w1.reshape(su, 8, C), w2.reshape(su, 8, C),
        row(tb), row(g1), row(s1), row(b1), row(g2), row(s2), row(b2),
    )


def solution(mesh):
    placed = (
        P(None, "height", "frame", None),
        P(), P(), P(), P(), P(),
        P("height", None),
        P(), P(), P(),
        P("height", None),
        P(),
    )
    return jax.shard_map(
        functools.partial(per_device, mesh.shape["frame"], mesh.shape["height"]),
        mesh=mesh,
        in_specs=placed,
        out_specs=P("frame", "height", None, None),
        check_vma=False,
    )
```

```python
import functools

import jax
import jax.numpy as jnp
from jax import lax
from jax.experimental import pallas as pl
from jax.experimental.pallas import tpu as pltpu
from jax.sharding import PartitionSpec as P

GROUPS = 32
C = 256
J = 8
MOST = 6
F32 = jnp.float32
BF16 = jnp.bfloat16
HIGH = lax.Precision.HIGHEST
MESH = pl.DeviceIdType.MESH
SUM_LANES = 128


def silu(v):
    half = 0.5 * v
    return half * jnp.tanh(half) + half


def hdot(a, b):
    return jnp.dot(a, b, precision=HIGH, preferred_element_type=F32)


def one_hot(rows, cols, fn):
    r = lax.broadcasted_iota(jnp.int32, (rows, cols), 0)
    c = lax.broadcasted_iota(jnp.int32, (rows, cols), 1)
    return jnp.where(fn(r, c), 1.0, 0.0).astype(F32)


def kernel(
    nf, nx, ny, frames, su, cells,
    counts, video, tw, w1, w2, tb_in, g1_in, s1_in, b1_in, g2_in, s2_in, b2_in,
    out,
    vid, twv, rowb, colb, hr, hc, gt, se, tc, bs, stage, sts, rs, ysc, xsc, fsb,
    rec, ha, hb, first, g4, so, wb, wr, stat, mu, sc, outv, pv, offs,
    local_sem, p1_send, p1_recv, wl_sem, wy_send, wy_recv, wx_send, wx_recv, wp_send, wp_recv,
    a2a_send, a2a_recv, st_send, st_recv, y_send, y_recv, x_send, x_recv,
    ha_send, ha_recv, hb_send, hb_recv, out_sem, pv_sem, known,
):
    nh = nx * ny
    tp = frames + 1
    wide = tp * J
    fr = bs.shape[0]
    width = nf * J
    f = lax.axis_index("frame")
    h = lax.axis_index("height")
    x = h // ny
    y = lax.rem(h, ny)
    core = lax.rem(f, 2)
    hup, hdn = lax.rem(h + nh - 1, nh), lax.rem(h + 1, nh)
    fl, fr_ = lax.rem(f + nf - 1, nf), lax.rem(f + 1, nf)

    def dev(hh, ff):
        return {"height": hh, "frame": ff}

    def remote(src, dst, send, recv, hh, ff):
        return pltpu.make_async_remote_copy(
            src_ref=src, dst_ref=dst, send_sem=send, recv_sem=recv,
            device_id=dev(hh, ff), device_id_type=MESH,
        )

    def await_bytes(ref, sem):
        pltpu.make_async_copy(ref, ref, sem).wait()

    barrier = pltpu.get_barrier_semaphore()

    def greet(sem, hh, ff):
        pl.semaphore_signal(sem, inc=1, device_id=dev(hh, ff), device_id_type=MESH)

    def on_z(s):
        return h, lax.rem(f + nf + s, nf)

    def on_y(s):
        return x * ny + lax.rem(y + ny + s, ny), f

    def on_x(s):
        return lax.rem(x + nx + s, nx) * ny + y, f

    near = [(hup, f), (hdn, f), (hup, fl), (hup, fr_), (hdn, fl), (hdn, fr_)]
    for step in (-1, 1):
        near += [on_z(step), on_y(step), on_x(step)]
    for hh, ff in near:
        greet(barrier, hh, ff)

    copy_video = pltpu.make_async_copy(video, vid, local_sem.at[0])
    copy_video.start()
    copy_tw = pltpu.make_async_copy(tw, twv, local_sem.at[1])
    copy_tw.start()
    lane0 = pl.multiple_of(core * 128, 128)
    lanes = pl.ds(lane0, 128)
    mine = pl.ds(h * su, su)
    own_w = [
        pltpu.make_async_copy(w.at[:, :, lanes], wb.at[i, mine, :, lanes], wl_sem.at[i])
        for i, w in enumerate((w1, w2))
    ]
    for copy in own_w:
        copy.start()

    vectors = [
        pltpu.make_async_copy(v, pv.at[n], pv_sem.at[n])
        for n, v in enumerate((tb_in, g1_in, s1_in, b1_in, g2_in, s2_in, b2_in))
    ]
    for copy in vectors:
        copy.start()
    tb, g1, s1, b1, g2, s2, b2 = (pv.at[n] for n in range(7))

    for i in range(2):
        hr[i, frames:tp] = jnp.zeros((1, J, C), BF16)
    pl.semaphore_wait(barrier, len(near))

    rows_out = [
        remote(video.at[:, 0], hr.at[1, 0:frames], p1_send.at[0], p1_recv.at[0], hup, f),
        remote(video.at[:, 1], hr.at[0, 0:frames], p1_send.at[1], p1_recv.at[1], hdn, f),
    ]
    for copy in rows_out:
        copy.start()

    rings = ((0, on_z, nf), (1, on_y, ny), (2, on_x, nx))

    def tell(reach):
        for n, on, size in rings:
            if reach < size // 2:
                for step in (-reach, reach):
                    greet(known.at[n, reach // 2], *on(step))

    def hear(reach):
        for n, on, size in rings:
            if reach < size // 2:
                pl.semaphore_wait(known.at[n, reach // 2], 2)

    tell(1)
    zero8 = jnp.zeros((8, C), F32)
    gt[0:8, :] = zero8
    gt[8 + wide : 16 + wide, :] = zero8
    pick_left = one_hot(fr, wide, lambda r, c: c == r * J).astype(BF16)
    pick_right = one_hot(fr, wide, lambda r, c: c == r * J + J - 1).astype(BF16)
    copy_video.wait()
    for i in range(2):
        act = silu(vid[:, i].astype(F32)).astype(BF16)
        rowb[i, 0:frames] = act
        rowb[i, frames:tp] = jnp.zeros((1, J, C), BF16)
        flat = rowb[i].astype(F32).reshape(wide, C).astype(BF16)
        colb[0, i] = jnp.dot(pick_left, flat, preferred_element_type=F32).astype(BF16)
        colb[1, i] = jnp.dot(pick_right, flat, preferred_element_type=F32).astype(BF16)

    borders = [
        (colb.at[0], hc.at[1, 1:3], h, fl),
        (colb.at[1], hc.at[0, 1:3], h, fr_),
        (colb.at[0, 0], hc.at[1, 3], hup, fl),
        (colb.at[1, 0], hc.at[0, 3], hup, fr_),
        (colb.at[0, 1], hc.at[1, 0], hdn, fl),
        (colb.at[1, 1], hc.at[0, 0], hdn, fr_),
    ]
    cols_out = [
        remote(src, dst, p1_send.at[2 + n], p1_recv.at[2 + n], hh, ff)
        for n, (src, dst, hh, ff) in enumerate(borders)
    ]
    for copy in cols_out:
        copy.start()
    hear(1)
    tell(2)

    total = jnp.int32(0)
    for k in range(nf):
        offs[k] = total
        total = total + counts[k]
    g4[0:8, :] = zero8
    g4[8 + width : 16 + width, :] = zero8
    for a in range(3):
        for i in range(2):
            tc[a, i, 0:16, :] = jnp.zeros((16, C), F32)

    put_left = one_hot(wide, fr, lambda r, c: r == c * J).astype(BF16)
    put_right = one_hot(wide, fr, lambda r, c: r == c * J + J - 1).astype(BF16)
    col = lax.rem(lax.broadcasted_iota(jnp.int32, (wide, C), 0), J)
    keep_left = jnp.where(f > 0, 1.0, 0.0)
    keep_right = jnp.where(f < nf - 1, 1.0, 0.0)
    keep_top = jnp.where(h > 0, 1.0, 0.0)
    keep_bottom = jnp.where(h < nh - 1, 1.0, 0.0)

    def bordered(ip):
        keep = (keep_top, 1.0, 1.0, keep_bottom)[ip]
        if ip in (1, 2):
            middle = rowb[ip - 1].astype(F32).reshape(wide, C)
        else:
            raw = hr[ip // 3].astype(F32).reshape(wide, C)
            middle = silu(raw).astype(BF16).astype(F32) * keep
        gt[8 : 8 + wide, :] = middle
        lefts = jnp.dot(put_left, hc[0, ip], preferred_element_type=F32) * (keep * keep_left)
        rights = jnp.dot(put_right, hc[1, ip], preferred_element_type=F32) * (keep * keep_right)
        rows = slice(ip * wide, (ip + 1) * wide)
        se[rows, 0:C] = jnp.where(col == 0, lefts, gt[7 : 7 + wide, :]).astype(BF16)
        se[rows, C : 2 * C] = middle.astype(BF16)
        se[rows, 2 * C : 3 * C] = jnp.where(col == J - 1, rights, gt[9 : 9 + wide, :]).astype(BF16)

    def tap(a, i, b):
        start = pl.multiple_of(a * (9 * C) + b * (3 * C), 3 * C)
        return jnp.dot(
            se[(i + b) * wide : (i + b + 1) * wide, :],
            twv[pl.ds(start, 3 * C), :],
            preferred_element_type=F32,
        )

    def own_taps(a, carry):
        tc[a, 0, 16 : 16 + wide, :] = tap(a, 0, 1) + tap(a, 0, 2)
        tc[a, 1, 16 : 16 + wide, :] = tap(a, 1, 0) + tap(a, 1, 1)
        return carry

    def border_taps(a, carry):
        tc[a, 0, 16 : 16 + wide, :] += tap(a, 0, 0)
        tc[a, 1, 16 : 16 + wide, :] += tap(a, 1, 2)
        return carry

    for copy in cols_out[:2]:
        copy.wait()
    bordered(1)
    bordered(2)
    hear(2)
    tell(4)

    for copy in own_w:
        copy.wait()
    for i in range(2):
        for s in range(1, ny):
            here = wb.at[i, mine, :, lanes]
            remote(here, here, wy_send.at[i], wy_recv.at[i], *on_y(s)).start()

    copy_tw.wait()
    for copy in vectors:
        copy.wait()
    lax.fori_loop(0, 3, own_taps, 0)
    for copy in rows_out + cols_out[2:]:
        copy.wait()
    bordered(0)
    bordered(3)
    lax.fori_loop(0, 3, border_taps, 0)
    hear(4)

    n_all = frames * J
    sums = jnp.zeros((n_all, C), F32)
    squares = jnp.zeros((n_all, C), F32)
    for i in range(2):
        value = (
            vid[:, i].astype(F32).reshape(n_all, C)
            + (tc[0, i, 0:n_all, :] + tc[1, i, 8 : 8 + n_all, :] + tc[2, i, 16 : 16 + n_all, :])
            + tb[...]
        )
        bs[0:frames, i] = value.reshape(frames, J, C).astype(BF16)
        rounded = bs[0:frames, i].astype(F32).reshape(n_all, C)
        sums = sums + rounded
        squares = squares + rounded * rounded
        bs[frames:fr, i] = jnp.zeros((fr - frames, J, C), BF16)

    per = C // GROUPS
    sum_map = one_hot(C, SUM_LANES, lambda r, c: c == r // per)
    sq_map = one_hot(C, SUM_LANES, lambda r, c: c == r // per + GROUPS)
    fsum = jnp.sum(sums.reshape(frames, J, C), axis=1)
    fsq = jnp.sum(squares.reshape(frames, J, C), axis=1)
    fsb[0:frames, :] = hdot(fsum, sum_map) + hdot(fsq, sq_map)
    fsb[frames:fr, :] = jnp.zeros((fr - frames, SUM_LANES), F32)

    def pack(k, carry):
        start = offs[k]
        sts[k] = fsb[pl.ds(start, 8), :]
        for r in range(MOST):
            stage[r, k] = bs[start + r]
        return carry

    lax.fori_loop(0, nf, pack, 0)

    def send_sums(s, carry):
        k = lax.rem(f + s, nf)
        remote(sts.at[k], rs.at[f], st_send, st_recv, h, k).start()
        return carry

    lax.fori_loop(1, nf, send_sums, 0)

    def send_slot(n, carry):
        r = n // (nf - 1)
        k = lax.rem(f + 1 + lax.rem(n, nf - 1), nf)
        remote(stage.at[r, k], rec.at[r, :, f], a2a_send, a2a_recv.at[r], h, k).start()
        return carry

    lax.fori_loop(0, MOST * (nf - 1), send_slot, 0)
    my_offset = offs[f]
    rs[f] = fsb[pl.ds(my_offset, 8), :]
    for r in range(MOST):
        rec[r, :, f] = bs[my_offset + r]

    size = ny * su
    half = size // 2

    def block(s):
        return lax.rem(x + nx + s, nx) * size

    def x_copy(i, start, count, sem, step):
        here = wb.at[i, pl.ds(start, count), :, lanes]
        remote(here, here, wx_send.at[i, sem], wx_recv.at[i, sem], *on_x(step)).start()

    def x_await(i, count, sem, which):
        await_bytes(wb.at[i, pl.ds(0, count), :, lanes], which.at[i, sem])

    def both_first():
        await_bytes(wb.at[0, pl.ds(0, (ny - 1) * su), :, lanes], wy_recv.at[0])
        x_copy(0, block(0), size, 0, 1)
        if nx > 2:
            x_copy(0, block(0), size, 1, -1)

    def both_second():
        x_await(0, size, 0, wx_recv)
        if nx > 2:
            x_copy(0, block(-1), half, 2, 1)
            x_await(0, size, 1, wx_recv)
            x_copy(0, block(1) + half, half, 3, -1)

    def both_last():
        if nx > 2:
            x_await(0, half, 2, wx_recv)
            x_await(0, half, 3, wx_recv)

    way = 1 - 2 * ((ny - y) // ny)

    def one_way(n):
        if n == 0:
            await_bytes(wb.at[1, pl.ds(0, (ny - 1) * su), :, lanes], wy_recv.at[1])
        else:
            x_await(1, size, n - 1, wx_recv)
        if n < nx - 1:
            x_copy(1, block(-n * way), size, n, way)

    partner = f + 1 - 2 * core
    other = pl.ds(pl.multiple_of(128 - core * 128, 128), 128)

    def to_partner(i):
        mine_half = wb.at[i, :, :, lanes]
        remote(mine_half, mine_half, wp_send.at[i], wp_recv.at[i], h, partner).start()

    def y_start(q, value):
        ysc[q, y] = value
        for s in range(1, ny):
            remote(
                ysc.at[q, y], ysc.at[q, y], y_send.at[q], y_recv.at[q],
                *on_y(s),
            ).start()

    def y_finish(q):
        await_bytes(ysc.at[q, 0 : ny - 1], y_recv.at[q])
        return jnp.sum(ysc[q], axis=0)

    def x_start(q, value):
        xsc[q, x] = value
        for s in range(1, nx):
            remote(
                xsc.at[q, x], xsc.at[q, x], x_send.at[q], x_recv.at[q],
                *on_x(s),
            ).start()

    def x_finish(q):
        await_bytes(xsc.at[q, 0 : nx - 1], x_recv.at[q])
        return jnp.sum(xsc[q], axis=0)

    def set_norm(q, totals, gain):
        sum_back = one_hot(SUM_LANES, C, lambda r, c: r == c // per)
        sq_back = one_hot(SUM_LANES, C, lambda r, c: r == c // per + GROUPS)
        mean = hdot(totals, sum_back) / cells
        var = hdot(totals, sq_back) / cells - mean * mean
        mu[q] = mean
        sc[q] = lax.rsqrt(jnp.maximum(var, 0.0) + 1e-06) * gain

    def ready_weight(i):
        await_bytes(wb.at[i, :, :, other], wp_recv.at[i])
        step = 18

        def widen(n, carry):
            rows = wb[i, pl.ds(n * step, step)].astype(F32).reshape(step * 8, C)
            wr[i, pl.ds(pl.multiple_of(n * step * 8, step * 8), step * 8), :] = rows.astype(BF16)
            return carry

        lax.fori_loop(0, nh * su // step, widen, 0)

    def slot_in(r):
        await_bytes(rec.at[r, :, 0 : nf - 1], a2a_recv.at[r])
        remote(rec.at[r, 0], ha.at[r, 1], ha_send.at[r, 0], ha_recv.at[r, 0], hup, f).start()
        remote(rec.at[r, 1], ha.at[r, 0], ha_send.at[r, 1], ha_recv.at[r, 1], hdn, f).start()

    both_first()
    await_bytes(rs.at[0 : nf - 1], st_recv)
    y_start(0, jnp.sum(rs[...], axis=0))
    both_second()
    slot_in(0)
    x_start(0, y_finish(0))
    one_way(0)
    slot_in(1)
    both_last()
    to_partner(0)
    set_norm(0, x_finish(0), g1[...])

    keeps = (keep_top, None, None, keep_bottom)

    def convolve(r, rows_of, q, shift, weight):
        mean = mu[q, pl.ds(r, 1), :]
        scale = sc[q, pl.ds(r, 1), :]
        for ip in range(4):
            normed = silu((rows_of(ip) - mean) * scale + shift)
            if keeps[ip] is not None:
                normed = normed * keeps[ip]
            g4[8 : 8 + width, :] = normed
            rows = slice(ip * width, (ip + 1) * width)
            so[rows, 0:C] = g4[7 : 7 + width, :].astype(BF16)
            so[rows, C : 2 * C] = normed.astype(BF16)
            so[rows, 2 * C : 3 * C] = g4[9 : 9 + width, :].astype(BF16)
        acc = jnp.zeros((2 * width, C), F32)
        for b in range(3):
            acc = acc + jnp.dot(
                so[b * width : (b + 2) * width, :],
                wr[weight, b * 3 * C : (b + 1) * 3 * C, :],
                preferred_element_type=F32,
            )
        return acc

    def first_rows(r):
        def get(ip):
            ref = (ha.at[r, 0], rec.at[r, 0], rec.at[r, 1], ha.at[r, 1])[ip]
            return ref[...].astype(F32).reshape(width, C)

        return get

    def second_rows(r):
        def get(ip):
            ref = (hb.at[r, 0], first.at[r, 0], first.at[r, 1], hb.at[r, 1])[ip]
            return ref[...].astype(F32)

        return get

    stat[...] = jnp.zeros_like(stat)
    split = MOST - 2

    def sums_start(q):
        y_start(q, hdot(stat[0], sum_map) + hdot(stat[1], sq_map))

    def first_conv(r, carry):
        @pl.when(r + 2 < MOST)
        def _():
            slot_in(r + 2)

        @pl.when(r == 0)
        def _():
            ready_weight(0)

        await_bytes(ha.at[r, 0], ha_recv.at[r, 0])
        await_bytes(ha.at[r, 1], ha_recv.at[r, 1])
        result = convolve(r, first_rows(r), 0, s1[...], 0) + b1[...]
        first[r, 0] = result[0:width].astype(BF16)
        first[r, 1] = result[width : 2 * width].astype(BF16)
        rounded = first[r, 0].astype(F32), first[r, 1].astype(F32)
        sums = rounded[0] + rounded[1]
        squares = rounded[0] * rounded[0] + rounded[1] * rounded[1]
        stat[0, pl.ds(r, 1), :] = jnp.sum(sums, axis=0, keepdims=True)
        stat[1, pl.ds(r, 1), :] = jnp.sum(squares, axis=0, keepdims=True)

        @pl.when(r == split - 1)
        def _():
            sums_start(1)

        @pl.when(r == MOST - 1)
        def _():
            sums_start(2)

        remote(first.at[r, 0], hb.at[r, 1], hb_send.at[r, 0], hb_recv.at[r, 0], hup, f).start()
        remote(first.at[r, 1], hb.at[r, 0], hb_send.at[r, 1], hb_recv.at[r, 1], hdn, f).start()

        for n in range(1, nx - 1):

            @pl.when(r == 2 * n - 1)
            def _():
                one_way(n)

        return carry

    lax.fori_loop(0, MOST, first_conv, 0)
    one_way(nx - 1)
    to_partner(1)
    x_start(1, y_finish(1))
    x_start(2, y_finish(2))
    ready_weight(1)
    set_norm(1, x_finish(1), g2[...])

    my_count = counts[f]

    def second_conv(q, r, carry):
        await_bytes(hb.at[r, 0], hb_recv.at[r, 0])
        await_bytes(hb.at[r, 1], hb_recv.at[r, 1])
        result = convolve(r, second_rows(r), q, s2[...], 1) + b2[...]
        live = r < my_count
        for i in range(2):
            kept = rec[r, i].astype(F32).reshape(width, C)
            value = kept + result[i * width : (i + 1) * width]
            outv[r, i] = jnp.where(live, value, 0.0).astype(BF16)
        pltpu.make_async_copy(outv.at[r], out.at[r], out_sem.at[r]).start()
        return carry

    lax.fori_loop(0, split, functools.partial(second_conv, 1), 0)
    set_norm(2, x_finish(2), g2[...])
    lax.fori_loop(split, MOST, functools.partial(second_conv, 2), 0)

    for i in range(2):
        await_bytes(wb.at[i, pl.ds(0, (ny - 1) * su), :, lanes], wy_send.at[i])
        await_bytes(wb.at[i, :, :, lanes], wp_send.at[i])
    x_await(0, size, 0, wx_send)
    if nx > 2:
        x_await(0, size, 1, wx_send)
        x_await(0, half, 2, wx_send)
        x_await(0, half, 3, wx_send)
    for n in range(nx - 1):
        x_await(1, size, n, wx_send)
    await_bytes(sts.at[0 : nf - 1], st_send)
    await_bytes(stage.at[:, 0 : nf - 1], a2a_send)
    for q in range(3):
        await_bytes(ysc.at[q, 0 : ny - 1], y_send.at[q])
        await_bytes(xsc.at[q, 0 : nx - 1], x_send.at[q])
    for r in range(MOST):
        for i in range(2):
            await_bytes(rec.at[r, i], ha_send.at[r, i])
            await_bytes(first.at[r, i], hb_send.at[r, i])
        pltpu.make_async_copy(outv.at[r], out.at[r], out_sem.at[r]).wait()


def per_device(nf, nh, video, counts, tw, tb, g1, s1, w1, b1, g2, s2, w2, b2):
    frames = video.shape[0]
    ny = 8 if nh % 16 == 0 else 2
    nx = nh // ny
    su = w1.shape[0] // 8
    tp = frames + 1
    wide = tp * J
    fr = -(-(frames + 7) // 8) * 8
    width = nf * J
    cells = float(2 * nh * width * (C // GROUPS))
    row = lambda v: v.reshape(1, C)
    anyspace = pl.BlockSpec(memory_space=pl.ANY)
    dma = pltpu.SemaphoreType.DMA
    V = pltpu.VMEM
    scratch = [
        V((frames, 2, J, C), BF16),
        V((27 * C, C), BF16),
        V((2, tp, J, C), BF16),
        V((2, 2, fr, C), BF16),
        V((2, tp, J, C), BF16),
        V((2, 4, fr, C), BF16),
        V((wide + 16, C), F32),
        V((4 * wide, 3 * C), BF16),
        V((3, 2, wide + 16, C), F32),
        V((fr, 2, J, C), BF16),
        V((MOST, nf, 2, J, C), BF16),
        V((nf, 8, SUM_LANES), F32),
        V((nf, 8, SUM_LANES), F32),
        V((3, ny, 8, SUM_LANES), F32),
        V((3, nx, 8, SUM_LANES), F32),
        V((fr, SUM_LANES), F32),
        V((MOST, 2, nf, J, C), BF16),
        V((MOST, 2, nf, J, C), BF16),
        V((MOST, 2, width, C), BF16),
        V((MOST, 2, width, C), BF16),
        V((width + 16, C), F32),
        V((4 * width, 3 * C), BF16),
        V((2, nh * su, 8, C), BF16),
        V((2, 9 * C, C), BF16),
        V((2, 8, C), F32),
        V((3, 8, C), F32),
        V((3, 8, C), F32),
        V((MOST, 2, width, C), BF16),
        V((7, 1, C), F32),
        pltpu.SMEM((nf,), jnp.int32),
        dma((2,)), dma((8,)), dma((8,)), dma((2,)),
        dma((2,)), dma((2,)), dma((2, 4)), dma((2, 4)), dma((2,)), dma((2,)),
        dma, dma((MOST,)), dma, dma, dma((3,)), dma((3,)), dma((3,)), dma((3,)),
        dma((MOST, 2)), dma((MOST, 2)), dma((MOST, 2)), dma((MOST, 2)), dma((MOST,)), dma((7,)),
        pltpu.SemaphoreType.REGULAR((3, 3)),
    ]
    return pl.pallas_call(
        functools.partial(kernel, nf, nx, ny, frames, su, cells),
        out_shape=jax.ShapeDtypeStruct((MOST, 2, width, C), BF16),
        in_specs=[pl.BlockSpec(memory_space=pltpu.SMEM)] + [anyspace] * 11,
        out_specs=anyspace,
        scratch_shapes=scratch,
        compiler_params=pltpu.CompilerParams(
            collective_id=0, has_side_effects=True, vmem_limit_bytes=60 * 2**20
        ),
        name="block",
    )(
        counts, video, tw, w1.reshape(su, 8, C), w2.reshape(su, 8, C),
        row(tb), row(g1), row(s1), row(b1), row(g2), row(s2), row(b2),
    )


def solution(mesh):
    placed = (
        P(None, "height", "frame", None),
        P(), P(), P(), P(), P(),
        P("height", None),
        P(), P(), P(),
        P("height", None),
        P(),
    )
    return jax.shard_map(
        functools.partial(per_device, mesh.shape["frame"], mesh.shape["height"]),
        mesh=mesh,
        in_specs=placed,
        out_specs=P("frame", "height", None, None),
        check_vma=False,
    )
```

```python
import functools

import jax
import jax.numpy as jnp
from jax import lax
from jax.experimental import pallas as pl
from jax.experimental.pallas import tpu as pltpu
from jax.sharding import PartitionSpec as P

GROUPS = 32
C = 256
J = 8
MOST = 6
F32 = jnp.float32
BF16 = jnp.bfloat16
HIGH = lax.Precision.HIGHEST
MESH = pl.DeviceIdType.MESH
SUM_LANES = 128


def silu(v):
    half = 0.5 * v
    return half * jnp.tanh(half) + half


def hdot(a, b):
    return jnp.dot(a, b, precision=HIGH, preferred_element_type=F32)


def one_hot(rows, cols, fn):
    r = lax.broadcasted_iota(jnp.int32, (rows, cols), 0)
    c = lax.broadcasted_iota(jnp.int32, (rows, cols), 1)
    return jnp.where(fn(r, c), 1.0, 0.0).astype(F32)


def kernel(
    nf, nx, ny, frames, su, cells,
    counts, video, tw, w1, w2, tb_in, g1_in, s1_in, b1_in, g2_in, s2_in, b2_in,
    out,
    vid, twv, rowb, colb, hr, hc, gt, se, tc, bs, stage, sts, rs, ysc, xsc, fsb,
    rec, ha, first, g4, so, wb, wr, stat, mu, sc, outv, pv, offs,
    local_sem, p1_send, p1_recv, wl_sem, wy_send, wy_recv, wx_send, wx_recv, wp_send, wp_recv,
    a2a_send, a2a_recv, st_send, st_recv, y_send, y_recv, x_send, x_recv,
    ha_send, ha_recv, out_sem, pv_sem, known,
):
    nh = nx * ny
    tp = frames + 1
    wide = tp * J
    fr = bs.shape[0]
    width = nf * J
    f = lax.axis_index("frame")
    h = lax.axis_index("height")
    x = h // ny
    y = lax.rem(h, ny)
    core = lax.rem(f, 2)
    hup, hdn = lax.rem(h + nh - 1, nh), lax.rem(h + 1, nh)
    fl, fr_ = lax.rem(f + nf - 1, nf), lax.rem(f + 1, nf)

    def dev(hh, ff):
        return {"height": hh, "frame": ff}

    def remote(src, dst, send, recv, hh, ff):
        return pltpu.make_async_remote_copy(
            src_ref=src, dst_ref=dst, send_sem=send, recv_sem=recv,
            device_id=dev(hh, ff), device_id_type=MESH,
        )

    def await_bytes(ref, sem):
        pltpu.make_async_copy(ref, ref, sem).wait()

    barrier = pltpu.get_barrier_semaphore()

    def greet(sem, hh, ff):
        pl.semaphore_signal(sem, inc=1, device_id=dev(hh, ff), device_id_type=MESH)

    def on_z(s):
        return h, lax.rem(f + nf + s, nf)

    def on_y(s):
        return x * ny + lax.rem(y + ny + s, ny), f

    def on_x(s):
        return lax.rem(x + nx + s, nx) * ny + y, f

    near = [(hup, f), (hdn, f), (hup, fl), (hup, fr_), (hdn, fl), (hdn, fr_)]
    for step in (-1, 1):
        near += [on_z(step), on_y(step), on_x(step)]
    for hh, ff in near:
        greet(barrier, hh, ff)

    copy_video = pltpu.make_async_copy(video, vid, local_sem.at[0])
    copy_video.start()
    copy_tw = pltpu.make_async_copy(tw, twv, local_sem.at[1])
    copy_tw.start()
    lane0 = pl.multiple_of(core * 128, 128)
    lanes = pl.ds(lane0, 128)
    mine = pl.ds(h * su, su)
    own_w = [
        pltpu.make_async_copy(w.at[:, :, lanes], wb.at[i, mine, :, lanes], wl_sem.at[i])
        for i, w in enumerate((w1, w2))
    ]
    for copy in own_w:
        copy.start()

    vectors = [
        pltpu.make_async_copy(v, pv.at[n], pv_sem.at[n])
        for n, v in enumerate((tb_in, g1_in, s1_in, b1_in, g2_in, s2_in, b2_in))
    ]
    for copy in vectors:
        copy.start()
    tb, g1, s1, b1, g2, s2, b2 = (pv.at[n] for n in range(7))

    for i in range(2):
        hr[i, frames:tp] = jnp.zeros((1, J, C), BF16)
    pl.semaphore_wait(barrier, len(near))

    rows_out = [
        remote(video.at[:, 0], hr.at[1, 0:frames], p1_send.at[0], p1_recv.at[0], hup, f),
        remote(video.at[:, 1], hr.at[0, 0:frames], p1_send.at[1], p1_recv.at[1], hdn, f),
    ]
    for copy in rows_out:
        copy.start()

    rings = ((0, on_z, nf), (1, on_y, ny), (2, on_x, nx))

    def tell(reach):
        for n, on, size in rings:
            if reach < size // 2:
                for step in (-reach, reach):
                    greet(known.at[n, reach // 2], *on(step))

    def hear(reach):
        for n, on, size in rings:
            if reach < size // 2:
                pl.semaphore_wait(known.at[n, reach // 2], 2)

    tell(1)
    zero8 = jnp.zeros((8, C), F32)
    gt[0:8, :] = zero8
    gt[8 + wide : 16 + wide, :] = zero8
    pick_left = one_hot(fr, wide, lambda r, c: c == r * J).astype(BF16)
    pick_right = one_hot(fr, wide, lambda r, c: c == r * J + J - 1).astype(BF16)
    copy_video.wait()
    for i in range(2):
        act = silu(vid[:, i].astype(F32)).astype(BF16)
        rowb[i, 0:frames] = act
        rowb[i, frames:tp] = jnp.zeros((1, J, C), BF16)
        flat = rowb[i].astype(F32).reshape(wide, C).astype(BF16)
        colb[0, i] = jnp.dot(pick_left, flat, preferred_element_type=F32).astype(BF16)
        colb[1, i] = jnp.dot(pick_right, flat, preferred_element_type=F32).astype(BF16)

    borders = [
        (colb.at[0], hc.at[1, 1:3], h, fl),
        (colb.at[1], hc.at[0, 1:3], h, fr_),
        (colb.at[0, 0], hc.at[1, 3], hup, fl),
        (colb.at[1, 0], hc.at[0, 3], hup, fr_),
        (colb.at[0, 1], hc.at[1, 0], hdn, fl),
        (colb.at[1, 1], hc.at[0, 0], hdn, fr_),
    ]
    cols_out = [
        remote(src, dst, p1_send.at[2 + n], p1_recv.at[2 + n], hh, ff)
        for n, (src, dst, hh, ff) in enumerate(borders)
    ]
    for copy in cols_out:
        copy.start()
    hear(1)
    tell(2)

    total = jnp.int32(0)
    for k in range(nf):
        offs[k] = total
        total = total + counts[k]
    g4[0:8, :] = zero8
    g4[8 + width : 16 + width, :] = zero8
    for a in range(3):
        for i in range(2):
            tc[a, i, 0:16, :] = jnp.zeros((16, C), F32)

    put_left = one_hot(wide, fr, lambda r, c: r == c * J).astype(BF16)
    put_right = one_hot(wide, fr, lambda r, c: r == c * J + J - 1).astype(BF16)
    col = lax.rem(lax.broadcasted_iota(jnp.int32, (wide, C), 0), J)
    keep_left = jnp.where(f > 0, 1.0, 0.0)
    keep_right = jnp.where(f < nf - 1, 1.0, 0.0)
    keep_top = jnp.where(h > 0, 1.0, 0.0)
    keep_bottom = jnp.where(h < nh - 1, 1.0, 0.0)

    def bordered(ip):
        keep = (keep_top, 1.0, 1.0, keep_bottom)[ip]
        if ip in (1, 2):
            middle = rowb[ip - 1].astype(F32).reshape(wide, C)
        else:
            raw = hr[ip // 3].astype(F32).reshape(wide, C)
            middle = silu(raw).astype(BF16).astype(F32) * keep
        gt[8 : 8 + wide, :] = middle
        lefts = jnp.dot(put_left, hc[0, ip], preferred_element_type=F32) * (keep * keep_left)
        rights = jnp.dot(put_right, hc[1, ip], preferred_element_type=F32) * (keep * keep_right)
        rows = slice(ip * wide, (ip + 1) * wide)
        se[rows, 0:C] = jnp.where(col == 0, lefts, gt[7 : 7 + wide, :]).astype(BF16)
        se[rows, C : 2 * C] = middle.astype(BF16)
        se[rows, 2 * C : 3 * C] = jnp.where(col == J - 1, rights, gt[9 : 9 + wide, :]).astype(BF16)

    def tap(a, i, b):
        start = pl.multiple_of(a * (9 * C) + b * (3 * C), 3 * C)
        return jnp.dot(
            se[(i + b) * wide : (i + b + 1) * wide, :],
            twv[pl.ds(start, 3 * C), :],
            preferred_element_type=F32,
        )

    def own_taps(a, carry):
        tc[a, 0, 16 : 16 + wide, :] = tap(a, 0, 1) + tap(a, 0, 2)
        tc[a, 1, 16 : 16 + wide, :] = tap(a, 1, 0) + tap(a, 1, 1)
        return carry

    def border_taps(a, carry):
        tc[a, 0, 16 : 16 + wide, :] += tap(a, 0, 0)
        tc[a, 1, 16 : 16 + wide, :] += tap(a, 1, 2)
        return carry

    for copy in cols_out[:2]:
        copy.wait()
    bordered(1)
    bordered(2)
    hear(2)
    tell(4)

    for copy in own_w:
        copy.wait()
    for i in range(2):
        for s in range(1, ny):
            here = wb.at[i, mine, :, lanes]
            remote(here, here, wy_send.at[i], wy_recv.at[i], *on_y(s)).start()

    copy_tw.wait()
    for copy in vectors:
        copy.wait()
    lax.fori_loop(0, 3, own_taps, 0)
    for copy in rows_out + cols_out[2:]:
        copy.wait()
    bordered(0)
    bordered(3)
    lax.fori_loop(0, 3, border_taps, 0)
    hear(4)

    n_all = frames * J
    sums = jnp.zeros((n_all, C), F32)
    squares = jnp.zeros((n_all, C), F32)
    for i in range(2):
        value = (
            vid[:, i].astype(F32).reshape(n_all, C)
            + (tc[0, i, 0:n_all, :] + tc[1, i, 8 : 8 + n_all, :] + tc[2, i, 16 : 16 + n_all, :])
            + tb[...]
        )
        bs[0:frames, i] = value.reshape(frames, J, C).astype(BF16)
        rounded = bs[0:frames, i].astype(F32).reshape(n_all, C)
        sums = sums + rounded
        squares = squares + rounded * rounded
        bs[frames:fr, i] = jnp.zeros((fr - frames, J, C), BF16)

    per = C // GROUPS
    sum_map = one_hot(C, SUM_LANES, lambda r, c: c == r // per)
    sq_map = one_hot(C, SUM_LANES, lambda r, c: c == r // per + GROUPS)
    fsum = jnp.sum(sums.reshape(frames, J, C), axis=1)
    fsq = jnp.sum(squares.reshape(frames, J, C), axis=1)
    fsb[0:frames, :] = hdot(fsum, sum_map) + hdot(fsq, sq_map)
    fsb[frames:fr, :] = jnp.zeros((fr - frames, SUM_LANES), F32)

    def pack(k, carry):
        start = offs[k]
        sts[k] = fsb[pl.ds(start, 8), :]
        for r in range(MOST):
            stage[r, k] = bs[start + r]
        return carry

    lax.fori_loop(0, nf, pack, 0)

    def send_sums(s, carry):
        k = lax.rem(f + s, nf)
        remote(sts.at[k], rs.at[f], st_send, st_recv, h, k).start()
        return carry

    lax.fori_loop(1, nf, send_sums, 0)

    def send_slot(n, carry):
        r = n // (nf - 1)
        k = lax.rem(f + 1 + lax.rem(n, nf - 1), nf)
        remote(stage.at[r, k], rec.at[r, :, f], a2a_send, a2a_recv.at[r], h, k).start()
        return carry

    lax.fori_loop(0, MOST * (nf - 1), send_slot, 0)
    my_offset = offs[f]
    rs[f] = fsb[pl.ds(my_offset, 8), :]
    for r in range(MOST):
        rec[r, :, f] = bs[my_offset + r]

    size = ny * su
    half = size // 2

    def block(s):
        return lax.rem(x + nx + s, nx) * size

    def x_copy(i, start, count, sem, step):
        here = wb.at[i, pl.ds(start, count), :, lanes]
        remote(here, here, wx_send.at[i, sem], wx_recv.at[i, sem], *on_x(step)).start()

    def x_await(i, count, sem, which):
        await_bytes(wb.at[i, pl.ds(0, count), :, lanes], which.at[i, sem])

    def both_first():
        await_bytes(wb.at[0, pl.ds(0, (ny - 1) * su), :, lanes], wy_recv.at[0])
        x_copy(0, block(0), size, 0, 1)
        if nx > 2:
            x_copy(0, block(0), size, 1, -1)

    def both_second():
        x_await(0, size, 0, wx_recv)
        if nx > 2:
            x_copy(0, block(-1), half, 2, 1)
            x_await(0, size, 1, wx_recv)
            x_copy(0, block(1) + half, half, 3, -1)

    def both_last():
        if nx > 2:
            x_await(0, half, 2, wx_recv)
            x_await(0, half, 3, wx_recv)

    way = 1 - 2 * ((ny - y) // ny)

    def one_way(n):
        if n == 0:
            await_bytes(wb.at[1, pl.ds(0, (ny - 1) * su), :, lanes], wy_recv.at[1])
        else:
            x_await(1, size, n - 1, wx_recv)
        if n < nx - 1:
            x_copy(1, block(-n * way), size, n, way)

    partner = f + 1 - 2 * core
    other = pl.ds(pl.multiple_of(128 - core * 128, 128), 128)

    def to_partner(i):
        mine_half = wb.at[i, :, :, lanes]
        remote(mine_half, mine_half, wp_send.at[i], wp_recv.at[i], h, partner).start()

    def y_start(q, value):
        ysc[q, y] = value
        for s in range(1, ny):
            remote(
                ysc.at[q, y], ysc.at[q, y], y_send.at[q], y_recv.at[q],
                *on_y(s),
            ).start()

    def y_finish(q):
        await_bytes(ysc.at[q, 0 : ny - 1], y_recv.at[q])
        return jnp.sum(ysc[q], axis=0)

    def x_start(q, value):
        xsc[q, x] = value
        for s in range(1, nx):
            remote(
                xsc.at[q, x], xsc.at[q, x], x_send.at[q], x_recv.at[q],
                *on_x(s),
            ).start()

    def x_finish(q):
        await_bytes(xsc.at[q, 0 : nx - 1], x_recv.at[q])
        return jnp.sum(xsc[q], axis=0)

    def set_norm(q, totals, gain):
        sum_back = one_hot(SUM_LANES, C, lambda r, c: r == c // per)
        sq_back = one_hot(SUM_LANES, C, lambda r, c: r == c // per + GROUPS)
        mean = hdot(totals, sum_back) / cells
        var = hdot(totals, sq_back) / cells - mean * mean
        mu[q] = mean
        sc[q] = lax.rsqrt(jnp.maximum(var, 0.0) + 1e-06) * gain

    def ready_weight(i):
        await_bytes(wb.at[i, :, :, other], wp_recv.at[i])
        step = 18

        def widen(n, carry):
            rows = wb[i, pl.ds(n * step, step)].astype(F32).reshape(step * 8, C)
            wr[i, pl.ds(pl.multiple_of(n * step * 8, step * 8), step * 8), :] = rows.astype(BF16)
            return carry

        lax.fori_loop(0, nh * su // step, widen, 0)

    def slot_in(r):
        await_bytes(rec.at[r, :, 0 : nf - 1], a2a_recv.at[r])
        remote(rec.at[r], ha.at[r, 1], ha_send.at[r, 0], ha_recv.at[r, 0], hup, f).start()
        remote(rec.at[r], ha.at[r, 0], ha_send.at[r, 1], ha_recv.at[r, 1], hdn, f).start()

    both_first()
    await_bytes(rs.at[0 : nf - 1], st_recv)
    y_start(0, jnp.sum(rs[...], axis=0))
    slot_in(0)
    both_second()
    x_start(0, y_finish(0))
    one_way(0)
    slot_in(1)
    both_last()
    to_partner(0)
    set_norm(0, x_finish(0), g1[...])

    def convolve(r, fields, keeps, q, shift, weight):
        mean = mu[q, pl.ds(r, 1), :]
        scale = sc[q, pl.ds(r, 1), :]
        for ip, field in enumerate(fields):
            value = field[...].astype(F32).reshape(width, C)
            normed = silu((value - mean) * scale + shift)
            if keeps[ip] is not None:
                normed = normed * keeps[ip]
            g4[8 : 8 + width, :] = normed
            rows = slice(ip * width, (ip + 1) * width)
            so[rows, 0:C] = g4[7 : 7 + width, :].astype(BF16)
            so[rows, C : 2 * C] = normed.astype(BF16)
            so[rows, 2 * C : 3 * C] = g4[9 : 9 + width, :].astype(BF16)
        pairs = []
        for top in range(0, len(fields) - 2, 2):
            acc = jnp.zeros((2 * width, C), F32)
            for b in range(3):
                acc = acc + jnp.dot(
                    so[(top + b) * width : (top + b + 2) * width, :],
                    wr[weight, b * 3 * C : (b + 1) * 3 * C, :],
                    preferred_element_type=F32,
                )
            pairs.append(acc)
        return pairs

    stat[...] = jnp.zeros_like(stat)
    split = MOST - 2

    def sums_start(q):
        y_start(q, hdot(stat[0], sum_map) + hdot(stat[1], sq_map))

    def first_conv(r, carry):
        @pl.when(r + 2 < MOST)
        def _():
            slot_in(r + 2)

        @pl.when(r == 0)
        def _():
            ready_weight(0)

        await_bytes(ha.at[r, 0], ha_recv.at[r, 0])
        await_bytes(ha.at[r, 1], ha_recv.at[r, 1])
        fields = (
            ha.at[r, 0, 0], ha.at[r, 0, 1], rec.at[r, 0], rec.at[r, 1], ha.at[r, 1, 0], ha.at[r, 1, 1],
        )
        keeps = (keep_top, keep_top, None, None, keep_bottom, keep_bottom)
        for n, pair in enumerate(convolve(r, fields, keeps, 0, s1[...], 0)):
            pair = pair + b1[...]
            first[r, 2 * n] = pair[0:width].astype(BF16)
            first[r, 2 * n + 1] = pair[width : 2 * width].astype(BF16)
        rounded = first[r, 1].astype(F32), first[r, 2].astype(F32)
        sums = rounded[0] + rounded[1]
        squares = rounded[0] * rounded[0] + rounded[1] * rounded[1]
        stat[0, pl.ds(r, 1), :] = jnp.sum(sums, axis=0, keepdims=True)
        stat[1, pl.ds(r, 1), :] = jnp.sum(squares, axis=0, keepdims=True)

        @pl.when(r == split - 1)
        def _():
            sums_start(1)

        @pl.when(r == MOST - 1)
        def _():
            sums_start(2)

        for n in range(1, nx - 1):

            @pl.when(r == 2 * n - 1)
            def _():
                one_way(n)

        return carry

    lax.fori_loop(0, MOST, first_conv, 0)
    one_way(nx - 1)
    to_partner(1)
    x_start(1, y_finish(1))
    x_start(2, y_finish(2))
    ready_weight(1)
    set_norm(1, x_finish(1), g2[...])

    my_count = counts[f]

    def second_conv(q, r, carry):
        fields = tuple(first.at[r, n] for n in range(4))
        keeps = (keep_top, None, None, keep_bottom)
        result = convolve(r, fields, keeps, q, s2[...], 1)[0] + b2[...]
        live = r < my_count
        for i in range(2):
            kept = rec[r, i].astype(F32).reshape(width, C)
            value = kept + result[i * width : (i + 1) * width]
            outv[r, i] = jnp.where(live, value, 0.0).astype(BF16)
        pltpu.make_async_copy(outv.at[r], out.at[r], out_sem.at[r]).start()
        return carry

    lax.fori_loop(0, split, functools.partial(second_conv, 1), 0)
    set_norm(2, x_finish(2), g2[...])
    lax.fori_loop(split, MOST, functools.partial(second_conv, 2), 0)

    for i in range(2):
        await_bytes(wb.at[i, pl.ds(0, (ny - 1) * su), :, lanes], wy_send.at[i])
        await_bytes(wb.at[i, :, :, lanes], wp_send.at[i])
    x_await(0, size, 0, wx_send)
    if nx > 2:
        x_await(0, size, 1, wx_send)
        x_await(0, half, 2, wx_send)
        x_await(0, half, 3, wx_send)
    for n in range(nx - 1):
        x_await(1, size, n, wx_send)
    await_bytes(sts.at[0 : nf - 1], st_send)
    await_bytes(stage.at[:, 0 : nf - 1], a2a_send)
    for q in range(3):
        await_bytes(ysc.at[q, 0 : ny - 1], y_send.at[q])
        await_bytes(xsc.at[q, 0 : nx - 1], x_send.at[q])
    for r in range(MOST):
        for i in range(2):
            await_bytes(rec.at[r], ha_send.at[r, i])
        pltpu.make_async_copy(outv.at[r], out.at[r], out_sem.at[r]).wait()


def per_device(nf, nh, video, counts, tw, tb, g1, s1, w1, b1, g2, s2, w2, b2):
    frames = video.shape[0]
    ny = 8 if nh % 16 == 0 else 2
    nx = nh // ny
    su = w1.shape[0] // 8
    tp = frames + 1
    wide = tp * J
    fr = -(-(frames + 7) // 8) * 8
    width = nf * J
    cells = float(2 * nh * width * (C // GROUPS))
    row = lambda v: v.reshape(1, C)
    anyspace = pl.BlockSpec(memory_space=pl.ANY)
    dma = pltpu.SemaphoreType.DMA
    V = pltpu.VMEM
    scratch = [
        V((frames, 2, J, C), BF16),
        V((27 * C, C), BF16),
        V((2, tp, J, C), BF16),
        V((2, 2, fr, C), BF16),
        V((2, tp, J, C), BF16),
        V((2, 4, fr, C), BF16),
        V((wide + 16, C), F32),
        V((4 * wide, 3 * C), BF16),
        V((3, 2, wide + 16, C), F32),
        V((fr, 2, J, C), BF16),
        V((MOST, nf, 2, J, C), BF16),
        V((nf, 8, SUM_LANES), F32),
        V((nf, 8, SUM_LANES), F32),
        V((3, ny, 8, SUM_LANES), F32),
        V((3, nx, 8, SUM_LANES), F32),
        V((fr, SUM_LANES), F32),
        V((MOST, 2, nf, J, C), BF16),
        V((MOST, 2, 2, nf, J, C), BF16),
        V((MOST, 4, width, C), BF16),
        V((width + 16, C), F32),
        V((6 * width, 3 * C), BF16),
        V((2, nh * su, 8, C), BF16),
        V((2, 9 * C, C), BF16),
        V((2, 8, C), F32),
        V((3, 8, C), F32),
        V((3, 8, C), F32),
        V((MOST, 2, width, C), BF16),
        V((7, 1, C), F32),
        pltpu.SMEM((nf,), jnp.int32),
        dma((2,)), dma((8,)), dma((8,)), dma((2,)),
        dma((2,)), dma((2,)), dma((2, 4)), dma((2, 4)), dma((2,)), dma((2,)),
        dma, dma((MOST,)), dma, dma, dma((3,)), dma((3,)), dma((3,)), dma((3,)),
        dma((MOST, 2)), dma((MOST, 2)), dma((MOST,)), dma((7,)),
        pltpu.SemaphoreType.REGULAR((3, 3)),
    ]
    return pl.pallas_call(
        functools.partial(kernel, nf, nx, ny, frames, su, cells),
        out_shape=jax.ShapeDtypeStruct((MOST, 2, width, C), BF16),
        in_specs=[pl.BlockSpec(memory_space=pltpu.SMEM)] + [anyspace] * 11,
        out_specs=anyspace,
        scratch_shapes=scratch,
        compiler_params=pltpu.CompilerParams(
            collective_id=0, has_side_effects=True, vmem_limit_bytes=60 * 2**20
        ),
        name="block",
    )(
        counts, video, tw, w1.reshape(su, 8, C), w2.reshape(su, 8, C),
        row(tb), row(g1), row(s1), row(b1), row(g2), row(s2), row(b2),
    )


def solution(mesh):
    placed = (
        P(None, "height", "frame", None),
        P(), P(), P(), P(), P(),
        P("height", None),
        P(), P(), P(),
        P("height", None),
        P(),
    )
    return jax.shard_map(
        functools.partial(per_device, mesh.shape["frame"], mesh.shape["height"]),
        mesh=mesh,
        in_specs=placed,
        out_specs=P("frame", "height", None, None),
        check_vma=False,
    )
```

```python
import functools

import jax
import jax.numpy as jnp
from jax import lax
from jax.experimental import pallas as pl
from jax.experimental.pallas import tpu as pltpu
from jax.sharding import PartitionSpec as P

GROUPS = 32
C = 256
J = 8
MOST = 6
F32 = jnp.float32
BF16 = jnp.bfloat16
HIGH = lax.Precision.HIGHEST
MESH = pl.DeviceIdType.MESH
SUM_LANES = 128


def silu(v):
    half = 0.5 * v
    return half * jnp.tanh(half) + half


def hdot(a, b):
    return jnp.dot(a, b, precision=HIGH, preferred_element_type=F32)


def one_hot(rows, cols, fn):
    r = lax.broadcasted_iota(jnp.int32, (rows, cols), 0)
    c = lax.broadcasted_iota(jnp.int32, (rows, cols), 1)
    return jnp.where(fn(r, c), 1.0, 0.0).astype(F32)


def size_y(nh):
    return 8 if nh % 16 == 0 else 2


def kernel(
    nf, nx, ny, frames, su, cells,
    counts, video, tw, w1, w2, tb_in, g1_in, s1_in, b1_in, g2_in, s2_in, b2_in,
    out,
    vid, twv, rowb, colb, hr, hc, gt, se, tc, bs, stage, sts, rs, ysc, xsc, fsb,
    rec, ha, hb, first, g4, so, wb, wr, stat, mu, sc, outv, pv, offs,
    local_sem, p1_send, p1_recv, wl_sem, ring_send, ring_recv, wy_send, wy_recv, wx_send, wx_recv, wp_send, wp_recv,
    a2a_send, a2a_recv, st_send, st_recv, y_send, y_recv, x_send, x_recv,
    ha_send, ha_recv, hb_send, hb_recv, out_sem, pv_sem, known,
):
    nh = nx * ny
    tp = frames + 1
    wide = tp * J
    fr = bs.shape[0]
    width = nf * J
    f = lax.axis_index("frame")
    h = lax.axis_index("height")
    x = h // ny
    y = lax.rem(h, ny)
    core = lax.rem(f, 2)
    hup, hdn = lax.rem(h + nh - 1, nh), lax.rem(h + 1, nh)
    fl, fr_ = lax.rem(f + nf - 1, nf), lax.rem(f + 1, nf)

    def dev(hh, ff):
        return {"height": hh, "frame": ff}

    def remote(src, dst, send, recv, hh, ff):
        return pltpu.make_async_remote_copy(
            src_ref=src, dst_ref=dst, send_sem=send, recv_sem=recv,
            device_id=dev(hh, ff), device_id_type=MESH,
        )

    def await_bytes(ref, sem):
        pltpu.make_async_copy(ref, ref, sem).wait()

    barrier = pltpu.get_barrier_semaphore()

    def greet(sem, hh, ff):
        pl.semaphore_signal(sem, inc=1, device_id=dev(hh, ff), device_id_type=MESH)

    def on_z(s):
        return h, lax.rem(f + nf + s, nf)

    def on_y(s):
        return x * ny + lax.rem(y + ny + s, ny), f

    def on_x(s):
        return lax.rem(x + nx + s, nx) * ny + y, f

    near = [(hup, f), (hdn, f), (hup, fl), (hup, fr_), (hdn, fl), (hdn, fr_)]
    for step in (-1, 1):
        near += [on_z(step), on_y(step), on_x(step)]
    for hh, ff in near:
        greet(barrier, hh, ff)

    copy_video = pltpu.make_async_copy(video, vid, local_sem.at[0])
    copy_video.start()
    copy_tw = pltpu.make_async_copy(tw, twv, local_sem.at[1])
    copy_tw.start()
    lane0 = pl.multiple_of(core * 128, 128)
    lanes = pl.ds(lane0, 128)

    def shards_at(i, yy):
        return wb.at[i, :, pl.ds(yy * su, su), :, lanes]

    def own_shard(i):
        return wb.at[i, x, pl.ds(y * su, su), :, lanes]

    own_w = [
        pltpu.make_async_copy(w.at[:, :, lanes], own_shard(i), wl_sem.at[i])
        for i, w in enumerate((w1, w2))
    ]
    for copy in own_w:
        copy.start()

    vectors = [
        pltpu.make_async_copy(v, pv.at[n], pv_sem.at[n])
        for n, v in enumerate((tb_in, g1_in, s1_in, b1_in, g2_in, s2_in, b2_in))
    ]
    for copy in vectors:
        copy.start()
    tb, g1, s1, b1, g2, s2, b2 = (pv.at[n] for n in range(7))

    for i in range(2):
        hr[i, frames:tp] = jnp.zeros((1, J, C), BF16)
    pl.semaphore_wait(barrier, len(near))

    rows_out = [
        remote(video.at[:, 0], hr.at[1, 0:frames], p1_send.at[0], p1_recv.at[0], hup, f),
        remote(video.at[:, 1], hr.at[0, 0:frames], p1_send.at[1], p1_recv.at[1], hdn, f),
    ]
    for copy in rows_out:
        copy.start()

    rings = ((0, on_z, nf), (1, on_y, ny), (2, on_x, nx))

    def tell(reach):
        for n, on, size in rings:
            if reach < size // 2:
                for step in (-reach, reach):
                    greet(known.at[n, reach // 2], *on(step))

    def hear(reach):
        for n, on, size in rings:
            if reach < size // 2:
                pl.semaphore_wait(known.at[n, reach // 2], 2)

    tell(1)
    zero8 = jnp.zeros((8, C), F32)
    gt[0:8, :] = zero8
    gt[8 + wide : 16 + wide, :] = zero8
    pick_left = one_hot(fr, wide, lambda r, c: c == r * J).astype(BF16)
    pick_right = one_hot(fr, wide, lambda r, c: c == r * J + J - 1).astype(BF16)
    copy_video.wait()
    for i in range(2):
        act = silu(vid[:, i].astype(F32)).astype(BF16)
        rowb[i, 0:frames] = act
        rowb[i, frames:tp] = jnp.zeros((1, J, C), BF16)
        flat = rowb[i].astype(F32).reshape(wide, C).astype(BF16)
        colb[0, i] = jnp.dot(pick_left, flat, preferred_element_type=F32).astype(BF16)
        colb[1, i] = jnp.dot(pick_right, flat, preferred_element_type=F32).astype(BF16)

    borders = [
        (colb.at[0], hc.at[1, 1:3], h, fl),
        (colb.at[1], hc.at[0, 1:3], h, fr_),
        (colb.at[0, 0], hc.at[1, 3], hup, fl),
        (colb.at[1, 0], hc.at[0, 3], hup, fr_),
        (colb.at[0, 1], hc.at[1, 0], hdn, fl),
        (colb.at[1, 1], hc.at[0, 0], hdn, fr_),
    ]
    cols_out = [
        remote(src, dst, p1_send.at[2 + n], p1_recv.at[2 + n], hh, ff)
        for n, (src, dst, hh, ff) in enumerate(borders)
    ]
    for copy in cols_out:
        copy.start()
    hear(1)
    tell(2)

    own_w[0].wait()
    for s in range(1, nx):
        remote(own_shard(0), own_shard(0), wx_send.at[0, 0], wx_recv.at[0, 0], *on_x(s)).start()
    plus, minus = ny // 2, ny - 1 - ny // 2
    others_x = wb.at[0, 0 : nx - 1, pl.ds(0, su), :, lanes]

    def ring(k):
        if k == 0:
            await_bytes(others_x, wx_recv.at[0, 0])
        for d, count, step in ((0, plus, 1), (1, minus, -1)):
            if 0 <= k - 1 < count:
                await_bytes(shards_at(0, 0), ring_recv.at[d, k - 1])
            if k < count:
                here = shards_at(0, lax.rem(y + ny - step * k, ny))
                remote(here, here, ring_send.at[d, k], ring_recv.at[d, k], *on_y(step)).start()


    total = jnp.int32(0)
    for k in range(nf):
        offs[k] = total
        total = total + counts[k]
    g4[0:8, :] = zero8
    g4[8 + width : 16 + width, :] = zero8
    for a in range(3):
        for i in range(2):
            tc[a, i, 0:16, :] = jnp.zeros((16, C), F32)

    put_left = one_hot(wide, fr, lambda r, c: r == c * J).astype(BF16)
    put_right = one_hot(wide, fr, lambda r, c: r == c * J + J - 1).astype(BF16)
    col = lax.rem(lax.broadcasted_iota(jnp.int32, (wide, C), 0), J)
    keep_left = jnp.where(f > 0, 1.0, 0.0)
    keep_right = jnp.where(f < nf - 1, 1.0, 0.0)
    keep_top = jnp.where(h > 0, 1.0, 0.0)
    keep_bottom = jnp.where(h < nh - 1, 1.0, 0.0)

    def bordered(ip):
        keep = (keep_top, 1.0, 1.0, keep_bottom)[ip]
        if ip in (1, 2):
            middle = rowb[ip - 1].astype(F32).reshape(wide, C)
        else:
            raw = hr[ip // 3].astype(F32).reshape(wide, C)
            middle = silu(raw).astype(BF16).astype(F32) * keep
        gt[8 : 8 + wide, :] = middle
        lefts = jnp.dot(put_left, hc[0, ip], preferred_element_type=F32) * (keep * keep_left)
        rights = jnp.dot(put_right, hc[1, ip], preferred_element_type=F32) * (keep * keep_right)
        rows = slice(ip * wide, (ip + 1) * wide)
        se[rows, 0:C] = jnp.where(col == 0, lefts, gt[7 : 7 + wide, :]).astype(BF16)
        se[rows, C : 2 * C] = middle.astype(BF16)
        se[rows, 2 * C : 3 * C] = jnp.where(col == J - 1, rights, gt[9 : 9 + wide, :]).astype(BF16)

    def tap(a, i, b):
        start = pl.multiple_of(a * (9 * C) + b * (3 * C), 3 * C)
        return jnp.dot(
            se[(i + b) * wide : (i + b + 1) * wide, :],
            twv[pl.ds(start, 3 * C), :],
            preferred_element_type=F32,
        )

    def own_taps(a, carry):
        tc[a, 0, 16 : 16 + wide, :] = tap(a, 0, 1) + tap(a, 0, 2)
        tc[a, 1, 16 : 16 + wide, :] = tap(a, 1, 0) + tap(a, 1, 1)
        return carry

    def border_taps(a, carry):
        tc[a, 0, 16 : 16 + wide, :] += tap(a, 0, 0)
        tc[a, 1, 16 : 16 + wide, :] += tap(a, 1, 2)
        return carry

    for copy in cols_out[:2]:
        copy.wait()
    bordered(1)
    bordered(2)
    hear(2)
    tell(4)

    ring(0)
    copy_tw.wait()
    for copy in vectors:
        copy.wait()
    lax.fori_loop(0, 3, own_taps, 0)
    for copy in rows_out + cols_out[2:]:
        copy.wait()
    bordered(0)
    bordered(3)
    lax.fori_loop(0, 3, border_taps, 0)
    ring(1)

    own_w[1].wait()
    for s in range(1, ny):
        remote(own_shard(1), own_shard(1), wy_send, wy_recv, *on_y(s)).start()

    hear(4)

    n_all = frames * J
    sums = jnp.zeros((n_all, C), F32)
    squares = jnp.zeros((n_all, C), F32)
    for i in range(2):
        value = (
            vid[:, i].astype(F32).reshape(n_all, C)
            + (tc[0, i, 0:n_all, :] + tc[1, i, 8 : 8 + n_all, :] + tc[2, i, 16 : 16 + n_all, :])
            + tb[...]
        )
        bs[0:frames, i] = value.reshape(frames, J, C).astype(BF16)
        rounded = bs[0:frames, i].astype(F32).reshape(n_all, C)
        sums = sums + rounded
        squares = squares + rounded * rounded
        bs[frames:fr, i] = jnp.zeros((fr - frames, J, C), BF16)

    per = C // GROUPS
    sum_map = one_hot(C, SUM_LANES, lambda r, c: c == r // per)
    sq_map = one_hot(C, SUM_LANES, lambda r, c: c == r // per + GROUPS)
    fsum = jnp.sum(sums.reshape(frames, J, C), axis=1)
    fsq = jnp.sum(squares.reshape(frames, J, C), axis=1)
    fsb[0:frames, :] = hdot(fsum, sum_map) + hdot(fsq, sq_map)
    fsb[frames:fr, :] = jnp.zeros((fr - frames, SUM_LANES), F32)

    def pack(k, carry):
        start = offs[k]
        sts[k] = fsb[pl.ds(start, 8), :]
        for r in range(MOST):
            stage[r, k] = bs[start + r]
        return carry

    lax.fori_loop(0, nf, pack, 0)

    def send_sums(s, carry):
        k = lax.rem(f + s, nf)
        remote(sts.at[k], rs.at[f], st_send, st_recv, h, k).start()
        return carry

    lax.fori_loop(1, nf, send_sums, 0)

    def send_slot(n, carry):
        r = n // (nf - 1)
        k = lax.rem(f + 1 + lax.rem(n, nf - 1), nf)
        remote(stage.at[r, k], rec.at[r, :, f], a2a_send, a2a_recv.at[r], h, k).start()
        return carry

    lax.fori_loop(0, MOST * (nf - 1), send_slot, 0)
    my_offset = offs[f]
    rs[f] = fsb[pl.ds(my_offset, 8), :]
    for r in range(MOST):
        rec[r, :, f] = bs[my_offset + r]

    way = 1 - 2 * ((ny - y) // ny)

    def one_way(n):
        if n == 0:
            await_bytes(wb.at[1, 0, pl.ds(0, (ny - 1) * su), :, lanes], wy_recv)
        else:
            await_bytes(wb.at[1, 0, :, :, lanes], wx_recv.at[1, n - 1])
        if n < nx - 1:
            here = wb.at[1, lax.rem(x + nx - n * way + nx, nx), :, :, lanes]
            remote(here, here, wx_send.at[1, n], wx_recv.at[1, n], *on_x(way)).start()

    partner = f + 1 - 2 * core
    other = pl.ds(pl.multiple_of(128 - core * 128, 128), 128)

    def to_partner(i):
        mine_half = wb.at[i, :, :, :, lanes]
        remote(mine_half, mine_half, wp_send.at[i], wp_recv.at[i], h, partner).start()

    def y_start(q, value):
        ysc[q, y] = value
        for s in range(1, ny):
            remote(
                ysc.at[q, y], ysc.at[q, y], y_send.at[q], y_recv.at[q],
                *on_y(s),
            ).start()

    def y_finish(q):
        await_bytes(ysc.at[q, 0 : ny - 1], y_recv.at[q])
        return jnp.sum(ysc[q], axis=0)

    def x_start(q, value):
        xsc[q, x] = value
        for s in range(1, nx):
            remote(
                xsc.at[q, x], xsc.at[q, x], x_send.at[q], x_recv.at[q],
                *on_x(s),
            ).start()

    def x_finish(q):
        await_bytes(xsc.at[q, 0 : nx - 1], x_recv.at[q])
        return jnp.sum(xsc[q], axis=0)

    def set_norm(q, totals, gain):
        sum_back = one_hot(SUM_LANES, C, lambda r, c: r == c // per)
        sq_back = one_hot(SUM_LANES, C, lambda r, c: r == c // per + GROUPS)
        mean = hdot(totals, sum_back) / cells
        var = hdot(totals, sq_back) / cells - mean * mean
        mu[q] = mean
        sc[q] = lax.rsqrt(jnp.maximum(var, 0.0) + 1e-06) * gain

    def ready_weight(i):
        await_bytes(wb.at[i, :, :, :, other], wp_recv.at[i])
        step = 18
        steps = ny * su // step

        def widen(n, carry):
            rows = wb[i, n // steps, pl.ds(lax.rem(n, steps) * step, step)]
            rows = rows.astype(F32).reshape(step * 8, C)
            wr[i, pl.ds(pl.multiple_of(n * step * 8, step * 8), step * 8), :] = rows.astype(BF16)
            return carry

        lax.fori_loop(0, nh * su // step, widen, 0)

    def slot_in(r):
        await_bytes(rec.at[r, :, 0 : nf - 1], a2a_recv.at[r])
        remote(rec.at[r, 0], ha.at[r, 1], ha_send.at[r, 0], ha_recv.at[r, 0], hup, f).start()
        remote(rec.at[r, 1], ha.at[r, 0], ha_send.at[r, 1], ha_recv.at[r, 1], hdn, f).start()

    ring(2)
    await_bytes(rs.at[0 : nf - 1], st_recv)
    y_start(0, jnp.sum(rs[...], axis=0))
    ring(3)
    slot_in(0)
    ring(4)
    to_partner(0)
    x_start(0, y_finish(0))
    one_way(0)
    slot_in(1)
    set_norm(0, x_finish(0), g1[...])

    keeps = (keep_top, None, None, keep_bottom)

    def convolve(r, rows_of, q, shift, weight):
        mean = mu[q, pl.ds(r, 1), :]
        scale = sc[q, pl.ds(r, 1), :]
        for ip in range(4):
            normed = silu((rows_of(ip) - mean) * scale + shift)
            if keeps[ip] is not None:
                normed = normed * keeps[ip]
            g4[8 : 8 + width, :] = normed
            rows = slice(ip * width, (ip + 1) * width)
            so[rows, 0:C] = g4[7 : 7 + width, :].astype(BF16)
            so[rows, C : 2 * C] = normed.astype(BF16)
            so[rows, 2 * C : 3 * C] = g4[9 : 9 + width, :].astype(BF16)
        acc = jnp.zeros((2 * width, C), F32)
        for b in range(3):
            acc = acc + jnp.dot(
                so[b * width : (b + 2) * width, :],
                wr[weight, b * 3 * C : (b + 1) * 3 * C, :],
                preferred_element_type=F32,
            )
        return acc

    def first_rows(r):
        def get(ip):
            ref = (ha.at[r, 0], rec.at[r, 0], rec.at[r, 1], ha.at[r, 1])[ip]
            return ref[...].astype(F32).reshape(width, C)

        return get

    def second_rows(r):
        def get(ip):
            ref = (hb.at[r, 0], first.at[r, 0], first.at[r, 1], hb.at[r, 1])[ip]
            return ref[...].astype(F32)

        return get

    stat[...] = jnp.zeros_like(stat)
    split = MOST - 2

    def sums_start(q):
        y_start(q, hdot(stat[0], sum_map) + hdot(stat[1], sq_map))

    def first_conv(r, carry):
        @pl.when(r + 2 < MOST)
        def _():
            slot_in(r + 2)

        @pl.when(r == 0)
        def _():
            ready_weight(0)

        await_bytes(ha.at[r, 0], ha_recv.at[r, 0])
        await_bytes(ha.at[r, 1], ha_recv.at[r, 1])
        result = convolve(r, first_rows(r), 0, s1[...], 0) + b1[...]
        first[r, 0] = result[0:width].astype(BF16)
        first[r, 1] = result[width : 2 * width].astype(BF16)
        rounded = first[r, 0].astype(F32), first[r, 1].astype(F32)
        sums = rounded[0] + rounded[1]
        squares = rounded[0] * rounded[0] + rounded[1] * rounded[1]
        stat[0, pl.ds(r, 1), :] = jnp.sum(sums, axis=0, keepdims=True)
        stat[1, pl.ds(r, 1), :] = jnp.sum(squares, axis=0, keepdims=True)

        @pl.when(r == split - 1)
        def _():
            sums_start(1)

        @pl.when(r == MOST - 1)
        def _():
            sums_start(2)

        remote(first.at[r, 0], hb.at[r, 1], hb_send.at[r, 0], hb_recv.at[r, 0], hup, f).start()
        remote(first.at[r, 1], hb.at[r, 0], hb_send.at[r, 1], hb_recv.at[r, 1], hdn, f).start()

        for n in range(1, nx - 1):

            @pl.when(r == 2 * n - 1)
            def _():
                one_way(n)

        return carry

    lax.fori_loop(0, MOST, first_conv, 0)
    one_way(nx - 1)
    to_partner(1)
    x_start(1, y_finish(1))
    x_start(2, y_finish(2))
    ready_weight(1)
    set_norm(1, x_finish(1), g2[...])

    my_count = counts[f]

    def second_conv(q, r, carry):
        await_bytes(hb.at[r, 0], hb_recv.at[r, 0])
        await_bytes(hb.at[r, 1], hb_recv.at[r, 1])
        result = convolve(r, second_rows(r), q, s2[...], 1) + b2[...]
        live = r < my_count
        for i in range(2):
            kept = rec[r, i].astype(F32).reshape(width, C)
            value = kept + result[i * width : (i + 1) * width]
            outv[r, i] = jnp.where(live, value, 0.0).astype(BF16)
        pltpu.make_async_copy(outv.at[r], out.at[r], out_sem.at[r]).start()
        return carry

    lax.fori_loop(0, split, functools.partial(second_conv, 1), 0)
    set_norm(2, x_finish(2), g2[...])
    lax.fori_loop(split, MOST, functools.partial(second_conv, 2), 0)

    await_bytes(others_x, wx_send.at[0, 0])
    for d, count in ((0, plus), (1, minus)):
        for k in range(count):
            await_bytes(shards_at(0, 0), ring_send.at[d, k])
    await_bytes(wb.at[1, 0, pl.ds(0, (ny - 1) * su), :, lanes], wy_send)
    for n in range(nx - 1):
        await_bytes(wb.at[1, 0, :, :, lanes], wx_send.at[1, n])
    for i in range(2):
        await_bytes(wb.at[i, :, :, :, lanes], wp_send.at[i])
    await_bytes(sts.at[0 : nf - 1], st_send)
    await_bytes(stage.at[:, 0 : nf - 1], a2a_send)
    for q in range(3):
        await_bytes(ysc.at[q, 0 : ny - 1], y_send.at[q])
        await_bytes(xsc.at[q, 0 : nx - 1], x_send.at[q])
    for r in range(MOST):
        for i in range(2):
            await_bytes(rec.at[r, i], ha_send.at[r, i])
            await_bytes(first.at[r, i], hb_send.at[r, i])
        pltpu.make_async_copy(outv.at[r], out.at[r], out_sem.at[r]).wait()


def per_device(nf, nh, video, counts, tw, tb, g1, s1, w1, b1, g2, s2, w2, b2):
    frames = video.shape[0]
    ny = size_y(nh)
    nx = nh // ny
    su = w1.shape[0] // 8
    tp = frames + 1
    wide = tp * J
    fr = -(-(frames + 7) // 8) * 8
    width = nf * J
    cells = float(2 * nh * width * (C // GROUPS))
    row = lambda v: v.reshape(1, C)
    anyspace = pl.BlockSpec(memory_space=pl.ANY)
    dma = pltpu.SemaphoreType.DMA
    V = pltpu.VMEM
    scratch = [
        V((frames, 2, J, C), BF16),
        V((27 * C, C), BF16),
        V((2, tp, J, C), BF16),
        V((2, 2, fr, C), BF16),
        V((2, tp, J, C), BF16),
        V((2, 4, fr, C), BF16),
        V((wide + 16, C), F32),
        V((4 * wide, 3 * C), BF16),
        V((3, 2, wide + 16, C), F32),
        V((fr, 2, J, C), BF16),
        V((MOST, nf, 2, J, C), BF16),
        V((nf, 8, SUM_LANES), F32),
        V((nf, 8, SUM_LANES), F32),
        V((3, ny, 8, SUM_LANES), F32),
        V((3, nx, 8, SUM_LANES), F32),
        V((fr, SUM_LANES), F32),
        V((MOST, 2, nf, J, C), BF16),
        V((MOST, 2, nf, J, C), BF16),
        V((MOST, 2, width, C), BF16),
        V((MOST, 2, width, C), BF16),
        V((width + 16, C), F32),
        V((4 * width, 3 * C), BF16),
        V((2, nx, ny * su, 8, C), BF16),
        V((2, 9 * C, C), BF16),
        V((2, 8, C), F32),
        V((3, 8, C), F32),
        V((3, 8, C), F32),
        V((MOST, 2, width, C), BF16),
        V((7, 1, C), F32),
        pltpu.SMEM((nf,), jnp.int32),
        dma((2,)), dma((8,)), dma((8,)), dma((2,)),
        dma((2, 4)), dma((2, 4)), dma, dma, dma((2, 4)), dma((2, 4)), dma((2,)), dma((2,)),
        dma, dma((MOST,)), dma, dma, dma((3,)), dma((3,)), dma((3,)), dma((3,)),
        dma((MOST, 2)), dma((MOST, 2)), dma((MOST, 2)), dma((MOST, 2)), dma((MOST,)), dma((7,)),
        pltpu.SemaphoreType.REGULAR((3, 3)),
    ]
    return pl.pallas_call(
        functools.partial(kernel, nf, nx, ny, frames, su, cells),
        out_shape=jax.ShapeDtypeStruct((MOST, 2, width, C), BF16),
        in_specs=[pl.BlockSpec(memory_space=pltpu.SMEM)] + [anyspace] * 11,
        out_specs=anyspace,
        scratch_shapes=scratch,
        compiler_params=pltpu.CompilerParams(
            collective_id=0, has_side_effects=True, vmem_limit_bytes=60 * 2**20
        ),
        name="block",
    )(
        counts, video, tw, w1.reshape(su, 8, C), w2.reshape(su, 8, C),
        row(tb), row(g1), row(s1), row(b1), row(g2), row(s2), row(b2),
    )


def solution(mesh):
    placed = (
        P(None, "height", "frame", None),
        P(), P(), P(), P(), P(),
        P("height", None),
        P(), P(), P(),
        P("height", None),
        P(),
    )
    return jax.shard_map(
        functools.partial(per_device, mesh.shape["frame"], mesh.shape["height"]),
        mesh=mesh,
        in_specs=placed,
        out_specs=P("frame", "height", None, None),
        check_vma=False,
    )
```

```python
import functools

import jax
import jax.numpy as jnp
from jax import lax
from jax.experimental import pallas as pl
from jax.experimental.pallas import tpu as pltpu
from jax.sharding import PartitionSpec as P

GROUPS = 32
C = 256
J = 8
MOST = 6
F32 = jnp.float32
BF16 = jnp.bfloat16
HIGH = lax.Precision.HIGHEST
MESH = pl.DeviceIdType.MESH
SUM_LANES = 128


def silu(v):
    half = 0.5 * v
    return half * jnp.tanh(half) + half


def hdot(a, b):
    return jnp.dot(a, b, precision=HIGH, preferred_element_type=F32)


def one_hot(rows, cols, fn):
    r = lax.broadcasted_iota(jnp.int32, (rows, cols), 0)
    c = lax.broadcasted_iota(jnp.int32, (rows, cols), 1)
    return jnp.where(fn(r, c), 1.0, 0.0).astype(F32)


def kernel(
    nf, nx, ny, frames, su, cells,
    counts, video, tw, w1, w2, tb_in, g1_in, s1_in, b1_in, g2_in, s2_in, b2_in,
    out,
    vid, twv, rowb, colb, hr, hc, gt, se, tc, bs, stage, sts, rs, ysc, xsc, fsb,
    rec, ha, hb, first, g4, so, wb, wr, stat, mu, sc, outv, pv, offs,
    local_sem, p1_send, p1_recv, wl_sem, wy_send, wy_recv, wx_send, wx_recv, wp_send, wp_recv,
    a2a_send, a2a_recv, st_send, st_recv, y_send, y_recv, x_send, x_recv,
    ha_send, ha_recv, hb_send, hb_recv, out_sem, pv_sem, known,
):
    nh = nx * ny
    tp = frames + 1
    wide = tp * J
    fr = bs.shape[0]
    width = nf * J
    f = lax.axis_index("frame")
    h = lax.axis_index("height")
    x = h // ny
    y = lax.rem(h, ny)
    core = lax.rem(f, 2)
    hup, hdn = lax.rem(h + nh - 1, nh), lax.rem(h + 1, nh)
    fl, fr_ = lax.rem(f + nf - 1, nf), lax.rem(f + 1, nf)

    def dev(hh, ff):
        return {"height": hh, "frame": ff}

    def remote(src, dst, send, recv, hh, ff):
        return pltpu.make_async_remote_copy(
            src_ref=src, dst_ref=dst, send_sem=send, recv_sem=recv,
            device_id=dev(hh, ff), device_id_type=MESH,
        )

    def await_bytes(ref, sem):
        pltpu.make_async_copy(ref, ref, sem).wait()

    barrier = pltpu.get_barrier_semaphore()

    def greet(sem, hh, ff):
        pl.semaphore_signal(sem, inc=1, device_id=dev(hh, ff), device_id_type=MESH)

    def on_z(s):
        return h, lax.rem(f + nf + s, nf)

    def on_y(s):
        return x * ny + lax.rem(y + ny + s, ny), f

    def on_x(s):
        return lax.rem(x + nx + s, nx) * ny + y, f

    near = [(hup, f), (hdn, f), (hup, fl), (hup, fr_), (hdn, fl), (hdn, fr_)]
    for step in (-1, 1):
        near += [on_z(step), on_y(step), on_x(step)]
    for hh, ff in near:
        greet(barrier, hh, ff)

    copy_video = pltpu.make_async_copy(video, vid, local_sem.at[0])
    copy_video.start()
    copy_tw = pltpu.make_async_copy(tw, twv, local_sem.at[1])
    copy_tw.start()
    lane0 = pl.multiple_of(core * 128, 128)
    lanes = pl.ds(lane0, 128)
    mine = pl.ds(h * su, su)
    own_w = [
        pltpu.make_async_copy(w.at[:, :, lanes], wb.at[i, mine, :, lanes], wl_sem.at[i])
        for i, w in enumerate((w1, w2))
    ]
    for copy in own_w:
        copy.start()

    vectors = [
        pltpu.make_async_copy(v, pv.at[n], pv_sem.at[n])
        for n, v in enumerate((tb_in, g1_in, s1_in, b1_in, g2_in, s2_in, b2_in))
    ]
    for copy in vectors:
        copy.start()
    tb, g1, s1, b1, g2, s2, b2 = (pv.at[n] for n in range(7))

    for i in range(2):
        hr[i, frames:tp] = jnp.zeros((1, J, C), BF16)
    pl.semaphore_wait(barrier, len(near))

    rows_out = [
        remote(video.at[:, 0], hr.at[1, 0:frames], p1_send.at[0], p1_recv.at[0], hup, f),
        remote(video.at[:, 1], hr.at[0, 0:frames], p1_send.at[1], p1_recv.at[1], hdn, f),
    ]
    for copy in rows_out:
        copy.start()

    rings = ((0, on_z, nf), (1, on_y, ny), (2, on_x, nx))

    def tell(reach):
        for n, on, size in rings:
            if reach < size // 2:
                for step in (-reach, reach):
                    greet(known.at[n, reach // 2], *on(step))

    def hear(reach):
        for n, on, size in rings:
            if reach < size // 2:
                pl.semaphore_wait(known.at[n, reach // 2], 2)

    tell(1)
    zero8 = jnp.zeros((8, C), F32)
    gt[0:8, :] = zero8
    gt[8 + wide : 16 + wide, :] = zero8
    pick_left = one_hot(fr, wide, lambda r, c: c == r * J).astype(BF16)
    pick_right = one_hot(fr, wide, lambda r, c: c == r * J + J - 1).astype(BF16)
    copy_video.wait()
    for i in range(2):
        act = silu(vid[:, i].astype(F32)).astype(BF16)
        rowb[i, 0:frames] = act
        rowb[i, frames:tp] = jnp.zeros((1, J, C), BF16)
        flat = rowb[i].astype(F32).reshape(wide, C).astype(BF16)
        colb[0, i] = jnp.dot(pick_left, flat, preferred_element_type=F32).astype(BF16)
        colb[1, i] = jnp.dot(pick_right, flat, preferred_element_type=F32).astype(BF16)

    borders = [
        (colb.at[0], hc.at[1, 1:3], h, fl),
        (colb.at[1], hc.at[0, 1:3], h, fr_),
        (colb.at[0, 0], hc.at[1, 3], hup, fl),
        (colb.at[1, 0], hc.at[0, 3], hup, fr_),
        (colb.at[0, 1], hc.at[1, 0], hdn, fl),
        (colb.at[1, 1], hc.at[0, 0], hdn, fr_),
    ]
    cols_out = [
        remote(src, dst, p1_send.at[2 + n], p1_recv.at[2 + n], hh, ff)
        for n, (src, dst, hh, ff) in enumerate(borders)
    ]
    for copy in cols_out:
        copy.start()
    hear(1)
    tell(2)

    total = jnp.int32(0)
    for k in range(nf):
        offs[k] = total
        total = total + counts[k]
    g4[0:8, :] = zero8
    g4[8 + width : 16 + width, :] = zero8
    for a in range(3):
        for i in range(2):
            tc[a, i, 0:16, :] = jnp.zeros((16, C), F32)

    put_left = one_hot(wide, fr, lambda r, c: r == c * J).astype(BF16)
    put_right = one_hot(wide, fr, lambda r, c: r == c * J + J - 1).astype(BF16)
    col = lax.rem(lax.broadcasted_iota(jnp.int32, (wide, C), 0), J)
    keep_left = jnp.where(f > 0, 1.0, 0.0)
    keep_right = jnp.where(f < nf - 1, 1.0, 0.0)
    keep_top = jnp.where(h > 0, 1.0, 0.0)
    keep_bottom = jnp.where(h < nh - 1, 1.0, 0.0)

    def bordered(ip):
        keep = (keep_top, 1.0, 1.0, keep_bottom)[ip]
        if ip in (1, 2):
            middle = rowb[ip - 1].astype(F32).reshape(wide, C)
        else:
            raw = hr[ip // 3].astype(F32).reshape(wide, C)
            middle = silu(raw).astype(BF16).astype(F32) * keep
        gt[8 : 8 + wide, :] = middle
        lefts = jnp.dot(put_left, hc[0, ip], preferred_element_type=F32) * (keep * keep_left)
        rights = jnp.dot(put_right, hc[1, ip], preferred_element_type=F32) * (keep * keep_right)
        rows = slice(ip * wide, (ip + 1) * wide)
        se[rows, 0:C] = jnp.where(col == 0, lefts, gt[7 : 7 + wide, :]).astype(BF16)
        se[rows, C : 2 * C] = middle.astype(BF16)
        se[rows, 2 * C : 3 * C] = jnp.where(col == J - 1, rights, gt[9 : 9 + wide, :]).astype(BF16)

    def tap(a, i, b):
        start = pl.multiple_of(a * (9 * C) + b * (3 * C), 3 * C)
        return jnp.dot(
            se[(i + b) * wide : (i + b + 1) * wide, :],
            twv[pl.ds(start, 3 * C), :],
            preferred_element_type=F32,
        )

    def own_taps(a, carry):
        tc[a, 0, 16 : 16 + wide, :] = tap(a, 0, 1) + tap(a, 0, 2)
        tc[a, 1, 16 : 16 + wide, :] = tap(a, 1, 0) + tap(a, 1, 1)
        return carry

    def border_taps(a, carry):
        tc[a, 0, 16 : 16 + wide, :] += tap(a, 0, 0)
        tc[a, 1, 16 : 16 + wide, :] += tap(a, 1, 2)
        return carry

    for copy in cols_out[:2]:
        copy.wait()
    bordered(1)
    bordered(2)
    hear(2)
    tell(4)

    for copy in own_w:
        copy.wait()
    for i in range(2):
        for s in range(1, ny):
            here = wb.at[i, mine, :, lanes]
            remote(here, here, wy_send.at[i], wy_recv.at[i], *on_y(s)).start()

    copy_tw.wait()
    for copy in vectors:
        copy.wait()
    lax.fori_loop(0, 3, own_taps, 0)
    for copy in rows_out + cols_out[2:]:
        copy.wait()
    bordered(0)
    bordered(3)
    lax.fori_loop(0, 3, border_taps, 0)
    hear(4)

    n_all = frames * J
    sums = jnp.zeros((n_all, C), F32)
    squares = jnp.zeros((n_all, C), F32)
    for i in range(2):
        value = (
            vid[:, i].astype(F32).reshape(n_all, C)
            + (tc[0, i, 0:n_all, :] + tc[1, i, 8 : 8 + n_all, :] + tc[2, i, 16 : 16 + n_all, :])
            + tb[...]
        )
        bs[0:frames, i] = value.reshape(frames, J, C).astype(BF16)
        rounded = bs[0:frames, i].astype(F32).reshape(n_all, C)
        sums = sums + rounded
        squares = squares + rounded * rounded
        bs[frames:fr, i] = jnp.zeros((fr - frames, J, C), BF16)

    per = C // GROUPS
    sum_map = one_hot(C, SUM_LANES, lambda r, c: c == r // per)
    sq_map = one_hot(C, SUM_LANES, lambda r, c: c == r // per + GROUPS)
    fsum = jnp.sum(sums.reshape(frames, J, C), axis=1)
    fsq = jnp.sum(squares.reshape(frames, J, C), axis=1)
    fsb[0:frames, :] = hdot(fsum, sum_map) + hdot(fsq, sq_map)
    fsb[frames:fr, :] = jnp.zeros((fr - frames, SUM_LANES), F32)

    def pack(k, carry):
        start = offs[k]
        sts[k] = fsb[pl.ds(start, 8), :]
        for r in range(MOST):
            stage[r, k] = bs[start + r]
        return carry

    lax.fori_loop(0, nf, pack, 0)

    def send_sums(s, carry):
        k = lax.rem(f + s, nf)
        remote(sts.at[k], rs.at[f], st_send, st_recv, h, k).start()
        return carry

    lax.fori_loop(1, nf, send_sums, 0)

    def send_slot(n, carry):
        r = n // (nf - 1)
        k = lax.rem(f + 1 + lax.rem(n, nf - 1), nf)
        remote(stage.at[r, k], rec.at[r, :, f], a2a_send, a2a_recv.at[r], h, k).start()
        return carry

    lax.fori_loop(0, MOST * (nf - 1), send_slot, 0)
    my_offset = offs[f]
    rs[f] = fsb[pl.ds(my_offset, 8), :]
    for r in range(MOST):
        rec[r, :, f] = bs[my_offset + r]

    size = ny * su
    half = size // 2

    def block(s):
        return lax.rem(x + nx + s, nx) * size

    def x_copy(i, start, count, sem, step):
        here = wb.at[i, pl.ds(start, count), :, lanes]
        remote(here, here, wx_send.at[i, sem], wx_recv.at[i, sem], *on_x(step)).start()

    def x_await(i, count, sem, which):
        await_bytes(wb.at[i, pl.ds(0, count), :, lanes], which.at[i, sem])

    partner = f + 1 - 2 * core
    other = pl.ds(pl.multiple_of(128 - core * 128, 128), 128)

    def to_partner(i, start, count):
        here = wb.at[i, pl.ds(start, count), :, lanes]
        remote(here, here, wp_send.at[i], wp_recv.at[i], h, partner).start()

    def both_first():
        await_bytes(wb.at[0, pl.ds(0, (ny - 1) * su), :, lanes], wy_recv.at[0])
        x_copy(0, block(0), size, 0, 1)
        if nx > 2:
            x_copy(0, block(0), size, 1, -1)
        to_partner(0, block(0), size)

    def both_second():
        x_await(0, size, 0, wx_recv)
        if nx > 2:
            x_copy(0, block(-1), half, 2, 1)
            x_await(0, size, 1, wx_recv)
            x_copy(0, block(1) + half, half, 3, -1)
            to_partner(0, block(-1), size)
        to_partner(0, block(1), size)

    def both_last():
        if nx > 2:
            x_await(0, half, 2, wx_recv)
            x_await(0, half, 3, wx_recv)
            to_partner(0, block(2), size)

    way = 1 - 2 * ((ny - y) // ny)

    def one_way(n):
        if n == 0:
            await_bytes(wb.at[1, pl.ds(0, (ny - 1) * su), :, lanes], wy_recv.at[1])
        else:
            x_await(1, size, n - 1, wx_recv)
        if n < nx - 1:
            x_copy(1, block(-n * way), size, n, way)

    def y_start(q, value):
        ysc[q, y] = value
        for s in range(1, ny):
            remote(
                ysc.at[q, y], ysc.at[q, y], y_send.at[q], y_recv.at[q],
                *on_y(s),
            ).start()

    def y_finish(q):
        await_bytes(ysc.at[q, 0 : ny - 1], y_recv.at[q])
        return jnp.sum(ysc[q], axis=0)

    def x_start(q, value):
        xsc[q, x] = value
        for s in range(1, nx):
            remote(
                xsc.at[q, x], xsc.at[q, x], x_send.at[q], x_recv.at[q],
                *on_x(s),
            ).start()

    def x_finish(q):
        await_bytes(xsc.at[q, 0 : nx - 1], x_recv.at[q])
        return jnp.sum(xsc[q], axis=0)

    def set_norm(q, totals, gain):
        sum_back = one_hot(SUM_LANES, C, lambda r, c: r == c // per)
        sq_back = one_hot(SUM_LANES, C, lambda r, c: r == c // per + GROUPS)
        mean = hdot(totals, sum_back) / cells
        var = hdot(totals, sq_back) / cells - mean * mean
        mu[q] = mean
        sc[q] = lax.rsqrt(jnp.maximum(var, 0.0) + 1e-06) * gain

    def ready_weight(i):
        await_bytes(wb.at[i, :, :, other], wp_recv.at[i])
        step = 18

        def widen(n, carry):
            rows = wb[i, pl.ds(n * step, step)].astype(F32).reshape(step * 8, C)
            wr[i, pl.ds(pl.multiple_of(n * step * 8, step * 8), step * 8), :] = rows.astype(BF16)
            return carry

        lax.fori_loop(0, nh * su // step, widen, 0)

    def slot_in(r):
        await_bytes(rec.at[r, :, 0 : nf - 1], a2a_recv.at[r])
        remote(rec.at[r, 0], ha.at[r, 1], ha_send.at[r, 0], ha_recv.at[r, 0], hup, f).start()
        remote(rec.at[r, 1], ha.at[r, 0], ha_send.at[r, 1], ha_recv.at[r, 1], hdn, f).start()

    both_first()
    await_bytes(rs.at[0 : nf - 1], st_recv)
    y_start(0, jnp.sum(rs[...], axis=0))
    both_second()
    slot_in(0)
    x_start(0, y_finish(0))
    one_way(0)
    slot_in(1)
    both_last()
    set_norm(0, x_finish(0), g1[...])

    keeps = (keep_top, None, None, keep_bottom)

    def convolve(r, rows_of, q, shift, weight):
        mean = mu[q, pl.ds(r, 1), :]
        scale = sc[q, pl.ds(r, 1), :]
        for ip in range(4):
            normed = silu((rows_of(ip) - mean) * scale + shift)
            if keeps[ip] is not None:
                normed = normed * keeps[ip]
            g4[8 : 8 + width, :] = normed
            rows = slice(ip * width, (ip + 1) * width)
            so[rows, 0:C] = g4[7 : 7 + width, :].astype(BF16)
            so[rows, C : 2 * C] = normed.astype(BF16)
            so[rows, 2 * C : 3 * C] = g4[9 : 9 + width, :].astype(BF16)
        acc = jnp.zeros((2 * width, C), F32)
        for b in range(3):
            acc = acc + jnp.dot(
                so[b * width : (b + 2) * width, :],
                wr[weight, b * 3 * C : (b + 1) * 3 * C, :],
                preferred_element_type=F32,
            )
        return acc

    def first_rows(r):
        def get(ip):
            ref = (ha.at[r, 0], rec.at[r, 0], rec.at[r, 1], ha.at[r, 1])[ip]
            return ref[...].astype(F32).reshape(width, C)

        return get

    def second_rows(r):
        def get(ip):
            ref = (hb.at[r, 0], first.at[r, 0], first.at[r, 1], hb.at[r, 1])[ip]
            return ref[...].astype(F32)

        return get

    stat[...] = jnp.zeros_like(stat)
    split = MOST - 2

    def send_first(r):
        remote(first.at[r, 0], hb.at[r, 1], hb_send.at[r, 0], hb_recv.at[r, 0], hup, f).start()
        remote(first.at[r, 1], hb.at[r, 0], hb_send.at[r, 1], hb_recv.at[r, 1], hdn, f).start()

    def sums_start(q):
        y_start(q, hdot(stat[0], sum_map) + hdot(stat[1], sq_map))

    def first_conv(r, carry):
        @pl.when(r + 2 < MOST)
        def _():
            slot_in(r + 2)

        @pl.when(r == 0)
        def _():
            ready_weight(0)

        await_bytes(ha.at[r, 0], ha_recv.at[r, 0])
        await_bytes(ha.at[r, 1], ha_recv.at[r, 1])
        result = convolve(r, first_rows(r), 0, s1[...], 0) + b1[...]
        first[r, 0] = result[0:width].astype(BF16)
        first[r, 1] = result[width : 2 * width].astype(BF16)
        rounded = first[r, 0].astype(F32), first[r, 1].astype(F32)
        sums = rounded[0] + rounded[1]
        squares = rounded[0] * rounded[0] + rounded[1] * rounded[1]
        stat[0, pl.ds(r, 1), :] = jnp.sum(sums, axis=0, keepdims=True)
        stat[1, pl.ds(r, 1), :] = jnp.sum(squares, axis=0, keepdims=True)

        @pl.when(r == split - 1)
        def _():
            sums_start(1)

        @pl.when(r == MOST - 1)
        def _():
            sums_start(2)

        @pl.when(r < MOST - 1)
        def _():
            send_first(r)

        for n in range(1, nx - 1):

            @pl.when(r == 2 * n - 1)
            def _():
                one_way(n)

        return carry

    lax.fori_loop(0, MOST, first_conv, 0)
    x_start(1, y_finish(1))
    one_way(nx - 1)
    to_partner(1, 0, nx * size)
    set_norm(1, x_finish(1), g2[...])
    ready_weight(1)

    my_count = counts[f]

    def second_conv(q, r, carry):
        await_bytes(hb.at[r, 0], hb_recv.at[r, 0])
        await_bytes(hb.at[r, 1], hb_recv.at[r, 1])
        result = convolve(r, second_rows(r), q, s2[...], 1) + b2[...]
        live = r < my_count
        for i in range(2):
            kept = rec[r, i].astype(F32).reshape(width, C)
            value = kept + result[i * width : (i + 1) * width]
            outv[r, i] = jnp.where(live, value, 0.0).astype(BF16)
        pltpu.make_async_copy(outv.at[r], out.at[r], out_sem.at[r]).start()
        return carry

    lax.fori_loop(0, 1, functools.partial(second_conv, 1), 0)
    x_start(2, y_finish(2))
    send_first(MOST - 1)
    lax.fori_loop(1, split, functools.partial(second_conv, 1), 0)
    set_norm(2, x_finish(2), g2[...])
    lax.fori_loop(split, MOST, functools.partial(second_conv, 2), 0)

    for i in range(2):
        await_bytes(wb.at[i, pl.ds(0, (ny - 1) * su), :, lanes], wy_send.at[i])
        await_bytes(wb.at[i, :, :, lanes], wp_send.at[i])
    x_await(0, size, 0, wx_send)
    if nx > 2:
        x_await(0, size, 1, wx_send)
        x_await(0, half, 2, wx_send)
        x_await(0, half, 3, wx_send)
    for n in range(nx - 1):
        x_await(1, size, n, wx_send)
    await_bytes(sts.at[0 : nf - 1], st_send)
    await_bytes(stage.at[:, 0 : nf - 1], a2a_send)
    for q in range(3):
        await_bytes(ysc.at[q, 0 : ny - 1], y_send.at[q])
        await_bytes(xsc.at[q, 0 : nx - 1], x_send.at[q])
    for r in range(MOST):
        for i in range(2):
            await_bytes(rec.at[r, i], ha_send.at[r, i])
            await_bytes(first.at[r, i], hb_send.at[r, i])
        pltpu.make_async_copy(outv.at[r], out.at[r], out_sem.at[r]).wait()


def per_device(nf, nh, video, counts, tw, tb, g1, s1, w1, b1, g2, s2, w2, b2):
    frames = video.shape[0]
    ny = 8 if nh % 16 == 0 else 2
    nx = nh // ny
    su = w1.shape[0] // 8
    tp = frames + 1
    wide = tp * J
    fr = -(-(frames + 7) // 8) * 8
    width = nf * J
    cells = float(2 * nh * width * (C // GROUPS))
    row = lambda v: v.reshape(1, C)
    anyspace = pl.BlockSpec(memory_space=pl.ANY)
    dma = pltpu.SemaphoreType.DMA
    V = pltpu.VMEM
    scratch = [
        V((frames, 2, J, C), BF16),
        V((27 * C, C), BF16),
        V((2, tp, J, C), BF16),
        V((2, 2, fr, C), BF16),
        V((2, tp, J, C), BF16),
        V((2, 4, fr, C), BF16),
        V((wide + 16, C), F32),
        V((4 * wide, 3 * C), BF16),
        V((3, 2, wide + 16, C), F32),
        V((fr, 2, J, C), BF16),
        V((MOST, nf, 2, J, C), BF16),
        V((nf, 8, SUM_LANES), F32),
        V((nf, 8, SUM_LANES), F32),
        V((3, ny, 8, SUM_LANES), F32),
        V((3, nx, 8, SUM_LANES), F32),
        V((fr, SUM_LANES), F32),
        V((MOST, 2, nf, J, C), BF16),
        V((MOST, 2, nf, J, C), BF16),
        V((MOST, 2, width, C), BF16),
        V((MOST, 2, width, C), BF16),
        V((width + 16, C), F32),
        V((4 * width, 3 * C), BF16),
        V((2, nh * su, 8, C), BF16),
        V((2, 9 * C, C), BF16),
        V((2, 8, C), F32),
        V((3, 8, C), F32),
        V((3, 8, C), F32),
        V((MOST, 2, width, C), BF16),
        V((7, 1, C), F32),
        pltpu.SMEM((nf,), jnp.int32),
        dma((2,)), dma((8,)), dma((8,)), dma((2,)),
        dma((2,)), dma((2,)), dma((2, 4)), dma((2, 4)), dma((2,)), dma((2,)),
        dma, dma((MOST,)), dma, dma, dma((3,)), dma((3,)), dma((3,)), dma((3,)),
        dma((MOST, 2)), dma((MOST, 2)), dma((MOST, 2)), dma((MOST, 2)), dma((MOST,)), dma((7,)),
        pltpu.SemaphoreType.REGULAR((3, 3)),
    ]
    return pl.pallas_call(
        functools.partial(kernel, nf, nx, ny, frames, su, cells),
        out_shape=jax.ShapeDtypeStruct((MOST, 2, width, C), BF16),
        in_specs=[pl.BlockSpec(memory_space=pltpu.SMEM)] + [anyspace] * 11,
        out_specs=anyspace,
        scratch_shapes=scratch,
        compiler_params=pltpu.CompilerParams(
            collective_id=0, has_side_effects=True, vmem_limit_bytes=60 * 2**20
        ),
        name="block",
    )(
        counts, video, tw, w1.reshape(su, 8, C), w2.reshape(su, 8, C),
        row(tb), row(g1), row(s1), row(b1), row(g2), row(s2), row(b2),
    )


def solution(mesh):
    placed = (
        P(None, "height", "frame", None),
        P(), P(), P(), P(), P(),
        P("height", None),
        P(), P(), P(),
        P("height", None),
        P(),
    )
    return jax.shard_map(
        functools.partial(per_device, mesh.shape["frame"], mesh.shape["height"]),
        mesh=mesh,
        in_specs=placed,
        out_specs=P("frame", "height", None, None),
        check_vma=False,
    )
```

```python
import functools

import jax
import jax.numpy as jnp
from jax import lax
from jax.experimental import pallas as pl
from jax.experimental.pallas import tpu as pltpu
from jax.sharding import PartitionSpec as P

GROUPS = 32
C = 256
J = 8
MOST = 6
F32 = jnp.float32
BF16 = jnp.bfloat16
HIGH = lax.Precision.HIGHEST
MESH = pl.DeviceIdType.MESH
SUM_LANES = 128
EARLY = 2


def silu(v):
    half = 0.5 * v
    return half * jnp.tanh(half) + half


def hdot(a, b):
    return jnp.dot(a, b, precision=HIGH, preferred_element_type=F32)


def one_hot(rows, cols, fn):
    r = lax.broadcasted_iota(jnp.int32, (rows, cols), 0)
    c = lax.broadcasted_iota(jnp.int32, (rows, cols), 1)
    return jnp.where(fn(r, c), 1.0, 0.0).astype(F32)


def kernel(
    nf, nx, ny, frames, su, cells,
    counts, video, tw, w1, w2, tb_in, g1_in, s1_in, b1_in, g2_in, s2_in, b2_in,
    out,
    vid, twv, rowb, colb, hr, hc, gt, se, tc, bs, stage, sts, rs, ysc, xsc, fsb,
    rec, ha, first, g4, so, wb, wr, stat, mu, sc, outv, pv, offs,
    local_sem, p1_send, p1_recv, wl_sem, wy_send, wy_recv, wx_send, wx_recv, wp_send, wp_recv,
    a2a_send, a2a_recv, st_send, st_recv, y_send, y_recv, x_send, x_recv,
    ha_send, ha_recv, hb_send, hb_recv, out_sem, pv_sem, known,
):
    nh = nx * ny
    tp = frames + 1
    wide = tp * J
    fr = bs.shape[0]
    width = nf * J
    f = lax.axis_index("frame")
    h = lax.axis_index("height")
    x = h // ny
    y = lax.rem(h, ny)
    core = lax.rem(f, 2)
    hup, hdn = lax.rem(h + nh - 1, nh), lax.rem(h + 1, nh)
    fl, fr_ = lax.rem(f + nf - 1, nf), lax.rem(f + 1, nf)

    def dev(hh, ff):
        return {"height": hh, "frame": ff}

    def remote(src, dst, send, recv, hh, ff):
        return pltpu.make_async_remote_copy(
            src_ref=src, dst_ref=dst, send_sem=send, recv_sem=recv,
            device_id=dev(hh, ff), device_id_type=MESH,
        )

    def await_bytes(ref, sem):
        pltpu.make_async_copy(ref, ref, sem).wait()

    barrier = pltpu.get_barrier_semaphore()

    def greet(sem, hh, ff):
        pl.semaphore_signal(sem, inc=1, device_id=dev(hh, ff), device_id_type=MESH)

    def on_z(s):
        return h, lax.rem(f + nf + s, nf)

    def on_y(s):
        return x * ny + lax.rem(y + ny + s, ny), f

    def on_x(s):
        return lax.rem(x + nx + s, nx) * ny + y, f

    near = [(hup, f), (hdn, f), (hup, fl), (hup, fr_), (hdn, fl), (hdn, fr_)]
    for step in (-1, 1):
        near += [on_z(step), on_y(step), on_x(step)]
    for hh, ff in near:
        greet(barrier, hh, ff)

    copy_video = pltpu.make_async_copy(video, vid, local_sem.at[0])
    copy_video.start()
    copy_tw = pltpu.make_async_copy(tw, twv, local_sem.at[1])
    copy_tw.start()
    lane0 = pl.multiple_of(core * 128, 128)
    lanes = pl.ds(lane0, 128)
    mine = pl.ds(h * su, su)
    own_w = [
        pltpu.make_async_copy(w.at[:, :, lanes], wb.at[i, mine, :, lanes], wl_sem.at[i])
        for i, w in enumerate((w1, w2))
    ]
    for copy in own_w:
        copy.start()

    vectors = [
        pltpu.make_async_copy(v, pv.at[n], pv_sem.at[n])
        for n, v in enumerate((tb_in, g1_in, s1_in, b1_in, g2_in, s2_in, b2_in))
    ]
    for copy in vectors:
        copy.start()
    tb, g1, s1, b1, g2, s2, b2 = (pv.at[n] for n in range(7))

    for i in range(2):
        hr[i, frames:tp] = jnp.zeros((1, J, C), BF16)
    pl.semaphore_wait(barrier, len(near))

    rows_out = [
        remote(video.at[:, 0], hr.at[1, 0:frames], p1_send.at[0], p1_recv.at[0], hup, f),
        remote(video.at[:, 1], hr.at[0, 0:frames], p1_send.at[1], p1_recv.at[1], hdn, f),
    ]
    for copy in rows_out:
        copy.start()

    rings = ((0, on_z, nf), (1, on_y, ny), (2, on_x, nx))

    def tell(reach):
        for n, on, size in rings:
            if reach < size // 2:
                for step in (-reach, reach):
                    greet(known.at[n, reach // 2], *on(step))

    def hear(reach):
        for n, on, size in rings:
            if reach < size // 2:
                pl.semaphore_wait(known.at[n, reach // 2], 2)

    tell(1)
    zero8 = jnp.zeros((8, C), F32)
    gt[0:8, :] = zero8
    gt[8 + wide : 16 + wide, :] = zero8
    pick_left = one_hot(fr, wide, lambda r, c: c == r * J).astype(BF16)
    pick_right = one_hot(fr, wide, lambda r, c: c == r * J + J - 1).astype(BF16)
    copy_video.wait()
    for i in range(2):
        act = silu(vid[:, i].astype(F32)).astype(BF16)
        rowb[i, 0:frames] = act
        rowb[i, frames:tp] = jnp.zeros((1, J, C), BF16)
        flat = rowb[i].astype(F32).reshape(wide, C).astype(BF16)
        colb[0, i] = jnp.dot(pick_left, flat, preferred_element_type=F32).astype(BF16)
        colb[1, i] = jnp.dot(pick_right, flat, preferred_element_type=F32).astype(BF16)

    borders = [
        (colb.at[0], hc.at[1, 1:3], h, fl),
        (colb.at[1], hc.at[0, 1:3], h, fr_),
        (colb.at[0, 0], hc.at[1, 3], hup, fl),
        (colb.at[1, 0], hc.at[0, 3], hup, fr_),
        (colb.at[0, 1], hc.at[1, 0], hdn, fl),
        (colb.at[1, 1], hc.at[0, 0], hdn, fr_),
    ]
    cols_out = [
        remote(src, dst, p1_send.at[2 + n], p1_recv.at[2 + n], hh, ff)
        for n, (src, dst, hh, ff) in enumerate(borders)
    ]
    for copy in cols_out:
        copy.start()
    hear(1)
    tell(2)

    total = jnp.int32(0)
    for k in range(nf):
        offs[k] = total
        total = total + counts[k]
    g4[0:8, :] = zero8
    g4[8 + width : 16 + width, :] = zero8
    for a in range(3):
        for i in range(2):
            tc[a, i, 0:16, :] = jnp.zeros((16, C), F32)

    put_left = one_hot(wide, fr, lambda r, c: r == c * J).astype(BF16)
    put_right = one_hot(wide, fr, lambda r, c: r == c * J + J - 1).astype(BF16)
    col = lax.rem(lax.broadcasted_iota(jnp.int32, (wide, C), 0), J)
    keep_left = jnp.where(f > 0, 1.0, 0.0)
    keep_right = jnp.where(f < nf - 1, 1.0, 0.0)
    keep_top = jnp.where(h > 0, 1.0, 0.0)
    keep_bottom = jnp.where(h < nh - 1, 1.0, 0.0)

    def bordered(ip):
        keep = (keep_top, 1.0, 1.0, keep_bottom)[ip]
        if ip in (1, 2):
            middle = rowb[ip - 1].astype(F32).reshape(wide, C)
        else:
            raw = hr[ip // 3].astype(F32).reshape(wide, C)
            middle = silu(raw).astype(BF16).astype(F32) * keep
        gt[8 : 8 + wide, :] = middle
        lefts = jnp.dot(put_left, hc[0, ip], preferred_element_type=F32) * (keep * keep_left)
        rights = jnp.dot(put_right, hc[1, ip], preferred_element_type=F32) * (keep * keep_right)
        rows = slice(ip * wide, (ip + 1) * wide)
        se[rows, 0:C] = jnp.where(col == 0, lefts, gt[7 : 7 + wide, :]).astype(BF16)
        se[rows, C : 2 * C] = middle.astype(BF16)
        se[rows, 2 * C : 3 * C] = jnp.where(col == J - 1, rights, gt[9 : 9 + wide, :]).astype(BF16)

    def tap(a, i, b):
        start = pl.multiple_of(a * (9 * C) + b * (3 * C), 3 * C)
        return jnp.dot(
            se[(i + b) * wide : (i + b + 1) * wide, :],
            twv[pl.ds(start, 3 * C), :],
            preferred_element_type=F32,
        )

    def own_taps(a, carry):
        tc[a, 0, 16 : 16 + wide, :] = tap(a, 0, 1) + tap(a, 0, 2)
        tc[a, 1, 16 : 16 + wide, :] = tap(a, 1, 0) + tap(a, 1, 1)
        return carry

    def border_taps(a, carry):
        tc[a, 0, 16 : 16 + wide, :] += tap(a, 0, 0)
        tc[a, 1, 16 : 16 + wide, :] += tap(a, 1, 2)
        return carry

    for copy in cols_out[:2]:
        copy.wait()
    bordered(1)
    bordered(2)
    hear(2)
    tell(4)

    for copy in own_w:
        copy.wait()
    for i in range(2):
        for s in range(1, ny):
            here = wb.at[i, mine, :, lanes]
            remote(here, here, wy_send.at[i], wy_recv.at[i], *on_y(s)).start()

    copy_tw.wait()
    for copy in vectors:
        copy.wait()
    lax.fori_loop(0, 3, own_taps, 0)
    for copy in rows_out + cols_out[2:]:
        copy.wait()
    bordered(0)
    bordered(3)
    lax.fori_loop(0, 3, border_taps, 0)
    hear(4)

    n_all = frames * J
    sums = jnp.zeros((n_all, C), F32)
    squares = jnp.zeros((n_all, C), F32)
    for i in range(2):
        value = (
            vid[:, i].astype(F32).reshape(n_all, C)
            + (tc[0, i, 0:n_all, :] + tc[1, i, 8 : 8 + n_all, :] + tc[2, i, 16 : 16 + n_all, :])
            + tb[...]
        )
        bs[0:frames, i] = value.reshape(frames, J, C).astype(BF16)
        rounded = bs[0:frames, i].astype(F32).reshape(n_all, C)
        sums = sums + rounded
        squares = squares + rounded * rounded
        bs[frames:fr, i] = jnp.zeros((fr - frames, J, C), BF16)

    per = C // GROUPS
    sum_map = one_hot(C, SUM_LANES, lambda r, c: c == r // per)
    sq_map = one_hot(C, SUM_LANES, lambda r, c: c == r // per + GROUPS)
    fsum = jnp.sum(sums.reshape(frames, J, C), axis=1)
    fsq = jnp.sum(squares.reshape(frames, J, C), axis=1)
    fsb[0:frames, :] = hdot(fsum, sum_map) + hdot(fsq, sq_map)
    fsb[frames:fr, :] = jnp.zeros((fr - frames, SUM_LANES), F32)

    def pack(k, carry):
        start = offs[k]
        sts[k] = fsb[pl.ds(start, 8), :]
        for r in range(MOST):
            stage[r, k] = bs[start + r]
        return carry

    lax.fori_loop(0, nf, pack, 0)

    def send_sums(s, carry):
        k = lax.rem(f + s, nf)
        remote(sts.at[k], rs.at[f], st_send, st_recv, h, k).start()
        return carry

    lax.fori_loop(1, nf, send_sums, 0)

    def send_slot(n, carry):
        r = n // (nf - 1)
        k = lax.rem(f + 1 + lax.rem(n, nf - 1), nf)
        remote(stage.at[r, k], rec.at[r, :, f], a2a_send, a2a_recv.at[r], h, k).start()
        return carry

    lax.fori_loop(0, MOST * (nf - 1), send_slot, 0)
    my_offset = offs[f]
    rs[f] = fsb[pl.ds(my_offset, 8), :]
    for r in range(MOST):
        rec[r, :, f] = bs[my_offset + r]

    size = ny * su
    half = size // 2

    def block(s):
        return lax.rem(x + nx + s, nx) * size

    def x_copy(i, start, count, sem, step):
        here = wb.at[i, pl.ds(start, count), :, lanes]
        remote(here, here, wx_send.at[i, sem], wx_recv.at[i, sem], *on_x(step)).start()

    def x_await(i, count, sem, which):
        await_bytes(wb.at[i, pl.ds(0, count), :, lanes], which.at[i, sem])

    partner = f + 1 - 2 * core
    other = pl.ds(pl.multiple_of(128 - core * 128, 128), 128)

    def to_partner(i, start, count):
        here = wb.at[i, pl.ds(start, count), :, lanes]
        remote(here, here, wp_send.at[i], wp_recv.at[i], h, partner).start()

    def both_first():
        await_bytes(wb.at[0, pl.ds(0, (ny - 1) * su), :, lanes], wy_recv.at[0])
        x_copy(0, block(0), size, 0, 1)
        if nx > 2:
            x_copy(0, block(0), size, 1, -1)
        to_partner(0, block(0), size)

    def both_second():
        x_await(0, size, 0, wx_recv)
        if nx > 2:
            x_copy(0, block(-1), half, 2, 1)
            x_await(0, size, 1, wx_recv)
            x_copy(0, block(1) + half, half, 3, -1)
            to_partner(0, block(-1), size)
        to_partner(0, block(1), size)

    def both_last():
        if nx > 2:
            x_await(0, half, 2, wx_recv)
            x_await(0, half, 3, wx_recv)
            to_partner(0, block(2), size)

    way = 1 - 2 * ((ny - y) // ny)

    def one_way(n):
        if n == 0:
            await_bytes(wb.at[1, pl.ds(0, (ny - 1) * su), :, lanes], wy_recv.at[1])
        else:
            x_await(1, size, n - 1, wx_recv)
        if n < nx - 1:
            x_copy(1, block(-n * way), size, n, way)

    def y_start(q, value):
        ysc[q, y] = value
        for s in range(1, ny):
            remote(
                ysc.at[q, y], ysc.at[q, y], y_send.at[q], y_recv.at[q],
                *on_y(s),
            ).start()

    def y_finish(q):
        await_bytes(ysc.at[q, 0 : ny - 1], y_recv.at[q])
        return jnp.sum(ysc[q], axis=0)

    def x_start(q, value):
        xsc[q, x] = value
        for s in range(1, nx):
            remote(
                xsc.at[q, x], xsc.at[q, x], x_send.at[q], x_recv.at[q],
                *on_x(s),
            ).start()

    def x_finish(q):
        await_bytes(xsc.at[q, 0 : nx - 1], x_recv.at[q])
        return jnp.sum(xsc[q], axis=0)

    def set_norm(q, totals, gain):
        sum_back = one_hot(SUM_LANES, C, lambda r, c: r == c // per)
        sq_back = one_hot(SUM_LANES, C, lambda r, c: r == c // per + GROUPS)
        mean = hdot(totals, sum_back) / cells
        var = hdot(totals, sq_back) / cells - mean * mean
        mu[q] = mean
        sc[q] = lax.rsqrt(jnp.maximum(var, 0.0) + 1e-06) * gain

    def ready_weight(i):
        await_bytes(wb.at[i, :, :, other], wp_recv.at[i])
        step = 18

        def widen(n, carry):
            rows = wb[i, pl.ds(n * step, step)].astype(F32).reshape(step * 8, C)
            wr[i, pl.ds(pl.multiple_of(n * step * 8, step * 8), step * 8), :] = rows.astype(BF16)
            return carry

        lax.fori_loop(0, nh * su // step, widen, 0)

    def slot_in(r, early):
        await_bytes(rec.at[r, :, 0 : nf - 1], a2a_recv.at[r])
        if early:
            pairs = (rec.at[r], ha.at[r, 1]), (rec.at[r], ha.at[r, 0])
        else:
            pairs = (rec.at[r, 0], ha.at[r, 1, 0]), (rec.at[r, 1], ha.at[r, 0, 1])
        for n, ((src, dst), hh) in enumerate(zip(pairs, (hup, hdn))):
            remote(src, dst, ha_send.at[r, n], ha_recv.at[r, n], hh, f).start()

    both_first()
    await_bytes(rs.at[0 : nf - 1], st_recv)
    y_start(0, jnp.sum(rs[...], axis=0))
    both_second()
    slot_in(0, True)
    x_start(0, y_finish(0))
    one_way(0)
    slot_in(1, True)
    both_last()
    set_norm(0, x_finish(0), g1[...])

    def convolve(r, fields, keeps, q, shift, weight):
        mean = mu[q, pl.ds(r, 1), :]
        scale = sc[q, pl.ds(r, 1), :]
        for ip, field in enumerate(fields):
            value = field[...].astype(F32).reshape(width, C)
            normed = silu((value - mean) * scale + shift)
            if keeps[ip] is not None:
                normed = normed * keeps[ip]
            g4[8 : 8 + width, :] = normed
            rows = slice(ip * width, (ip + 1) * width)
            so[rows, 0:C] = g4[7 : 7 + width, :].astype(BF16)
            so[rows, C : 2 * C] = normed.astype(BF16)
            so[rows, 2 * C : 3 * C] = g4[9 : 9 + width, :].astype(BF16)
        pairs = []
        for top in range(0, len(fields) - 2, 2):
            acc = jnp.zeros((2 * width, C), F32)
            for b in range(3):
                acc = acc + jnp.dot(
                    so[(top + b) * width : (top + b + 2) * width, :],
                    wr[weight, b * 3 * C : (b + 1) * 3 * C, :],
                    preferred_element_type=F32,
                )
            pairs.append(acc)
        return pairs

    stat[...] = jnp.zeros_like(stat)
    split = MOST - 2

    def send_first(r):
        up, down = first.at[r, 1], first.at[r, 2]
        remote(up, first.at[r, 3], hb_send.at[r, 0], hb_recv.at[r, 0], hup, f).start()
        remote(down, first.at[r, 0], hb_send.at[r, 1], hb_recv.at[r, 1], hdn, f).start()

    def sums_start(q):
        y_start(q, hdot(stat[0], sum_map) + hdot(stat[1], sq_map))

    def first_conv(early, r, carry):
        @pl.when(r + 2 < MOST)
        def _():
            slot_in(r + 2, False)

        above = ha.at[r, 0] if early else ha.at[r, 0, 1]
        below = ha.at[r, 1] if early else ha.at[r, 1, 0]
        await_bytes(below, ha_recv.at[r, 0])
        await_bytes(above, ha_recv.at[r, 1])
        own = (rec.at[r, 0], rec.at[r, 1])
        if early:
            fields = (above.at[0], above.at[1]) + own + (below.at[0], below.at[1])
            keeps = (keep_top, keep_top, None, None, keep_bottom, keep_bottom)
        else:
            fields = (above,) + own + (below,)
            keeps = (keep_top, None, None, keep_bottom)
        place = 0 if early else 1
        for n, pair in enumerate(convolve(r, fields, keeps, 0, s1[...], 0)):
            pair = pair + b1[...]
            first[r, place + 2 * n] = pair[0:width].astype(BF16)
            first[r, place + 2 * n + 1] = pair[width : 2 * width].astype(BF16)
        rounded = first[r, 1].astype(F32), first[r, 2].astype(F32)
        sums = rounded[0] + rounded[1]
        squares = rounded[0] * rounded[0] + rounded[1] * rounded[1]
        stat[0, pl.ds(r, 1), :] = jnp.sum(sums, axis=0, keepdims=True)
        stat[1, pl.ds(r, 1), :] = jnp.sum(squares, axis=0, keepdims=True)

        @pl.when(r == split - 1)
        def _():
            sums_start(1)

        @pl.when(r == MOST - 1)
        def _():
            sums_start(2)

        if not early:

            @pl.when(r < MOST - 1)
            def _():
                send_first(r)

        for n in range(1, nx - 1):

            @pl.when(r == 2 * n - 1)
            def _():
                one_way(n)

        return carry

    ready_weight(0)
    for r in range(EARLY):
        first_conv(True, r, 0)
    lax.fori_loop(EARLY, MOST, functools.partial(first_conv, False), 0)
    x_start(1, y_finish(1))
    one_way(nx - 1)
    to_partner(1, 0, nx * size)
    set_norm(1, x_finish(1), g2[...])
    ready_weight(1)

    my_count = counts[f]

    def second_conv(q, r, carry):
        @pl.when(r >= EARLY)
        def _():
            await_bytes(first.at[r, 3], hb_recv.at[r, 0])
            await_bytes(first.at[r, 0], hb_recv.at[r, 1])

        fields = tuple(first.at[r, n] for n in range(4))
        keeps = (keep_top, None, None, keep_bottom)
        result = convolve(r, fields, keeps, q, s2[...], 1)[0] + b2[...]
        live = r < my_count
        for i in range(2):
            kept = rec[r, i].astype(F32).reshape(width, C)
            value = kept + result[i * width : (i + 1) * width]
            outv[r, i] = jnp.where(live, value, 0.0).astype(BF16)
        pltpu.make_async_copy(outv.at[r], out.at[r], out_sem.at[r]).start()
        return carry

    lax.fori_loop(0, 1, functools.partial(second_conv, 1), 0)
    x_start(2, y_finish(2))
    send_first(MOST - 1)
    lax.fori_loop(1, split, functools.partial(second_conv, 1), 0)
    set_norm(2, x_finish(2), g2[...])
    lax.fori_loop(split, MOST, functools.partial(second_conv, 2), 0)

    for i in range(2):
        await_bytes(wb.at[i, pl.ds(0, (ny - 1) * su), :, lanes], wy_send.at[i])
        await_bytes(wb.at[i, :, :, lanes], wp_send.at[i])
    x_await(0, size, 0, wx_send)
    if nx > 2:
        x_await(0, size, 1, wx_send)
        x_await(0, half, 2, wx_send)
        x_await(0, half, 3, wx_send)
    for n in range(nx - 1):
        x_await(1, size, n, wx_send)
    await_bytes(sts.at[0 : nf - 1], st_send)
    await_bytes(stage.at[:, 0 : nf - 1], a2a_send)
    for q in range(3):
        await_bytes(ysc.at[q, 0 : ny - 1], y_send.at[q])
        await_bytes(xsc.at[q, 0 : nx - 1], x_send.at[q])
    for r in range(MOST):
        for i in range(2):
            await_bytes(rec.at[r] if r < EARLY else rec.at[r, i], ha_send.at[r, i])
            if r >= EARLY:
                await_bytes(first.at[r, 1 + i], hb_send.at[r, i])
        pltpu.make_async_copy(outv.at[r], out.at[r], out_sem.at[r]).wait()


def per_device(nf, nh, video, counts, tw, tb, g1, s1, w1, b1, g2, s2, w2, b2):
    frames = video.shape[0]
    ny = 8 if nh % 16 == 0 else 2
    nx = nh // ny
    su = w1.shape[0] // 8
    tp = frames + 1
    wide = tp * J
    fr = -(-(frames + 7) // 8) * 8
    width = nf * J
    cells = float(2 * nh * width * (C // GROUPS))
    row = lambda v: v.reshape(1, C)
    anyspace = pl.BlockSpec(memory_space=pl.ANY)
    dma = pltpu.SemaphoreType.DMA
    V = pltpu.VMEM
    scratch = [
        V((frames, 2, J, C), BF16),
        V((27 * C, C), BF16),
        V((2, tp, J, C), BF16),
        V((2, 2, fr, C), BF16),
        V((2, tp, J, C), BF16),
        V((2, 4, fr, C), BF16),
        V((wide + 16, C), F32),
        V((4 * wide, 3 * C), BF16),
        V((3, 2, wide + 16, C), F32),
        V((fr, 2, J, C), BF16),
        V((MOST, nf, 2, J, C), BF16),
        V((nf, 8, SUM_LANES), F32),
        V((nf, 8, SUM_LANES), F32),
        V((3, ny, 8, SUM_LANES), F32),
        V((3, nx, 8, SUM_LANES), F32),
        V((fr, SUM_LANES), F32),
        V((MOST, 2, nf, J, C), BF16),
        V((MOST, 2, 2, nf, J, C), BF16),
        V((MOST, 4, width, C), BF16),
        V((width + 16, C), F32),
        V((6 * width, 3 * C), BF16),
        V((2, nh * su, 8, C), BF16),
        V((2, 9 * C, C), BF16),
        V((2, 8, C), F32),
        V((3, 8, C), F32),
        V((3, 8, C), F32),
        V((MOST, 2, width, C), BF16),
        V((7, 1, C), F32),
        pltpu.SMEM((nf,), jnp.int32),
        dma((2,)), dma((8,)), dma((8,)), dma((2,)),
        dma((2,)), dma((2,)), dma((2, 4)), dma((2, 4)), dma((2,)), dma((2,)),
        dma, dma((MOST,)), dma, dma, dma((3,)), dma((3,)), dma((3,)), dma((3,)),
        dma((MOST, 2)), dma((MOST, 2)), dma((MOST, 2)), dma((MOST, 2)), dma((MOST,)), dma((7,)),
        pltpu.SemaphoreType.REGULAR((3, 3)),
    ]
    return pl.pallas_call(
        functools.partial(kernel, nf, nx, ny, frames, su, cells),
        out_shape=jax.ShapeDtypeStruct((MOST, 2, width, C), BF16),
        in_specs=[pl.BlockSpec(memory_space=pltpu.SMEM)] + [anyspace] * 11,
        out_specs=anyspace,
        scratch_shapes=scratch,
        compiler_params=pltpu.CompilerParams(
            collective_id=0, has_side_effects=True, vmem_limit_bytes=60 * 2**20
        ),
        name="block",
    )(
        counts, video, tw, w1.reshape(su, 8, C), w2.reshape(su, 8, C),
        row(tb), row(g1), row(s1), row(b1), row(g2), row(s2), row(b2),
    )


def solution(mesh):
    placed = (
        P(None, "height", "frame", None),
        P(), P(), P(), P(), P(),
        P("height", None),
        P(), P(), P(),
        P("height", None),
        P(),
    )
    return jax.shard_map(
        functools.partial(per_device, mesh.shape["frame"], mesh.shape["height"]),
        mesh=mesh,
        in_specs=placed,
        out_specs=P("frame", "height", None, None),
        check_vma=False,
    )
```

```python
import functools

import jax
import jax.numpy as jnp
from jax import lax
from jax.experimental import pallas as pl
from jax.experimental.pallas import tpu as pltpu
from jax.sharding import PartitionSpec as P

GROUPS = 32
C = 256
J = 8
MOST = 6
F32 = jnp.float32
BF16 = jnp.bfloat16
HIGH = lax.Precision.HIGHEST
MESH = pl.DeviceIdType.MESH
SUM_LANES = 128


def silu(v):
    half = 0.5 * v
    return half * jnp.tanh(half) + half


def hdot(a, b):
    return jnp.dot(a, b, precision=HIGH, preferred_element_type=F32)


def one_hot(rows, cols, fn):
    r = lax.broadcasted_iota(jnp.int32, (rows, cols), 0)
    c = lax.broadcasted_iota(jnp.int32, (rows, cols), 1)
    return jnp.where(fn(r, c), 1.0, 0.0).astype(F32)


def size_y(nh):
    return 8 if nh % 16 == 0 else 2


def kernel(
    nf, nx, ny, frames, su, cells,
    counts, video, tw, w1, w2, tb_in, g1_in, s1_in, b1_in, g2_in, s2_in, b2_in,
    out,
    vid, twv, rowb, colb, hr, hc, gt, se, tc, bs, stage, sts, rs, ysc, xsc, fsb,
    rec, ha, hb, first, g4, so, wb, wr, stat, mu, sc, outv, pv, offs,
    local_sem, p1_send, p1_recv, wl_sem, ring_send, ring_recv, wy_send, wy_recv, wx_send, wx_recv, wp_send, wp_recv,
    a2a_send, a2a_recv, st_send, st_recv, y_send, y_recv, x_send, x_recv,
    ha_send, ha_recv, hb_send, hb_recv, out_sem, pv_sem, known,
):
    nh = nx * ny
    tp = frames + 1
    wide = tp * J
    fr = bs.shape[0]
    width = nf * J
    f = lax.axis_index("frame")
    h = lax.axis_index("height")
    x = h // ny
    y = lax.rem(h, ny)
    core = lax.rem(f, 2)
    hup, hdn = lax.rem(h + nh - 1, nh), lax.rem(h + 1, nh)
    fl, fr_ = lax.rem(f + nf - 1, nf), lax.rem(f + 1, nf)

    def dev(hh, ff):
        return {"height": hh, "frame": ff}

    def remote(src, dst, send, recv, hh, ff):
        return pltpu.make_async_remote_copy(
            src_ref=src, dst_ref=dst, send_sem=send, recv_sem=recv,
            device_id=dev(hh, ff), device_id_type=MESH,
        )

    def await_bytes(ref, sem):
        pltpu.make_async_copy(ref, ref, sem).wait()

    barrier = pltpu.get_barrier_semaphore()

    def greet(sem, hh, ff):
        pl.semaphore_signal(sem, inc=1, device_id=dev(hh, ff), device_id_type=MESH)

    def on_z(s):
        return h, lax.rem(f + nf + s, nf)

    def on_y(s):
        return x * ny + lax.rem(y + ny + s, ny), f

    def on_x(s):
        return lax.rem(x + nx + s, nx) * ny + y, f

    near = [(hup, f), (hdn, f), (hup, fl), (hup, fr_), (hdn, fl), (hdn, fr_)]
    for step in (-1, 1):
        near += [on_z(step), on_y(step), on_x(step)]
    for hh, ff in near:
        greet(barrier, hh, ff)

    copy_video = pltpu.make_async_copy(video, vid, local_sem.at[0])
    copy_video.start()
    copy_tw = pltpu.make_async_copy(tw, twv, local_sem.at[1])
    copy_tw.start()
    lane0 = pl.multiple_of(core * 128, 128)
    lanes = pl.ds(lane0, 128)

    def shards_at(i, yy):
        return wb.at[i, :, pl.ds(yy * su, su), :, lanes]

    def own_shard(i):
        return wb.at[i, x, pl.ds(y * su, su), :, lanes]

    own_w = [
        pltpu.make_async_copy(w.at[:, :, lanes], own_shard(i), wl_sem.at[i])
        for i, w in enumerate((w1, w2))
    ]
    for copy in own_w:
        copy.start()

    vectors = [
        pltpu.make_async_copy(v, pv.at[n], pv_sem.at[n])
        for n, v in enumerate((tb_in, g1_in, s1_in, b1_in, g2_in, s2_in, b2_in))
    ]
    for copy in vectors:
        copy.start()
    tb, g1, s1, b1, g2, s2, b2 = (pv.at[n] for n in range(7))

    for i in range(2):
        hr[i, frames:tp] = jnp.zeros((1, J, C), BF16)
    pl.semaphore_wait(barrier, len(near))

    rows_out = [
        remote(video.at[:, 0], hr.at[1, 0:frames], p1_send.at[0], p1_recv.at[0], hup, f),
        remote(video.at[:, 1], hr.at[0, 0:frames], p1_send.at[1], p1_recv.at[1], hdn, f),
    ]
    for copy in rows_out:
        copy.start()

    rings = ((0, on_z, nf), (1, on_y, ny), (2, on_x, nx))

    def tell(reach):
        for n, on, size in rings:
            if reach < size // 2:
                for step in (-reach, reach):
                    greet(known.at[n, reach // 2], *on(step))

    def hear(reach):
        for n, on, size in rings:
            if reach < size // 2:
                pl.semaphore_wait(known.at[n, reach // 2], 2)

    tell(1)
    zero8 = jnp.zeros((8, C), F32)
    gt[0:8, :] = zero8
    gt[8 + wide : 16 + wide, :] = zero8
    pick_left = one_hot(fr, wide, lambda r, c: c == r * J).astype(BF16)
    pick_right = one_hot(fr, wide, lambda r, c: c == r * J + J - 1).astype(BF16)
    copy_video.wait()
    for i in range(2):
        act = silu(vid[:, i].astype(F32)).astype(BF16)
        rowb[i, 0:frames] = act
        rowb[i, frames:tp] = jnp.zeros((1, J, C), BF16)
        flat = rowb[i].astype(F32).reshape(wide, C).astype(BF16)
        colb[0, i] = jnp.dot(pick_left, flat, preferred_element_type=F32).astype(BF16)
        colb[1, i] = jnp.dot(pick_right, flat, preferred_element_type=F32).astype(BF16)

    borders = [
        (colb.at[0], hc.at[1, 1:3], h, fl),
        (colb.at[1], hc.at[0, 1:3], h, fr_),
        (colb.at[0, 0], hc.at[1, 3], hup, fl),
        (colb.at[1, 0], hc.at[0, 3], hup, fr_),
        (colb.at[0, 1], hc.at[1, 0], hdn, fl),
        (colb.at[1, 1], hc.at[0, 0], hdn, fr_),
    ]
    cols_out = [
        remote(src, dst, p1_send.at[2 + n], p1_recv.at[2 + n], hh, ff)
        for n, (src, dst, hh, ff) in enumerate(borders)
    ]
    for copy in cols_out:
        copy.start()
    hear(1)
    tell(2)

    own_w[0].wait()
    for s in range(1, nx):
        remote(own_shard(0), own_shard(0), wx_send.at[0, 0], wx_recv.at[0, 0], *on_x(s)).start()
    plus, minus = ny // 2, ny - 1 - ny // 2
    others_x = wb.at[0, 0 : nx - 1, pl.ds(0, su), :, lanes]

    def ring(k):
        if k == 0:
            await_bytes(others_x, wx_recv.at[0, 0])
        for d, count, step in ((0, plus, 1), (1, minus, -1)):
            if 0 <= k - 1 < count:
                await_bytes(shards_at(0, 0), ring_recv.at[d, k - 1])
            if k < count:
                here = shards_at(0, lax.rem(y + ny - step * k, ny))
                remote(here, here, ring_send.at[d, k], ring_recv.at[d, k], *on_y(step)).start()


    total = jnp.int32(0)
    for k in range(nf):
        offs[k] = total
        total = total + counts[k]
    g4[0:8, :] = zero8
    g4[8 + width : 16 + width, :] = zero8
    for a in range(3):
        for i in range(2):
            tc[a, i, 0:16, :] = jnp.zeros((16, C), F32)

    put_left = one_hot(wide, fr, lambda r, c: r == c * J).astype(BF16)
    put_right = one_hot(wide, fr, lambda r, c: r == c * J + J - 1).astype(BF16)
    col = lax.rem(lax.broadcasted_iota(jnp.int32, (wide, C), 0), J)
    keep_left = jnp.where(f > 0, 1.0, 0.0)
    keep_right = jnp.where(f < nf - 1, 1.0, 0.0)
    keep_top = jnp.where(h > 0, 1.0, 0.0)
    keep_bottom = jnp.where(h < nh - 1, 1.0, 0.0)

    def bordered(ip):
        keep = (keep_top, 1.0, 1.0, keep_bottom)[ip]
        if ip in (1, 2):
            middle = rowb[ip - 1].astype(F32).reshape(wide, C)
        else:
            raw = hr[ip // 3].astype(F32).reshape(wide, C)
            middle = silu(raw).astype(BF16).astype(F32) * keep
        gt[8 : 8 + wide, :] = middle
        lefts = jnp.dot(put_left, hc[0, ip], preferred_element_type=F32) * (keep * keep_left)
        rights = jnp.dot(put_right, hc[1, ip], preferred_element_type=F32) * (keep * keep_right)
        rows = slice(ip * wide, (ip + 1) * wide)
        se[rows, 0:C] = jnp.where(col == 0, lefts, gt[7 : 7 + wide, :]).astype(BF16)
        se[rows, C : 2 * C] = middle.astype(BF16)
        se[rows, 2 * C : 3 * C] = jnp.where(col == J - 1, rights, gt[9 : 9 + wide, :]).astype(BF16)

    def tap(a, i, b):
        start = pl.multiple_of(a * (9 * C) + b * (3 * C), 3 * C)
        return jnp.dot(
            se[(i + b) * wide : (i + b + 1) * wide, :],
            twv[pl.ds(start, 3 * C), :],
            preferred_element_type=F32,
        )

    def own_taps(a, carry):
        tc[a, 0, 16 : 16 + wide, :] = tap(a, 0, 1) + tap(a, 0, 2)
        tc[a, 1, 16 : 16 + wide, :] = tap(a, 1, 0) + tap(a, 1, 1)
        return carry

    def border_taps(a, carry):
        tc[a, 0, 16 : 16 + wide, :] += tap(a, 0, 0)
        tc[a, 1, 16 : 16 + wide, :] += tap(a, 1, 2)
        return carry

    for copy in cols_out[:2]:
        copy.wait()
    bordered(1)
    bordered(2)
    hear(2)
    tell(4)

    ring(0)
    copy_tw.wait()
    for copy in vectors:
        copy.wait()
    lax.fori_loop(0, 3, own_taps, 0)
    for copy in rows_out + cols_out[2:]:
        copy.wait()
    bordered(0)
    bordered(3)
    lax.fori_loop(0, 3, border_taps, 0)

    own_w[1].wait()
    for s in range(1, ny):
        remote(own_shard(1), own_shard(1), wy_send, wy_recv, *on_y(s)).start()

    hear(4)

    n_all = frames * J
    sums = jnp.zeros((n_all, C), F32)
    squares = jnp.zeros((n_all, C), F32)
    for i in range(2):
        value = (
            vid[:, i].astype(F32).reshape(n_all, C)
            + (tc[0, i, 0:n_all, :] + tc[1, i, 8 : 8 + n_all, :] + tc[2, i, 16 : 16 + n_all, :])
            + tb[...]
        )
        bs[0:frames, i] = value.reshape(frames, J, C).astype(BF16)
        rounded = bs[0:frames, i].astype(F32).reshape(n_all, C)
        sums = sums + rounded
        squares = squares + rounded * rounded
        bs[frames:fr, i] = jnp.zeros((fr - frames, J, C), BF16)

    per = C // GROUPS
    sum_map = one_hot(C, SUM_LANES, lambda r, c: c == r // per)
    sq_map = one_hot(C, SUM_LANES, lambda r, c: c == r // per + GROUPS)
    fsum = jnp.sum(sums.reshape(frames, J, C), axis=1)
    fsq = jnp.sum(squares.reshape(frames, J, C), axis=1)
    fsb[0:frames, :] = hdot(fsum, sum_map) + hdot(fsq, sq_map)
    fsb[frames:fr, :] = jnp.zeros((fr - frames, SUM_LANES), F32)

    def pack(k, carry):
        start = offs[k]
        sts[k] = fsb[pl.ds(start, 8), :]
        for r in range(MOST):
            stage[r, k] = bs[start + r]
        return carry

    lax.fori_loop(0, nf, pack, 0)

    def send_sums(s, carry):
        k = lax.rem(f + s, nf)
        remote(sts.at[k], rs.at[f], st_send, st_recv, h, k).start()
        return carry

    lax.fori_loop(1, nf, send_sums, 0)

    def send_slot(n, carry):
        r = n // (nf - 1)
        k = lax.rem(f + 1 + lax.rem(n, nf - 1), nf)
        remote(stage.at[r, k], rec.at[r, :, f], a2a_send, a2a_recv.at[r], h, k).start()
        return carry

    lax.fori_loop(0, MOST * (nf - 1), send_slot, 0)
    my_offset = offs[f]
    rs[f] = fsb[pl.ds(my_offset, 8), :]
    for r in range(MOST):
        rec[r, :, f] = bs[my_offset + r]

    way = 1 - 2 * ((ny - y) // ny)

    def one_way(n):
        if n == 0:
            await_bytes(wb.at[1, 0, pl.ds(0, (ny - 1) * su), :, lanes], wy_recv)
        else:
            await_bytes(wb.at[1, 0, :, :, lanes], wx_recv.at[1, n - 1])
        if n < nx - 1:
            here = wb.at[1, lax.rem(x + nx - n * way + nx, nx), :, :, lanes]
            remote(here, here, wx_send.at[1, n], wx_recv.at[1, n], *on_x(way)).start()

    partner = f + 1 - 2 * core
    other = pl.ds(pl.multiple_of(128 - core * 128, 128), 128)

    def to_partner(i):
        mine_half = wb.at[i, :, :, :, lanes]
        remote(mine_half, mine_half, wp_send.at[i], wp_recv.at[i], h, partner).start()

    def y_start(q, value):
        ysc[q, y] = value
        for s in range(1, ny):
            remote(
                ysc.at[q, y], ysc.at[q, y], y_send.at[q], y_recv.at[q],
                *on_y(s),
            ).start()

    def y_finish(q):
        await_bytes(ysc.at[q, 0 : ny - 1], y_recv.at[q])
        return jnp.sum(ysc[q], axis=0)

    def x_start(q, value):
        xsc[q, x] = value
        for s in range(1, nx):
            remote(
                xsc.at[q, x], xsc.at[q, x], x_send.at[q], x_recv.at[q],
                *on_x(s),
            ).start()

    def x_finish(q):
        await_bytes(xsc.at[q, 0 : nx - 1], x_recv.at[q])
        return jnp.sum(xsc[q], axis=0)

    def set_norm(q, totals, gain):
        sum_back = one_hot(SUM_LANES, C, lambda r, c: r == c // per)
        sq_back = one_hot(SUM_LANES, C, lambda r, c: r == c // per + GROUPS)
        mean = hdot(totals, sum_back) / cells
        var = hdot(totals, sq_back) / cells - mean * mean
        mu[q] = mean
        sc[q] = lax.rsqrt(jnp.maximum(var, 0.0) + 1e-06) * gain

    def ready_weight(i):
        await_bytes(wb.at[i, :, :, :, other], wp_recv.at[i])
        step = 18
        steps = ny * su // step

        def widen(n, carry):
            rows = wb[i, n // steps, pl.ds(lax.rem(n, steps) * step, step)]
            rows = rows.astype(F32).reshape(step * 8, C)
            wr[i, pl.ds(pl.multiple_of(n * step * 8, step * 8), step * 8), :] = rows.astype(BF16)
            return carry

        lax.fori_loop(0, nh * su // step, widen, 0)

    def slot_in(r):
        await_bytes(rec.at[r, :, 0 : nf - 1], a2a_recv.at[r])
        remote(rec.at[r, 0], ha.at[r, 1], ha_send.at[r, 0], ha_recv.at[r, 0], hup, f).start()
        remote(rec.at[r, 1], ha.at[r, 0], ha_send.at[r, 1], ha_recv.at[r, 1], hdn, f).start()

    ring(1)
    await_bytes(rs.at[0 : nf - 1], st_recv)
    y_start(0, jnp.sum(rs[...], axis=0))
    ring(2)
    slot_in(0)
    x_start(0, y_finish(0))
    ring(3)
    slot_in(1)
    one_way(0)
    set_norm(0, x_finish(0), g1[...])
    ring(4)
    to_partner(0)

    keeps = (keep_top, None, None, keep_bottom)

    def convolve(r, rows_of, q, shift, weight):
        mean = mu[q, pl.ds(r, 1), :]
        scale = sc[q, pl.ds(r, 1), :]
        for ip in range(4):
            normed = silu((rows_of(ip) - mean) * scale + shift)
            if keeps[ip] is not None:
                normed = normed * keeps[ip]
            g4[8 : 8 + width, :] = normed
            rows = slice(ip * width, (ip + 1) * width)
            so[rows, 0:C] = g4[7 : 7 + width, :].astype(BF16)
            so[rows, C : 2 * C] = normed.astype(BF16)
            so[rows, 2 * C : 3 * C] = g4[9 : 9 + width, :].astype(BF16)
        acc = jnp.zeros((2 * width, C), F32)
        for b in range(3):
            acc = acc + jnp.dot(
                so[b * width : (b + 2) * width, :],
                wr[weight, b * 3 * C : (b + 1) * 3 * C, :],
                preferred_element_type=F32,
            )
        return acc

    def first_rows(r):
        def get(ip):
            ref = (ha.at[r, 0], rec.at[r, 0], rec.at[r, 1], ha.at[r, 1])[ip]
            return ref[...].astype(F32).reshape(width, C)

        return get

    def second_rows(r):
        def get(ip):
            ref = (hb.at[r, 0], first.at[r, 0], first.at[r, 1], hb.at[r, 1])[ip]
            return ref[...].astype(F32)

        return get

    stat[...] = jnp.zeros_like(stat)
    split = MOST - 2

    def send_first(r):
        remote(first.at[r, 0], hb.at[r, 1], hb_send.at[r, 0], hb_recv.at[r, 0], hup, f).start()
        remote(first.at[r, 1], hb.at[r, 0], hb_send.at[r, 1], hb_recv.at[r, 1], hdn, f).start()

    def sums_start(q):
        y_start(q, hdot(stat[0], sum_map) + hdot(stat[1], sq_map))

    def first_conv(r, carry):
        @pl.when(r + 2 < MOST)
        def _():
            slot_in(r + 2)

        @pl.when(r == 0)
        def _():
            ready_weight(0)

        await_bytes(ha.at[r, 0], ha_recv.at[r, 0])
        await_bytes(ha.at[r, 1], ha_recv.at[r, 1])
        result = convolve(r, first_rows(r), 0, s1[...], 0) + b1[...]
        first[r, 0] = result[0:width].astype(BF16)
        first[r, 1] = result[width : 2 * width].astype(BF16)
        rounded = first[r, 0].astype(F32), first[r, 1].astype(F32)
        sums = rounded[0] + rounded[1]
        squares = rounded[0] * rounded[0] + rounded[1] * rounded[1]
        stat[0, pl.ds(r, 1), :] = jnp.sum(sums, axis=0, keepdims=True)
        stat[1, pl.ds(r, 1), :] = jnp.sum(squares, axis=0, keepdims=True)

        @pl.when(r == split - 1)
        def _():
            sums_start(1)

        @pl.when(r == MOST - 1)
        def _():
            sums_start(2)

        @pl.when(r < MOST - 1)
        def _():
            send_first(r)

        for n in range(1, nx - 1):

            @pl.when(r == 2 * n - 1)
            def _():
                one_way(n)

        return carry

    lax.fori_loop(0, MOST, first_conv, 0)
    x_start(1, y_finish(1))
    one_way(nx - 1)
    to_partner(1)
    set_norm(1, x_finish(1), g2[...])
    ready_weight(1)

    my_count = counts[f]

    def second_conv(q, r, carry):
        await_bytes(hb.at[r, 0], hb_recv.at[r, 0])
        await_bytes(hb.at[r, 1], hb_recv.at[r, 1])
        result = convolve(r, second_rows(r), q, s2[...], 1) + b2[...]
        live = r < my_count
        for i in range(2):
            kept = rec[r, i].astype(F32).reshape(width, C)
            value = kept + result[i * width : (i + 1) * width]
            outv[r, i] = jnp.where(live, value, 0.0).astype(BF16)
        pltpu.make_async_copy(outv.at[r], out.at[r], out_sem.at[r]).start()
        return carry

    lax.fori_loop(0, 1, functools.partial(second_conv, 1), 0)
    x_start(2, y_finish(2))
    send_first(MOST - 1)
    lax.fori_loop(1, split, functools.partial(second_conv, 1), 0)
    set_norm(2, x_finish(2), g2[...])
    lax.fori_loop(split, MOST, functools.partial(second_conv, 2), 0)

    await_bytes(others_x, wx_send.at[0, 0])
    for d, count in ((0, plus), (1, minus)):
        for k in range(count):
            await_bytes(shards_at(0, 0), ring_send.at[d, k])
    await_bytes(wb.at[1, 0, pl.ds(0, (ny - 1) * su), :, lanes], wy_send)
    for n in range(nx - 1):
        await_bytes(wb.at[1, 0, :, :, lanes], wx_send.at[1, n])
    for i in range(2):
        await_bytes(wb.at[i, :, :, :, lanes], wp_send.at[i])
    await_bytes(sts.at[0 : nf - 1], st_send)
    await_bytes(stage.at[:, 0 : nf - 1], a2a_send)
    for q in range(3):
        await_bytes(ysc.at[q, 0 : ny - 1], y_send.at[q])
        await_bytes(xsc.at[q, 0 : nx - 1], x_send.at[q])
    for r in range(MOST):
        for i in range(2):
            await_bytes(rec.at[r, i], ha_send.at[r, i])
            await_bytes(first.at[r, i], hb_send.at[r, i])
        pltpu.make_async_copy(outv.at[r], out.at[r], out_sem.at[r]).wait()


def per_device(nf, nh, video, counts, tw, tb, g1, s1, w1, b1, g2, s2, w2, b2):
    frames = video.shape[0]
    ny = size_y(nh)
    nx = nh // ny
    su = w1.shape[0] // 8
    tp = frames + 1
    wide = tp * J
    fr = -(-(frames + 7) // 8) * 8
    width = nf * J
    cells = float(2 * nh * width * (C // GROUPS))
    row = lambda v: v.reshape(1, C)
    anyspace = pl.BlockSpec(memory_space=pl.ANY)
    dma = pltpu.SemaphoreType.DMA
    V = pltpu.VMEM
    scratch = [
        V((frames, 2, J, C), BF16),
        V((27 * C, C), BF16),
        V((2, tp, J, C), BF16),
        V((2, 2, fr, C), BF16),
        V((2, tp, J, C), BF16),
        V((2, 4, fr, C), BF16),
        V((wide + 16, C), F32),
        V((4 * wide, 3 * C), BF16),
        V((3, 2, wide + 16, C), F32),
        V((fr, 2, J, C), BF16),
        V((MOST, nf, 2, J, C), BF16),
        V((nf, 8, SUM_LANES), F32),
        V((nf, 8, SUM_LANES), F32),
        V((3, ny, 8, SUM_LANES), F32),
        V((3, nx, 8, SUM_LANES), F32),
        V((fr, SUM_LANES), F32),
        V((MOST, 2, nf, J, C), BF16),
        V((MOST, 2, nf, J, C), BF16),
        V((MOST, 2, width, C), BF16),
        V((MOST, 2, width, C), BF16),
        V((width + 16, C), F32),
        V((4 * width, 3 * C), BF16),
        V((2, nx, ny * su, 8, C), BF16),
        V((2, 9 * C, C), BF16),
        V((2, 8, C), F32),
        V((3, 8, C), F32),
        V((3, 8, C), F32),
        V((MOST, 2, width, C), BF16),
        V((7, 1, C), F32),
        pltpu.SMEM((nf,), jnp.int32),
        dma((2,)), dma((8,)), dma((8,)), dma((2,)),
        dma((2, 4)), dma((2, 4)), dma, dma, dma((2, 4)), dma((2, 4)), dma((2,)), dma((2,)),
        dma, dma((MOST,)), dma, dma, dma((3,)), dma((3,)), dma((3,)), dma((3,)),
        dma((MOST, 2)), dma((MOST, 2)), dma((MOST, 2)), dma((MOST, 2)), dma((MOST,)), dma((7,)),
        pltpu.SemaphoreType.REGULAR((3, 3)),
    ]
    return pl.pallas_call(
        functools.partial(kernel, nf, nx, ny, frames, su, cells),
        out_shape=jax.ShapeDtypeStruct((MOST, 2, width, C), BF16),
        in_specs=[pl.BlockSpec(memory_space=pltpu.SMEM)] + [anyspace] * 11,
        out_specs=anyspace,
        scratch_shapes=scratch,
        compiler_params=pltpu.CompilerParams(
            collective_id=0, has_side_effects=True, vmem_limit_bytes=60 * 2**20
        ),
        name="block",
    )(
        counts, video, tw, w1.reshape(su, 8, C), w2.reshape(su, 8, C),
        row(tb), row(g1), row(s1), row(b1), row(g2), row(s2), row(b2),
    )


def solution(mesh):
    placed = (
        P(None, "height", "frame", None),
        P(), P(), P(), P(), P(),
        P("height", None),
        P(), P(), P(),
        P("height", None),
        P(),
    )
    return jax.shard_map(
        functools.partial(per_device, mesh.shape["frame"], mesh.shape["height"]),
        mesh=mesh,
        in_specs=placed,
        out_specs=P("frame", "height", None, None),
        check_vma=False,
    )
```
